256 devices in a mesh: seq: 32 (over y, z_hi, core), sub: 8 (over z_lo, x).
Axes of the slice: x: 4, y: 4, z: 8 (z_hi: 4, z_lo: 2; z = z_hi * 2 + z_lo), core: 2. Of those that a mesh axis runs over, the one named last changes fastest.
Arguments:
- tokens: bfloat16 [32768, 1024], P(('seq', 'sub')), may hold values from -6 to 6
- cotangent: bfloat16 [32768, 1024], P(('seq', 'sub')), may hold values from -6 to 6
- fine_qkv: bfloat16 [1024, 3, 1024], replicated, may hold values from -0.1875 to 0.1875
- fine_out: bfloat16 [1024, 1024], replicated, may hold values from -0.1875 to 0.1875
- coarse_qkv: bfloat16 [1024, 3, 1024], P(None, None, 'sub'), may hold values from -0.1875 to 0.1875
- coarse_out: bfloat16 [1024, 1024], P('sub'), may hold values from -0.5 to 0.5
Outputs:
- output: bfloat16 [32768, 1024], P(('seq', 'sub'))
- grad_tokens: bfloat16 [32768, 1024], P(('seq', 'sub'))
The draws below stay inside these ranges and needn't reach their ends.
All inputs are finite; a program needn't handle non-finite values.
Results may differ from the reference program's by a relative error of at most 0.02.
Values may be sent and summed in bfloat16 or wider, within the bound.
No kernel may reach another device: no remote copies, remote signals or barrier semaphores. Data moves between devices by JAX's collectives and lax.ppermute only.
A program may use at most 128 MiB of HBM per device.

```python
import jax
import jax.numpy as jnp
from jax import lax

D = 1024
HEADS = 16
HEAD_DIM = 64
WINDOW = 512
POOL = 16
SEQ_LEN = 32768


def level_of(key, dims, cuts, low, top_value):
    factor_of, own = 1.0, jax.random.fold_in(key, 6)
    for axis_at, parts in cuts:
        steps = jnp.exp(jax.random.uniform(jax.random.fold_in(own, axis_at), (parts,), jnp.float32, low / len(cuts), top_value / len(cuts)))
        factor_of = factor_of * jnp.repeat(steps, dims[axis_at] // parts).reshape([-1 if axis == axis_at else 1 for axis in range(len(dims))])
    return factor_of


def normal_values(key, shape, deviation, bound, shards=(), kind=jnp.bfloat16):
    entries = deviation * jax.random.normal(key, shape, jnp.float32)
    if shards:
        entries = entries * level_of(key, shape, shards, -0.22, 0.18)
    return jnp.clip(entries, -bound, bound).astype(kind)


def setup_inputs(seed: int = 0) -> dict:
    splits = jax.random.split(jax.random.key(seed), 7)
    tokens = normal_values(splits[0], (SEQ_LEN, D), 1.0, 6.0, ((0, 256),))
    cotangent = normal_values(splits[1], (SEQ_LEN, D), 1.0, 6.0, ((0, 256),))
    fine_qkv = normal_values(splits[2], (D, 3, D), D ** -0.5, 0.1875)
    fine_out = normal_values(splits[3], (D, D), D ** -0.5, 0.1875)
    coarse_qkv = normal_values(splits[4], (D, 3, D), D ** -0.5, 0.1875, ((2, 8),))
    coarse_out = normal_values(splits[5], (D, D), (D // 8) ** -0.5, 0.5, ((0, 8),))
    return {"tokens": tokens, "cotangent": cotangent, "fine_qkv": fine_qkv, "fine_out": fine_out, "coarse_qkv": coarse_qkv, "coarse_out": coarse_out}


EPS = 1e-06

def rms_rows(values):
    widened = values.astype(jnp.float32)
    factor = lax.rsqrt(lax.optimization_barrier(jnp.mean(widened * widened, axis=-1, keepdims=True)) + EPS)
    return (widened * factor, factor)

def norm_back(grad_rows, normed, factor):
    return factor * (grad_rows - normed * lax.optimization_barrier(jnp.mean(normed * grad_rows, axis=-1, keepdims=True)))

def project_rows(normed_b, weight):
    row_count = normed_b.shape[0]
    local_width = weight.shape[2]
    projected = jnp.dot(normed_b, weight.reshape(weight.shape[0], 3 * local_width), preferred_element_type=jnp.float32)
    projected = projected.reshape(row_count, 3, local_width // HEAD_DIM, HEAD_DIM)
    query_unit, query_scale = rms_rows(projected[:, 0])
    key_unit, key_scale = rms_rows(projected[:, 1])
    return (query_unit, query_scale, key_unit, key_scale, projected[:, 2])

def fdot(spec, left, right):
    return jnp.einsum(spec, left.astype(jnp.float32), right.astype(jnp.float32), precision=lax.Precision.HIGHEST)

def window_exp(query_blk, key_blk, first_pos):
    scores = fdot('qhd,khd->hqk', query_blk, key_blk) * HEAD_DIM ** (-0.5)
    query_pos = lax.broadcasted_iota(jnp.int32, (query_blk.shape[0], key_blk.shape[0]), 0)
    key_pos = lax.broadcasted_iota(jnp.int32, (query_blk.shape[0], key_blk.shape[0]), 1)
    gap = WINDOW + query_pos - key_pos
    allowed = (gap >= 0) & (gap < WINDOW) & (first_pos - WINDOW + key_pos >= 0)
    return jnp.where(allowed[None], jnp.exp(scores), 0.0)

def padded_front(rows):
    return jnp.concatenate([jnp.zeros((WINDOW,) + rows.shape[1:], rows.dtype), rows])

def window_forward(queries, key_rows, value_rows):
    total_len = queries.shape[0]
    key_pad = padded_front(key_rows)
    value_pad = padded_front(value_rows)

    def one_block(block_index):
        first_pos = block_index * WINDOW
        query_blk = lax.dynamic_slice_in_dim(queries, first_pos, WINDOW)
        key_blk = lax.dynamic_slice_in_dim(key_pad, first_pos, 2 * WINDOW)
        value_blk = lax.dynamic_slice_in_dim(value_pad, first_pos, 2 * WINDOW)
        numer = window_exp(query_blk, key_blk, first_pos)
        totals = lax.optimization_barrier(jnp.sum(numer, axis=-1))
        probs_half = (numer / totals[:, :, None]).astype(jnp.bfloat16)
        attended = fdot('hqk,khd->qhd', probs_half, value_blk).astype(jnp.bfloat16)
        return (attended, totals)
    attended, totals = lax.map(one_block, jnp.arange(total_len // WINDOW, dtype=jnp.int32))
    return (attended.reshape(queries.shape), totals)

def window_query_grads(queries, key_rows, value_rows, grad_out, totals, deltas):
    total_len = queries.shape[0]
    key_pad = padded_front(key_rows)
    value_pad = padded_front(value_rows)

    def one_block(inputs):
        block_index, block_totals = inputs
        first_pos = block_index * WINDOW
        query_blk = lax.dynamic_slice_in_dim(queries, first_pos, WINDOW)
        key_blk = lax.dynamic_slice_in_dim(key_pad, first_pos, 2 * WINDOW)
        value_blk = lax.dynamic_slice_in_dim(value_pad, first_pos, 2 * WINDOW)
        grad_blk = lax.dynamic_slice_in_dim(grad_out, first_pos, WINDOW)
        delta_blk = lax.dynamic_slice_in_dim(deltas, first_pos, WINDOW)
        probs_full = window_exp(query_blk, key_blk, first_pos) / block_totals[:, :, None]
        prob_grad = fdot('qhd,khd->hqk', grad_blk, value_blk)
        dscore = (probs_full * (prob_grad - delta_blk.T[:, :, None])).astype(jnp.bfloat16)
        return fdot('hqk,khd->qhd', dscore, key_blk) * HEAD_DIM ** (-0.5)
    grads = lax.map(one_block, (jnp.arange(total_len // WINDOW, dtype=jnp.int32), totals))
    return grads.reshape(queries.shape)

def window_key_grads(queries, key_rows, value_rows, grad_out, totals_rows, deltas):
    total_len = queries.shape[0]
    query_pad = jnp.concatenate([queries, jnp.zeros((WINDOW,) + queries.shape[1:], queries.dtype)])
    grad_pad = jnp.concatenate([grad_out, jnp.zeros((WINDOW,) + grad_out.shape[1:], grad_out.dtype)])
    total_pad = jnp.concatenate([totals_rows, jnp.ones((WINDOW, totals_rows.shape[1]), jnp.float32)])
    delta_pad = jnp.concatenate([deltas, jnp.zeros((WINDOW, deltas.shape[1]), jnp.float32)])

    def one_block(block_index):
        first_key = block_index * WINDOW
        key_blk = lax.dynamic_slice_in_dim(key_rows, first_key, WINDOW)
        value_blk = lax.dynamic_slice_in_dim(value_rows, first_key, WINDOW)
        query_blk = lax.dynamic_slice_in_dim(query_pad, first_key, 2 * WINDOW)
        grad_blk = lax.dynamic_slice_in_dim(grad_pad, first_key, 2 * WINDOW)
        total_blk = lax.dynamic_slice_in_dim(total_pad, first_key, 2 * WINDOW)
        delta_blk = lax.dynamic_slice_in_dim(delta_pad, first_key, 2 * WINDOW)
        scores = fdot('qhd,khd->hqk', query_blk, key_blk) * HEAD_DIM ** (-0.5)
        query_pos = lax.broadcasted_iota(jnp.int32, (2 * WINDOW, WINDOW), 0)
        key_pos = lax.broadcasted_iota(jnp.int32, (2 * WINDOW, WINDOW), 1)
        gap = query_pos - key_pos
        allowed = (gap >= 0) & (gap < WINDOW) & (first_key + query_pos < total_len)
        numer = jnp.where(allowed[None], jnp.exp(scores), 0.0)
        probs_full = numer / total_blk.T[:, :, None]
        probs_half = probs_full.astype(jnp.bfloat16)
        prob_grad = fdot('qhd,khd->hqk', grad_blk, value_blk)
        dscore = (probs_full * (prob_grad - delta_blk.T[:, :, None])).astype(jnp.bfloat16)
        key_grad = fdot('hqk,qhd->khd', dscore, query_blk) * HEAD_DIM ** (-0.5)
        value_grad = fdot('hqk,qhd->khd', probs_half, grad_blk)
        return (key_grad, value_grad)
    key_grad, value_grad = lax.map(one_block, jnp.arange(total_len // WINDOW, dtype=jnp.int32))
    return (key_grad.reshape(key_rows.shape), value_grad.reshape(value_rows.shape))

def coarse_head(head_inputs):
    queries, key_rows, value_rows = head_inputs
    length = queries.shape[0]
    scores = jnp.dot(queries, key_rows.T, preferred_element_type=jnp.float32) * HEAD_DIM ** (-0.5)
    query_pos = lax.broadcasted_iota(jnp.int32, (length, length), 0)
    key_pos = lax.broadcasted_iota(jnp.int32, (length, length), 1)
    numer = jnp.where(key_pos <= query_pos, jnp.exp(scores), 0.0)
    totals = lax.optimization_barrier(jnp.sum(numer, axis=-1))
    probs_half = (numer / totals[:, None]).astype(jnp.bfloat16)
    attended = jnp.dot(probs_half, value_rows, preferred_element_type=jnp.float32).astype(jnp.bfloat16)
    return (attended, totals)

def coarse_head_back(head_inputs):
    queries, key_rows, value_rows, attended, grad_out, totals = head_inputs
    length = queries.shape[0]
    scores = jnp.dot(queries, key_rows.T, preferred_element_type=jnp.float32) * HEAD_DIM ** (-0.5)
    query_pos = lax.broadcasted_iota(jnp.int32, (length, length), 0)
    key_pos = lax.broadcasted_iota(jnp.int32, (length, length), 1)
    numer = jnp.where(key_pos <= query_pos, jnp.exp(scores), 0.0)
    probs_full = numer / totals[:, None]
    probs_half = probs_full.astype(jnp.bfloat16)
    deltas = lax.optimization_barrier(jnp.sum(grad_out.astype(jnp.float32) * attended.astype(jnp.float32), axis=-1))
    prob_grad = jnp.dot(grad_out, value_rows.T, preferred_element_type=jnp.float32)
    dscore = (probs_full * (prob_grad - deltas[:, None])).astype(jnp.bfloat16)
    query_grad = jnp.dot(dscore, key_rows, preferred_element_type=jnp.float32) * HEAD_DIM ** (-0.5)
    key_grad = jnp.dot(dscore.T, queries, preferred_element_type=jnp.float32) * HEAD_DIM ** (-0.5)
    value_grad = jnp.dot(probs_half.T, grad_out, preferred_element_type=jnp.float32)
    return (query_grad, key_grad, value_grad)

def contract_last(left, right):
    return lax.dot_general(left, right, (((1,), (1,)), ((), ())), preferred_element_type=jnp.float32)

def reference(tokens, cotangent, fine_qkv, fine_out, coarse_qkv, coarse_out):
    total_len = tokens.shape[0]
    lead_rows = POOL - 1
    coarse_len = total_len // POOL
    normed_fine, scale_fine = rms_rows(tokens)
    query_unit1, query_scale1, key_unit1, key_scale1, value_raw1 = project_rows(normed_fine.astype(jnp.bfloat16), fine_qkv)
    query_one = query_unit1.astype(jnp.bfloat16)
    key_one = key_unit1.astype(jnp.bfloat16)
    value_one = value_raw1.astype(jnp.bfloat16)
    attended_one, totals_one = window_forward(query_one, key_one, value_one)
    hidden = (tokens.astype(jnp.float32) + jnp.dot(attended_one.reshape(total_len, D), fine_out, preferred_element_type=jnp.float32)).astype(jnp.bfloat16)
    shifted = jnp.concatenate([jnp.zeros((lead_rows, D), jnp.bfloat16), hidden[:total_len - lead_rows]])
    pooled = shifted.reshape(coarse_len, POOL, D).astype(jnp.float32).mean(axis=1).astype(jnp.bfloat16)
    normed_coarse, scale_coarse = rms_rows(pooled)
    query_unit2, query_scale2, key_unit2, key_scale2, value_raw2 = project_rows(normed_coarse.astype(jnp.bfloat16), coarse_qkv)
    query_two = jnp.transpose(query_unit2.astype(jnp.bfloat16), (1, 0, 2))
    key_two = jnp.transpose(key_unit2.astype(jnp.bfloat16), (1, 0, 2))
    value_two = jnp.transpose(value_raw2.astype(jnp.bfloat16), (1, 0, 2))
    attended_two, totals_two = lax.map(coarse_head, (query_two, key_two, value_two))
    attended_rows = jnp.transpose(attended_two, (1, 0, 2)).reshape(coarse_len, D)
    coarse_state = (pooled.astype(jnp.float32) + jnp.dot(attended_rows, coarse_out, preferred_element_type=jnp.float32)).astype(jnp.bfloat16)
    output = (hidden.astype(jnp.float32) + jnp.repeat(coarse_state, POOL, axis=0).astype(jnp.float32)).astype(jnp.bfloat16)
    grad_rows = cotangent.astype(jnp.float32)
    coarse_grad = grad_rows.reshape(coarse_len, POOL, D).sum(axis=1)
    grad_att2 = contract_last(coarse_grad.astype(jnp.bfloat16), coarse_out).astype(jnp.bfloat16)
    grad_att2 = jnp.transpose(grad_att2.reshape(coarse_len, HEADS, HEAD_DIM), (1, 0, 2))
    query_grad2, key_grad2, value_grad2 = lax.map(coarse_head_back, (query_two, key_two, value_two, attended_two, grad_att2, totals_two))
    query_grad2 = norm_back(jnp.transpose(query_grad2, (1, 0, 2)), query_unit2, query_scale2)
    key_grad2 = norm_back(jnp.transpose(key_grad2, (1, 0, 2)), key_unit2, key_scale2)
    value_grad2 = jnp.transpose(value_grad2, (1, 0, 2))
    qkv_grad2 = jnp.stack([query_grad2, key_grad2, value_grad2], axis=1).astype(jnp.bfloat16).reshape(coarse_len, 3 * D)
    normed_grad2 = contract_last(qkv_grad2, coarse_qkv.reshape(D, 3 * D))
    pooled_grad = coarse_grad + norm_back(normed_grad2, normed_coarse, scale_coarse)
    spread = jnp.repeat(pooled_grad / POOL, POOL, axis=0)
    hidden_grad = grad_rows + jnp.concatenate([spread[lead_rows:], jnp.zeros((lead_rows, D), jnp.float32)])
    grad_att1 = contract_last(hidden_grad.astype(jnp.bfloat16), fine_out).astype(jnp.bfloat16).reshape(total_len, HEADS, HEAD_DIM)
    deltas_one = lax.optimization_barrier(jnp.sum(grad_att1.astype(jnp.float32) * attended_one.astype(jnp.float32), axis=-1))
    totals_rows = jnp.transpose(totals_one, (0, 2, 1)).reshape(total_len, HEADS)
    query_grad1 = window_query_grads(query_one, key_one, value_one, grad_att1, totals_one, deltas_one)
    key_grad1, value_grad1 = window_key_grads(query_one, key_one, value_one, grad_att1, totals_rows, deltas_one)
    query_grad1 = norm_back(query_grad1, query_unit1, query_scale1)
    key_grad1 = norm_back(key_grad1, key_unit1, key_scale1)
    qkv_grad1 = jnp.stack([query_grad1, key_grad1, value_grad1], axis=1).astype(jnp.bfloat16).reshape(total_len, 3 * D)
    normed_grad1 = contract_last(qkv_grad1, fine_qkv.reshape(D, 3 * D))
    grad_tokens = (hidden_grad + norm_back(normed_grad1, normed_fine, scale_fine)).astype(jnp.bfloat16)
    return (output, grad_tokens)
```

```python
import jax
import jax.numpy as jnp
from jax import lax
from jax.experimental import pallas as pl
from jax.experimental.pallas import tpu as pltpu
from jax.sharding import Mesh
from jax.sharding import PartitionSpec as P

D = 1024
HEADS = 16
HEAD_DIM = 64
WINDOW = 512
POOL = 16
EPS = 1e-06

LINE = ("y", "z_hi", "core", "z_lo", "x")
GROUP = ("core", "z_lo", "x")
FAR = ("y", "z_hi")

ROWS = 128
HALO = WINDOW
OWN_KEYS = HALO + ROWS
EXTRA = 16
ALL_KEYS = OWN_KEYS + EXTRA
QUERIES = EXTRA + ROWS
PAIR = 2 * HEAD_DIM
PAIRS = D // PAIR
COARSE = ROWS // POOL
SCALE = HEAD_DIM ** (-0.5)
NEG = -1e30

BF = jnp.bfloat16
F32 = jnp.float32


def shifted_by(value, steps):
    count = 1
    for name in LINE:
        count *= lax.axis_size(name)
    first, last = (max(0, -steps), min(count, count - steps))
    return lax.ppermute(value, LINE, [(source, source + steps) for source in range(first, last)])


def exchanged(pieces, axes):
    return lax.all_to_all(pieces, axes, 0, 0, tiled=True)


def last_last(left, right):
    return lax.dot_general(left, right, (((1,), (1,)), ((), ())), preferred_element_type=F32)


def first_first(left, right):
    return lax.dot_general(left, right, (((0,), (0,)), ((), ())), preferred_element_type=F32)


def plain(left, right):
    return jnp.dot(left, right, preferred_element_type=F32)


def low_lanes():
    return lax.broadcasted_iota(jnp.int32, (1, PAIR), 1) < HEAD_DIM


def pair_sums(values, low):
    low_sum = jnp.sum(jnp.where(low, values, 0.0), axis=-1, keepdims=True)
    high_sum = jnp.sum(jnp.where(low, 0.0, values), axis=-1, keepdims=True)
    return jnp.where(low, low_sum, high_sum)


def pair_norm(values, low):
    factor = lax.rsqrt(pair_sums(values * values, low) * (1.0 / HEAD_DIM) + EPS)
    return values * factor, factor


def pair_norm_back(grad, unit, factor, low):
    return factor * (grad - unit * (pair_sums(unit * grad, low) * (1.0 / HEAD_DIM)))


def row_norm(rows):
    factor = lax.rsqrt(jnp.mean(rows * rows, axis=-1, keepdims=True) + EPS)
    return rows * factor, factor


def row_norm_back(grad, normed, factor):
    return factor * (grad - normed * jnp.mean(normed * grad, axis=-1, keepdims=True))


def fine_forward_kernel(
    anchor_ref, t5, t4, t3, t2, t1, t0, cot_ref, w_ref, out_w_ref,
    q_ref, k_ref, v_ref, qf_ref, kf_ref, p_ref, att_ref, hid_ref, send_ref, cg_ref,
    normed, bias, acc,
):
    step = pl.program_id(0)
    anchor = anchor_ref[0]
    low = low_lanes()

    @pl.when(step == 0)
    def _():
        at = 0
        for ref in (t4, t3, t2, t1, t0, t5):
            rows = ref.shape[0]
            normed[at : at + rows, :] = row_norm(ref[...].astype(F32))[0].astype(BF)
            at += rows
        query_pos = lax.broadcasted_iota(jnp.int32, (QUERIES, ALL_KEYS), 0) - EXTRA
        column = lax.broadcasted_iota(jnp.int32, (QUERIES, ALL_KEYS), 1)
        key_pos = jnp.where(column < OWN_KEYS, column - HALO, column - (OWN_KEYS + HALO + EXTRA))
        gap = query_pos - key_pos
        allowed = (gap >= 0) & (gap < WINDOW) & (anchor + key_pos >= 0)
        bias[...] = jnp.where(allowed, 0.0, NEG)
        acc[...] = jnp.zeros_like(acc)

    query, q_factor = pair_norm(plain(normed[HALO - EXTRA : OWN_KEYS, :], w_ref[0]), low)
    both = plain(normed[...], jnp.concatenate([w_ref[1], w_ref[2]], axis=1))
    key, k_factor = pair_norm(both[:, :PAIR], low)
    value = both[:, PAIR:]
    key_b = key.astype(BF)
    q_ref[...] = query[EXTRA:].astype(BF)
    k_ref[...] = key_b[:OWN_KEYS]
    v_ref[...] = value[:OWN_KEYS].astype(BF)
    qf_ref[...] = q_factor[EXTRA:]
    kf_ref[...] = k_factor[:OWN_KEYS]
    attended = None
    for head, mask in enumerate((low, jnp.logical_not(low))):
        query_h = jnp.where(mask, query * SCALE, 0.0).astype(BF)
        numer = jnp.exp(last_last(query_h, key_b) + bias[...])
        total = jnp.sum(numer, axis=-1, keepdims=True)
        prob = (numer * (1.0 / jnp.where(total > 0.0, total, 1.0))).astype(BF)
        p_ref[head] = prob[EXTRA:, :OWN_KEYS]
        part = plain(prob, jnp.where(mask, value, 0.0).astype(BF))
        attended = part if attended is None else attended + part
    attended = attended.astype(BF)
    att_ref[...] = attended[EXTRA:]
    acc[...] += plain(attended, out_w_ref[...])

    @pl.when(step == PAIRS - 1)
    def _():
        before = t1[ROWS - EXTRA :, :].astype(F32) + acc[:EXTRA, :]
        before = jnp.where(anchor > 0, before, 0.0).astype(BF)
        own = (t0[...].astype(F32) + acc[EXTRA:, :]).astype(BF)
        hid_ref[...] = own
        chunk = lax.broadcasted_iota(jnp.int32, (COARSE, QUERIES), 0) * POOL
        row = lax.broadcasted_iota(jnp.int32, (COARSE, QUERIES), 1)
        member = jnp.where((row > chunk) & (row <= chunk + POOL), 1.0, 0.0).astype(BF)
        pooled = plain(member, jnp.concatenate([before, own], axis=0)) * (1.0 / POOL)
        chunk = lax.broadcasted_iota(jnp.int32, (COARSE, ROWS), 0) * POOL
        row = lax.broadcasted_iota(jnp.int32, (COARSE, ROWS), 1)
        member = jnp.where((row >= chunk) & (row < chunk + POOL), 1.0, 0.0).astype(BF)
        coarse_grad = plain(member, cot_ref[...])
        cg_ref[...] = coarse_grad
        message = jnp.concatenate([pooled, coarse_grad], axis=0).astype(BF)
        for peer in range(send_ref.shape[0]):
            send_ref[peer] = message


def coarse_project_kernel(got_ref, in_w_ref, out_w_ref, send_ref, factor_ref):
    low = low_lanes()
    rows = got_ref[...].astype(F32)
    count = rows.shape[0] * COARSE
    pooled = rows[:, :COARSE, :].reshape(count, D)
    coarse_grad = rows[:, COARSE:, :].reshape(count, D)
    normed = row_norm(pooled)[0].astype(BF)
    raw = plain(normed, in_w_ref[...]) + last_last(coarse_grad.astype(BF), out_w_ref[...])
    units, factors = [], []
    for tile in (raw[:, :PAIR], raw[:, PAIR:]):
        unit, factor = pair_norm(tile, low)
        units.append(jnp.where(low, unit, tile))
        factors.append(factor)
    message = jnp.concatenate(units, axis=1).astype(BF)
    factor_ref[...] = jnp.concatenate(factors, axis=1)
    for peer in range(send_ref.shape[0]):
        send_ref[peer] = message


def coarse_attention_kernel(
    start_ref, got_ref, factor_ref, in_w_ref, out_w_ref, send_ref, own_grad, left, right
):
    low = low_lanes()
    own_start = pl.multiple_of(start_ref[0], ROWS)
    length = got_ref.shape[0]
    block = 256
    chunk = 512

    left[...] = got_ref[:, :PAIR]
    right[...] = got_ref[:, PAIR:]
    own_left = left[pl.ds(own_start, ROWS), :]
    own_right = right[pl.ds(own_start, ROWS), :]
    zero = jnp.zeros((), BF)
    own_grad[...] = jnp.zeros_like(own_grad)

    def masked_halves(tile):
        wide = tile.astype(F32)
        return (
            jnp.where(low, wide * SCALE, 0.0).astype(BF),
            jnp.where(low, 0.0, wide).astype(BF),
        )

    def one_block(index, carry):
        first = pl.multiple_of(index * block, block)
        query, grad = masked_halves(left[pl.ds(first, block), :])
        query_pos = first + lax.broadcasted_iota(jnp.int32, (block, 1), 0)

        def one_chunk(at, sums):
            total, product = sums
            key_start = pl.multiple_of(at * chunk, chunk)
            keys = right[pl.ds(key_start, chunk), :]
            key_pos = key_start + lax.broadcasted_iota(jnp.int32, (1, chunk), 1)
            numer = jnp.where(key_pos <= query_pos, jnp.exp(last_last(query, keys)), 0.0)
            prob_grad = last_last(grad, keys)
            total = total + jnp.sum(numer, axis=-1, keepdims=True)
            product = product + jnp.sum(numer * prob_grad, axis=-1, keepdims=True)
            return total, product

        nothing = jnp.zeros((block, 1), F32)
        total, product = lax.fori_loop(0, index // (chunk // block) + 1, one_chunk, (nothing, nothing))
        inverse = 1.0 / total
        delta = product * inverse
        own_pos = own_start + lax.broadcasted_iota(jnp.int32, (1, ROWS), 1)
        numer = jnp.where(own_pos <= query_pos, jnp.exp(last_last(query, own_right)), 0.0)
        prob = numer * inverse
        score_grad = (prob * (last_last(grad, own_right) - delta)).astype(BF)
        own_grad[...] += first_first(score_grad, query) + first_first(prob.astype(BF), grad)
        return carry

    lax.fori_loop(own_start // block, length // block, one_block, 0)

    query, grad = masked_halves(own_left)
    query_pos = own_start + lax.broadcasted_iota(jnp.int32, (ROWS, 1), 0)
    key_pos = lax.broadcasted_iota(jnp.int32, (1, length), 1)
    keys = right[...]
    key_scaled, value = masked_halves(keys)
    numer = jnp.where(key_pos <= query_pos, jnp.exp(last_last(query, keys)), 0.0)
    prob_grad = last_last(grad, keys)
    inverse = 1.0 / jnp.sum(numer, axis=-1, keepdims=True)
    delta = jnp.sum(numer * prob_grad, axis=-1, keepdims=True) * inverse
    prob = numer * inverse
    score_grad = (prob * (prob_grad - delta)).astype(BF)
    mine = plain(score_grad, key_scaled) + plain(prob.astype(BF), value)

    parts = []
    for tile, unit, factor in (
        (mine, own_left, factor_ref[:, :PAIR]),
        (own_grad[...], own_right, factor_ref[:, PAIR:]),
    ):
        back = pair_norm_back(tile, unit.astype(F32), factor, low)
        parts.append(jnp.where(low, back, tile))
    parts = jnp.concatenate(parts, axis=1).astype(BF)
    peers = send_ref.shape[0]
    normed_grad = last_last(parts, in_w_ref[...]).reshape(peers, COARSE, D)
    mixed = plain(parts, out_w_ref[...]).reshape(peers, COARSE, D)
    send_ref[...] = jnp.concatenate([normed_grad, mixed], axis=1).astype(BF)


def coarse_finish_kernel(got_ref, pooled_ref, cg_ref, spread_ref, state_ref):
    summed = jnp.sum(got_ref[...].astype(F32), axis=0)
    pooled = pooled_ref[...].astype(F32)[:COARSE]
    normed, factor = row_norm(pooled)
    pooled_grad = cg_ref[...] + row_norm_back(summed[:COARSE], normed, factor)
    spread_ref[...] = pooled_grad * (1.0 / POOL)
    state_ref[...] = pooled + summed[COARSE:]


def fine_backward_kernel(
    cot_ref, spread_ref, next_ref, out_w_ref, w_ref, q_ref, k_ref, v_ref, qf_ref, kf_ref, p_ref,
    att_ref,
    h4, h3, h2, h1, own_ref, hg_ref,
    hidden_grad, acc,
):
    step = pl.program_id(0)
    low = low_lanes()

    @pl.when(step == 0)
    def _():
        block = (lax.broadcasted_iota(jnp.int32, (ROWS, 1), 0) + (POOL - 1)) // POOL
        added = jnp.zeros((ROWS, D), F32)
        for at in range(COARSE):
            added = jnp.where(block == at, spread_ref[at : at + 1, :], added)
        added = jnp.where(block == COARSE, next_ref[0:1, :], added)
        total = cot_ref[...].astype(F32) + added
        hg_ref[...] = total
        hidden_grad[...] = total.astype(BF)
        acc[...] = jnp.zeros_like(acc)

    att_grad = last_last(hidden_grad[...], out_w_ref[...]).astype(BF).astype(F32)
    delta_all = att_grad * att_ref[...].astype(F32)
    key = k_ref[...]
    value = v_ref[...]
    key_wide = key.astype(F32)
    query_wide = q_ref[...].astype(F32)
    query_grad = key_grad = value_grad = None
    for head, mask in enumerate((low, jnp.logical_not(low))):
        grad = jnp.where(mask, att_grad, 0.0).astype(BF)
        delta = jnp.sum(jnp.where(mask, delta_all, 0.0), axis=-1, keepdims=True)
        prob = p_ref[head]
        score_grad = (prob.astype(F32) * (last_last(grad, value) - delta)).astype(BF)
        dq = plain(score_grad, jnp.where(mask, key_wide * SCALE, 0.0).astype(BF))
        dk = first_first(score_grad, jnp.where(mask, query_wide * SCALE, 0.0).astype(BF))
        dv = first_first(prob, grad)
        if head == 0:
            query_grad, key_grad, value_grad = dq, dk, dv
        else:
            query_grad, key_grad, value_grad = query_grad + dq, key_grad + dk, value_grad + dv
    query_grad = pair_norm_back(query_grad, query_wide, qf_ref[...], low).astype(BF)
    key_grad = pair_norm_back(key_grad, key_wide, kf_ref[...], low).astype(BF)
    both = jnp.concatenate([key_grad, value_grad.astype(BF)], axis=1)
    acc[...] += last_last(both, jnp.concatenate([w_ref[1], w_ref[2]], axis=1))
    acc[HALO:, :] += last_last(query_grad, w_ref[0])

    @pl.when(step == PAIRS - 1)
    def _():
        for at, ref in enumerate((h4, h3, h2, h1)):
            ref[...] = acc[at * ROWS : (at + 1) * ROWS, :].astype(BF)
        own_ref[...] = acc[HALO:, :]


def fine_finish_kernel(own_ref, a1, a2, a3, a4, hg_ref, tokens_ref, out_ref):
    total = own_ref[...]
    for ref in (a1, a2, a3, a4):
        total = total + ref[...].astype(F32)
    normed, factor = row_norm(tokens_ref[...].astype(F32))
    out_ref[...] = (hg_ref[...] + row_norm_back(total, normed, factor)).astype(BF)


def whole(shape):
    return pl.BlockSpec(shape, lambda *_: (0,) * len(shape))


def pair_columns(rows):
    return pl.BlockSpec((rows, PAIR), lambda p: (0, p))


def shaped(shape, kind):
    return jax.ShapeDtypeStruct(shape, kind)


def params(mib):
    return pltpu.CompilerParams(vmem_limit_bytes=mib << 20)


def cost(flops, moved, exps=0):
    return pl.CostEstimate(flops=flops, bytes_accessed=moved, transcendentals=exps)


def per_device(tokens, cotangent, fine_qkv, fine_out, coarse_qkv, coarse_out):
    peers = 1
    for name in GROUP:
        peers *= lax.axis_size(name)
    groups = 1
    for name in FAR:
        groups *= lax.axis_size(name)
    core = lax.axis_index("core")
    scalar = pl.BlockSpec(memory_space=pltpu.SMEM)
    weights = jnp.transpose(fine_qkv, (1, 0, 2))
    coarse_all = jnp.transpose(coarse_qkv, (1, 0, 2))
    picked = jnp.where(core == 0, coarse_all[:, :, :HEAD_DIM], coarse_all[:, :, HEAD_DIM:])
    blank = jnp.zeros((D, HEAD_DIM), BF)
    coarse_in = jnp.concatenate([picked[0], blank, picked[1], picked[2]], axis=1)
    picked_out = jnp.where(core == 0, coarse_out[:HEAD_DIM], coarse_out[HEAD_DIM:])
    coarse_back = jnp.pad(picked_out, ((HEAD_DIM, PAIR), (0, 0)))

    t1, t2, t3, t4 = (shifted_by(tokens, steps) for steps in (1, 2, 3, 4))
    t5 = shifted_by(tokens[ROWS - EXTRA :], 5)
    anchor = (lax.axis_index(LINE) * ROWS).astype(jnp.int32).reshape(1)

    weight_block = pl.BlockSpec((3, D, PAIR), lambda p: (0, 0, p))
    out_block = pl.BlockSpec((PAIR, D), lambda p: (p, 0))
    query, key, value, q_factor, k_factor, probs, attended, hidden, message, coarse_grad = (
        pl.pallas_call(
            fine_forward_kernel,
            grid=(PAIRS,),
            in_specs=[scalar, whole((EXTRA, D))]
            + [whole((ROWS, D))] * 6
            + [weight_block, out_block],
            out_specs=[
                pair_columns(ROWS),
                pair_columns(OWN_KEYS),
                pair_columns(OWN_KEYS),
                pair_columns(ROWS),
                pair_columns(OWN_KEYS),
                pl.BlockSpec((2, ROWS, OWN_KEYS), lambda p: (p, 0, 0)),
                pair_columns(ROWS),
                whole((ROWS, D)),
                whole((peers, 2 * COARSE, D)),
                whole((COARSE, D)),
            ],
            out_shape=[
                shaped((ROWS, D), BF),
                shaped((OWN_KEYS, D), BF),
                shaped((OWN_KEYS, D), BF),
                shaped((ROWS, D), F32),
                shaped((OWN_KEYS, D), F32),
                shaped((HEADS, ROWS, OWN_KEYS), BF),
                shaped((ROWS, D), BF),
                shaped((ROWS, D), BF),
                shaped((peers, 2 * COARSE, D), BF),
                shaped((COARSE, D), F32),
            ],
            scratch_shapes=[
                pltpu.VMEM((ALL_KEYS, D), BF),
                pltpu.VMEM((QUERIES, ALL_KEYS), F32),
                pltpu.VMEM((QUERIES, D), F32),
            ],
            compiler_params=params(32),
            cost_estimate=cost(4_500_000_000, 20_000_000, 1_600_000),
            name="fine_forward",
        )(anchor, t5, t4, t3, t2, t1, tokens, cotangent, weights, fine_out)
    )
    gathered = exchanged(message, GROUP)
    group_rows = peers * COARSE
    coarse_send, coarse_factor = pl.pallas_call(
        coarse_project_kernel,
        out_shape=[
            shaped((groups, group_rows, 2 * PAIR), BF),
            shaped((group_rows, 2 * PAIR), F32),
        ],
        compiler_params=params(16),
        cost_estimate=cost(140_000_000, 3_000_000),
        name="coarse_project",
    )(gathered, coarse_in, coarse_back)
    everyone = exchanged(coarse_send, FAR).reshape(groups * group_rows, 2 * PAIR)
    own_start = (lax.axis_index(FAR) * group_rows).astype(jnp.int32).reshape(1)
    vmem = pl.BlockSpec(memory_space=pltpu.VMEM)
    partial = pl.pallas_call(
        coarse_attention_kernel,
        in_specs=[scalar] + [vmem] * 4,
        out_shape=shaped((peers, 2 * COARSE, D), BF),
        scratch_shapes=[
            pltpu.VMEM((group_rows, PAIR), F32),
            pltpu.VMEM((groups * group_rows, PAIR), BF),
            pltpu.VMEM((groups * group_rows, PAIR), BF),
        ],
        compiler_params=params(32),
        cost_estimate=cost(1_500_000_000, 3_000_000, 3_000_000),
        name="coarse_attention",
    )(own_start, everyone, coarse_factor, coarse_in, coarse_back)
    returned = exchanged(partial, GROUP)
    spread, state = pl.pallas_call(
        coarse_finish_kernel,
        out_shape=[shaped((COARSE, D), F32), shaped((COARSE, D), F32)],
        compiler_params=params(16),
        cost_estimate=cost(1_000_000, 1_000_000),
        name="coarse_finish",
    )(returned, message[0], coarse_grad)
    after = shifted_by(spread[0:1], -1)
    state = state.astype(BF)
    output = (
        hidden.astype(F32) + jnp.repeat(state, POOL, axis=0).astype(F32)
    ).astype(BF)
    h4, h3, h2, h1, own, hidden_grad = pl.pallas_call(
        fine_backward_kernel,
        grid=(PAIRS,),
        in_specs=[
            whole((ROWS, D)),
            whole((COARSE, D)),
            whole((1, D)),
            out_block,
            weight_block,
            pair_columns(ROWS),
            pair_columns(OWN_KEYS),
            pair_columns(OWN_KEYS),
            pair_columns(ROWS),
            pair_columns(OWN_KEYS),
            pl.BlockSpec((2, ROWS, OWN_KEYS), lambda p: (p, 0, 0)),
            pair_columns(ROWS),
        ],
        out_specs=[whole((ROWS, D))] * 6,
        out_shape=[shaped((ROWS, D), BF)] * 4 + [shaped((ROWS, D), F32)] * 2,
        scratch_shapes=[pltpu.VMEM((ROWS, D), BF), pltpu.VMEM((OWN_KEYS, D), F32)],
        compiler_params=params(32),
        cost_estimate=cost(5_000_000_000, 20_000_000),
        name="fine_backward",
    )(
        cotangent, spread, after, fine_out, weights, query, key, value, q_factor, k_factor, probs,
        attended,
    )
    a1, a2, a3, a4 = (
        shifted_by(rows, -steps) for rows, steps in ((h1, 1), (h2, 2), (h3, 3), (h4, 4))
    )
    grad_tokens = pl.pallas_call(
        fine_finish_kernel,
        out_shape=shaped((ROWS, D), BF),
        compiler_params=params(16),
        cost_estimate=cost(1_000_000, 3_000_000),
        name="fine_finish",
    )(own, a1, a2, a3, a4, hidden_grad, tokens)
    return (output, grad_tokens)


def solution(mesh):
    sizes = (4, 4, 2, 2, 4)
    fine_mesh = Mesh(mesh.devices.reshape(sizes), LINE)
    placed = (
        P(LINE, None),
        P(LINE, None),
        P(),
        P(),
        P(None, None, ("z_lo", "x")),
        P(("z_lo", "x"), None),
    )
    return jax.shard_map(
        per_device,
        mesh=fine_mesh,
        in_specs=placed,
        out_specs=(P(LINE, None), P(LINE, None)),
        check_vma=False,
    )
```

```python
import jax
import jax.numpy as jnp
from jax import lax
from jax.experimental import pallas as pl
from jax.experimental.pallas import tpu as pltpu
from jax.sharding import Mesh
from jax.sharding import PartitionSpec as P

D = 1024
HEADS = 16
HEAD_DIM = 64
WINDOW = 512
POOL = 16
EPS = 1e-06

LINE = ("y", "z_hi", "core", "z_lo", "x")
GROUP = ("core", "z_lo", "x")
FAR = ("y", "z_hi")

ROWS = 128
HALO = WINDOW
OWN_KEYS = HALO + ROWS
EXTRA = 16
ALL_KEYS = OWN_KEYS + EXTRA
QUERIES = EXTRA + ROWS
PAIR = 2 * HEAD_DIM
COARSE = ROWS // POOL
SCALE = HEAD_DIM ** (-0.5)
NEG = -1e30
VMEM_MIB = 32

BF = jnp.bfloat16
F32 = jnp.float32


def shifted_by(value, steps):
    count = 1
    for name in LINE:
        count *= lax.axis_size(name)
    first, last = (max(0, -steps), min(count, count - steps))
    return lax.ppermute(value, LINE, [(source, source + steps) for source in range(first, last)])


def exchanged(pieces, axes):
    return lax.all_to_all(pieces, axes, 0, 0, tiled=True)


def last_last(left, right):
    return lax.dot_general(left, right, (((1,), (1,)), ((), ())), preferred_element_type=F32)


def first_first(left, right):
    return lax.dot_general(left, right, (((0,), (0,)), ((), ())), preferred_element_type=F32)


def plain(left, right):
    return jnp.dot(left, right, preferred_element_type=F32)


def low_lanes():
    return lax.broadcasted_iota(jnp.int32, (1, PAIR), 1) < HEAD_DIM


def pair_sums(values, low):
    low_sum = jnp.sum(jnp.where(low, values, 0.0), axis=-1, keepdims=True)
    high_sum = jnp.sum(jnp.where(low, 0.0, values), axis=-1, keepdims=True)
    return jnp.where(low, low_sum, high_sum)


def pair_norm(values, low):
    factor = lax.rsqrt(pair_sums(values * values, low) * (1.0 / HEAD_DIM) + EPS)
    return values * factor, factor


def pair_norm_back(grad, unit, factor, low):
    return factor * (grad - unit * (pair_sums(unit * grad, low) * (1.0 / HEAD_DIM)))


def row_norm(rows):
    factor = lax.rsqrt(jnp.mean(rows * rows, axis=-1, keepdims=True) + EPS)
    return rows * factor, factor


def row_norm_back(grad, normed, factor):
    return factor * (grad - normed * jnp.mean(normed * grad, axis=-1, keepdims=True))


def fine_forward_kernel(
    anchor_ref, t5, t4, t3, t2, t1, t0, cot_ref, w_ref, out_w_ref,
    q_ref, k_ref, v_ref, qf_ref, kf_ref, p_ref, att_ref, hid_ref, send_ref, cg_ref,
    normed, bias, acc,
):
    step = pl.program_id(0)
    anchor = anchor_ref[0]
    low = low_lanes()

    @pl.when(step == 0)
    def _():
        at = 0
        for ref in (t4, t3, t2, t1, t0, t5):
            rows = ref.shape[0]
            normed[at : at + rows, :] = row_norm(ref[...].astype(F32))[0].astype(BF)
            at += rows
        row = lax.broadcasted_iota(jnp.int32, (2 * QUERIES, ALL_KEYS), 0)
        query_pos = jnp.where(row < QUERIES, row, row - QUERIES) - EXTRA
        column = lax.broadcasted_iota(jnp.int32, (2 * QUERIES, ALL_KEYS), 1)
        key_pos = jnp.where(column < OWN_KEYS, column - HALO, column - (OWN_KEYS + HALO + EXTRA))
        gap = query_pos - key_pos
        allowed = (gap >= 0) & (gap < WINDOW) & (anchor + key_pos >= 0)
        bias[...] = jnp.where(allowed, 0.0, NEG)
        acc[...] = jnp.zeros_like(acc)

    width = q_ref.shape[1]
    queries = plain(normed[HALO - EXTRA : OWN_KEYS, :], w_ref[0])
    both = plain(normed[...], jnp.concatenate([w_ref[1], w_ref[2]], axis=1))
    mixed = []
    for at in range(0, width, PAIR):
        here = slice(at, at + PAIR)
        query, q_factor = pair_norm(queries[:, here], low)
        key, k_factor = pair_norm(both[:, here], low)
        value = both[:, width + at : width + at + PAIR]
        key_b = key.astype(BF)
        q_ref[:, here] = query[EXTRA:].astype(BF)
        k_ref[:, here] = key_b[:OWN_KEYS]
        v_ref[:, here] = value[:OWN_KEYS].astype(BF)
        qf_ref[:, here] = q_factor[EXTRA:]
        kf_ref[:, here] = k_factor[:OWN_KEYS]
        scaled = query * SCALE
        stacked = jnp.concatenate([jnp.where(low, scaled, 0.0), jnp.where(low, 0.0, scaled)], axis=0)
        numer = jnp.exp(last_last(stacked.astype(BF), key_b) + bias[...])
        total = jnp.sum(numer, axis=-1, keepdims=True)
        prob = (numer * (1.0 / jnp.where(total > 0.0, total, 1.0))).astype(BF)
        p_ref[at // HEAD_DIM] = prob[EXTRA:QUERIES, :OWN_KEYS]
        p_ref[at // HEAD_DIM + 1] = prob[QUERIES + EXTRA :, :OWN_KEYS]
        twice = plain(prob, value.astype(BF))
        attended = jnp.where(low, twice[:QUERIES], twice[QUERIES:])
        attended = attended.astype(BF)
        att_ref[:, here] = attended[EXTRA:]
        mixed.append(attended)
    acc[...] += plain(jnp.concatenate(mixed, axis=1), out_w_ref[...])

    @pl.when(step == pl.num_programs(0) - 1)
    def _():
        before = t1[ROWS - EXTRA :, :].astype(F32) + acc[:EXTRA, :]
        before = jnp.where(anchor > 0, before, 0.0).astype(BF)
        own = (t0[...].astype(F32) + acc[EXTRA:, :]).astype(BF)
        hid_ref[...] = own
        chunk = lax.broadcasted_iota(jnp.int32, (COARSE, QUERIES), 0) * POOL
        row = lax.broadcasted_iota(jnp.int32, (COARSE, QUERIES), 1)
        member = jnp.where((row > chunk) & (row <= chunk + POOL), 1.0, 0.0).astype(BF)
        pooled = plain(member, jnp.concatenate([before, own], axis=0)) * (1.0 / POOL)
        chunk = lax.broadcasted_iota(jnp.int32, (COARSE, ROWS), 0) * POOL
        row = lax.broadcasted_iota(jnp.int32, (COARSE, ROWS), 1)
        member = jnp.where((row >= chunk) & (row < chunk + POOL), 1.0, 0.0).astype(BF)
        coarse_grad = plain(member, cot_ref[...])
        cg_ref[...] = coarse_grad
        message = jnp.concatenate([pooled, coarse_grad], axis=0).astype(BF)
        for peer in range(send_ref.shape[0]):
            send_ref[peer] = message


def coarse_project_kernel(got_ref, in_w_ref, out_w_ref, send_ref, factor_ref):
    low = low_lanes()
    rows = got_ref[...].astype(F32)
    count = rows.shape[0] * COARSE
    pooled = rows[:, :COARSE, :].reshape(count, D)
    coarse_grad = rows[:, COARSE:, :].reshape(count, D)
    normed = row_norm(pooled)[0].astype(BF)
    raw = plain(normed, in_w_ref[...]) + last_last(coarse_grad.astype(BF), out_w_ref[...])
    units, factors = [], []
    for tile in (raw[:, :PAIR], raw[:, PAIR:]):
        unit, factor = pair_norm(tile, low)
        units.append(jnp.where(low, unit, tile))
        factors.append(factor)
    message = jnp.concatenate(units, axis=1).astype(BF)
    factor_ref[...] = jnp.concatenate(factors, axis=1)
    for peer in range(send_ref.shape[0]):
        send_ref[peer] = message


def coarse_attention_kernel(start_ref, got_ref, factor_ref, in_w_ref, out_w_ref, send_ref, own_grad):
    low = low_lanes()
    own_start = pl.multiple_of(start_ref[0], ROWS)
    length = got_ref.shape[0]
    block = 512
    own_left = got_ref[pl.ds(own_start, ROWS), :PAIR]
    own_right = got_ref[pl.ds(own_start, ROWS), PAIR:]
    own_grad[...] = jnp.zeros_like(own_grad)

    def masked_halves(tile):
        wide = tile.astype(F32)
        return (
            jnp.where(low, wide * SCALE, 0.0).astype(BF),
            jnp.where(low, 0.0, wide).astype(BF),
        )

    def lane_partials(values):
        total = values[:, :PAIR]
        for at in range(PAIR, values.shape[1], PAIR):
            total = total + values[:, at : at + PAIR]
        return total

    def one_block(index, carry):
        first = pl.multiple_of(index * block, block)
        query, grad = masked_halves(got_ref[pl.ds(first, block), :PAIR])
        stacked = jnp.concatenate([query, grad], axis=0)

        def scored(keys):
            both = last_last(stacked, keys)
            return jnp.exp(both[:block]), both[block:]

        def one_chunk(at, sums):
            total, product = sums
            numer, prob_grad = scored(got_ref[pl.ds(pl.multiple_of(at * block, block), block), PAIR:])
            return total + lane_partials(numer), product + lane_partials(numer * prob_grad)

        nothing = jnp.zeros((block, PAIR), F32)
        total, product = lax.fori_loop(0, index, one_chunk, (nothing, nothing))
        numer, prob_grad = scored(got_ref[pl.ds(first, block), PAIR:])
        query_at = lax.broadcasted_iota(jnp.int32, (block, 1), 0)
        numer = jnp.where(lax.broadcasted_iota(jnp.int32, (1, block), 1) <= query_at, numer, 0.0)
        total = jnp.sum(total + lane_partials(numer), axis=-1, keepdims=True)
        product = jnp.sum(product + lane_partials(numer * prob_grad), axis=-1, keepdims=True)
        inverse = 1.0 / total
        delta = product * inverse
        own_pos = own_start + lax.broadcasted_iota(jnp.int32, (1, ROWS), 1)
        numer, prob_grad = scored(own_right)
        numer = jnp.where(own_pos <= query_at + first, numer, 0.0)
        prob = numer * inverse
        score_grad = (prob * (prob_grad - delta)).astype(BF)
        own_grad[...] += first_first(
            jnp.concatenate([score_grad, prob.astype(BF)], axis=0), stacked
        )
        return carry

    lax.fori_loop(own_start // block, length // block, one_block, 0)

    query, grad = masked_halves(own_left)
    query_pos = own_start + lax.broadcasted_iota(jnp.int32, (ROWS, 1), 0)
    key_pos = lax.broadcasted_iota(jnp.int32, (1, length), 1)
    keys = got_ref[:, PAIR:]
    key_scaled, value = masked_halves(keys)
    numer = jnp.where(key_pos <= query_pos, jnp.exp(last_last(query, keys)), 0.0)
    prob_grad = last_last(grad, keys)
    inverse = 1.0 / jnp.sum(numer, axis=-1, keepdims=True)
    delta = jnp.sum(numer * prob_grad, axis=-1, keepdims=True) * inverse
    prob = numer * inverse
    score_grad = (prob * (prob_grad - delta)).astype(BF)
    mine = plain(score_grad, key_scaled) + plain(prob.astype(BF), value)

    parts = []
    for tile, unit, factor in (
        (mine, own_left, factor_ref[:, :PAIR]),
        (own_grad[...], own_right, factor_ref[:, PAIR:]),
    ):
        back = pair_norm_back(tile, unit.astype(F32), factor, low)
        parts.append(jnp.where(low, back, tile))
    parts = jnp.concatenate(parts, axis=1).astype(BF)
    peers = send_ref.shape[0]
    normed_grad = last_last(parts, in_w_ref[...]).reshape(peers, COARSE, D)
    mixed = plain(parts, out_w_ref[...]).reshape(peers, COARSE, D)
    send_ref[...] = jnp.concatenate([normed_grad, mixed], axis=1).astype(BF)


def coarse_finish_kernel(got_ref, pooled_ref, cg_ref, spread_ref, state_ref):
    summed = jnp.sum(got_ref[...].astype(F32), axis=0)
    pooled = pooled_ref[...].astype(F32)[:COARSE]
    normed, factor = row_norm(pooled)
    pooled_grad = cg_ref[...] + row_norm_back(summed[:COARSE], normed, factor)
    spread_ref[...] = pooled_grad * (1.0 / POOL)
    state_ref[...] = pooled + summed[COARSE:]


def fine_backward_kernel(
    cot_ref, spread_ref, next_ref, out_w_ref, w_ref, q_ref, k_ref, v_ref, qf_ref, kf_ref, p_ref,
    att_ref,
    h4, h3, h2, h1, own_ref, hg_ref,
    hidden_grad, acc,
):
    step = pl.program_id(0)
    low = low_lanes()

    @pl.when(step == 0)
    def _():
        block = (lax.broadcasted_iota(jnp.int32, (ROWS, 1), 0) + (POOL - 1)) // POOL
        added = jnp.zeros((ROWS, D), F32)
        for at in range(COARSE):
            added = jnp.where(block == at, spread_ref[at : at + 1, :], added)
        added = jnp.where(block == COARSE, next_ref[0:1, :], added)
        total = cot_ref[...].astype(F32) + added
        hg_ref[...] = total
        hidden_grad[...] = total.astype(BF)
        acc[...] = jnp.zeros_like(acc)

    width = q_ref.shape[1]
    att_grads = last_last(hidden_grad[...], out_w_ref[...]).astype(BF).astype(F32)
    query_grads, key_grads, value_grads = [], [], []
    for at in range(0, width, PAIR):
        here = slice(at, at + PAIR)
        att_grad = att_grads[:, here]
        delta_all = att_grad * att_ref[:, here].astype(F32)
        value = v_ref[:, here]
        key_wide = k_ref[:, here].astype(F32)
        query_wide = q_ref[:, here].astype(F32)
        grad = jnp.concatenate(
            [jnp.where(low, att_grad, 0.0), jnp.where(low, 0.0, att_grad)], axis=0
        ).astype(BF)
        delta = jnp.sum(
            jnp.concatenate([jnp.where(low, delta_all, 0.0), jnp.where(low, 0.0, delta_all)], axis=0),
            axis=-1,
            keepdims=True,
        )
        scaled = query_wide * SCALE
        query = jnp.concatenate(
            [jnp.where(low, scaled, 0.0), jnp.where(low, 0.0, scaled)], axis=0
        ).astype(BF)
        first = at // HEAD_DIM
        prob = p_ref[first : first + 2].reshape(2 * ROWS, OWN_KEYS)
        score_grad = (prob.astype(F32) * (last_last(grad, value) - delta)).astype(BF)
        twice = plain(score_grad, (key_wide * SCALE).astype(BF))
        query_grad = jnp.where(low, twice[:ROWS], twice[ROWS:])
        key_grad = first_first(score_grad, query)
        value_grad = first_first(prob, grad)
        query_grads.append(pair_norm_back(query_grad, query_wide, qf_ref[:, here], low).astype(BF))
        key_grads.append(pair_norm_back(key_grad, key_wide, kf_ref[:, here], low).astype(BF))
        value_grads.append(value_grad.astype(BF))
    both = jnp.concatenate(key_grads + value_grads, axis=1)
    acc[...] += last_last(both, jnp.concatenate([w_ref[1], w_ref[2]], axis=1))
    acc[HALO:, :] += last_last(jnp.concatenate(query_grads, axis=1), w_ref[0])

    @pl.when(step == pl.num_programs(0) - 1)
    def _():
        for at, ref in enumerate((h4, h3, h2, h1)):
            ref[...] = acc[at * ROWS : (at + 1) * ROWS, :].astype(BF)
        own_ref[...] = acc[HALO:, :]


def fine_finish_kernel(own_ref, a1, a2, a3, a4, hg_ref, tokens_ref, out_ref):
    total = own_ref[...]
    for ref in (a1, a2, a3, a4):
        total = total + ref[...].astype(F32)
    normed, factor = row_norm(tokens_ref[...].astype(F32))
    out_ref[...] = (hg_ref[...] + row_norm_back(total, normed, factor)).astype(BF)


def whole(shape):
    return pl.BlockSpec(shape, lambda *_: (0,) * len(shape))


def columns(rows, width):
    return pl.BlockSpec((rows, width), lambda p: (0, p))


def shaped(shape, kind):
    return jax.ShapeDtypeStruct(shape, kind)


def params(mib):
    return pltpu.CompilerParams(vmem_limit_bytes=mib << 20)


def cost(flops, moved, exps=0):
    return pl.CostEstimate(flops=flops, bytes_accessed=moved, transcendentals=exps)


SCALAR = pl.BlockSpec(memory_space=pltpu.SMEM)
IN_VMEM = pl.BlockSpec(memory_space=pltpu.VMEM)
FORWARD_WIDTH = 2 * PAIR
BACKWARD_WIDTH = 2 * PAIR


def in_hbm(x):
    return pltpu.with_memory_space_constraint(x, pltpu.HBM)


def fine_forward(anchor, t5, t4, t3, t2, t1, tokens, cotangent, weights, fine_out, peers):
    width = FORWARD_WIDTH
    return pl.pallas_call(
        fine_forward_kernel,
        grid=(D // width,),
        in_specs=[SCALAR, whole((EXTRA, D))]
        + [whole((ROWS, D))] * 6
        + [
            pl.BlockSpec((3, D, width), lambda p: (0, 0, p)),
            pl.BlockSpec((width, D), lambda p: (p, 0)),
        ],
        out_specs=[
            columns(ROWS, width),
            columns(OWN_KEYS, width),
            columns(OWN_KEYS, width),
            columns(ROWS, width),
            columns(OWN_KEYS, width),
            pl.BlockSpec((width // HEAD_DIM, ROWS, OWN_KEYS), lambda p: (p, 0, 0)),
            columns(ROWS, width),
            whole((ROWS, D)),
            whole((peers, 2 * COARSE, D)),
            whole((COARSE, D)),
        ],
        out_shape=[
            pltpu.HBM((ROWS, D), BF),
            pltpu.HBM((OWN_KEYS, D), BF),
            pltpu.HBM((OWN_KEYS, D), BF),
            pltpu.HBM((ROWS, D), F32),
            pltpu.HBM((OWN_KEYS, D), F32),
            pltpu.HBM((HEADS, ROWS, OWN_KEYS), BF),
            pltpu.HBM((ROWS, D), BF),
            pltpu.HBM((ROWS, D), BF),
            shaped((peers, 2 * COARSE, D), BF),
            shaped((COARSE, D), F32),
        ],
        scratch_shapes=[
            pltpu.VMEM((ALL_KEYS, D), BF),
            pltpu.VMEM((2 * QUERIES, ALL_KEYS), F32),
            pltpu.VMEM((QUERIES, D), F32),
        ],
        compiler_params=params(VMEM_MIB),
        cost_estimate=cost(4_500_000_000, 20_000_000, 1_600_000),
        name="fine_forward",
    )(
        anchor, t5, t4, t3, t2, t1, in_hbm(tokens), in_hbm(cotangent), in_hbm(weights),
        in_hbm(fine_out),
    )


def coarse_project(gathered, coarse_in, coarse_back, groups):
    rows = gathered.shape[0] * COARSE
    return pl.pallas_call(
        coarse_project_kernel,
        out_shape=[shaped((groups, rows, 2 * PAIR), BF), shaped((rows, 2 * PAIR), F32)],
        compiler_params=params(VMEM_MIB),
        cost_estimate=cost(140_000_000, 3_000_000),
        name="coarse_project",
    )(gathered, coarse_in, coarse_back)


def coarse_attention(own_start, everyone, factor, coarse_in, coarse_back):
    rows = factor.shape[0]
    return pl.pallas_call(
        coarse_attention_kernel,
        in_specs=[SCALAR] + [IN_VMEM] * 4,
        out_shape=shaped((rows // COARSE, 2 * COARSE, D), BF),
        scratch_shapes=[pltpu.VMEM((rows, PAIR), F32)],
        compiler_params=params(VMEM_MIB),
        cost_estimate=cost(1_500_000_000, 3_000_000, 3_000_000),
        name="coarse_attention",
    )(own_start, everyone, factor, coarse_in, coarse_back)


def coarse_finish(returned, pooled, coarse_grad):
    return pl.pallas_call(
        coarse_finish_kernel,
        out_shape=[shaped((COARSE, D), F32), shaped((COARSE, D), F32)],
        compiler_params=params(VMEM_MIB),
        cost_estimate=cost(1_000_000, 1_000_000),
        name="coarse_finish",
    )(returned, pooled, coarse_grad)


def fine_backward(
    cotangent, spread, after, fine_out, weights, query, key, value, q_factor, k_factor, probs,
    attended,
):
    width = BACKWARD_WIDTH
    return pl.pallas_call(
        fine_backward_kernel,
        grid=(D // width,),
        in_specs=[
            whole((ROWS, D)),
            whole((COARSE, D)),
            whole((1, D)),
            pl.BlockSpec((width, D), lambda p: (p, 0)),
            pl.BlockSpec((3, D, width), lambda p: (0, 0, p)),
            columns(ROWS, width),
            columns(OWN_KEYS, width),
            columns(OWN_KEYS, width),
            columns(ROWS, width),
            columns(OWN_KEYS, width),
            pl.BlockSpec((width // HEAD_DIM, ROWS, OWN_KEYS), lambda p: (p, 0, 0)),
            columns(ROWS, width),
        ],
        out_specs=[whole((ROWS, D))] * 6,
        out_shape=[shaped((ROWS, D), BF)] * 4 + [shaped((ROWS, D), F32)] * 2,
        scratch_shapes=[pltpu.VMEM((ROWS, D), BF), pltpu.VMEM((OWN_KEYS, D), F32)],
        compiler_params=params(VMEM_MIB),
        cost_estimate=cost(5_000_000_000, 20_000_000),
        name="fine_backward",
    )(
        in_hbm(cotangent), spread, after,
        *(in_hbm(x) for x in (fine_out, weights, query, key, value, q_factor, k_factor, probs)),
        in_hbm(attended),
    )


def fine_finish(own, arrived, hidden_grad, tokens):
    return pl.pallas_call(
        fine_finish_kernel,
        out_shape=shaped((ROWS, D), BF),
        compiler_params=params(VMEM_MIB),
        cost_estimate=cost(1_000_000, 3_000_000),
        name="fine_finish",
    )(own, *arrived, hidden_grad, tokens)


def per_device(tokens, cotangent, fine_qkv, fine_out, coarse_qkv, coarse_out):
    peers = 1
    for name in GROUP:
        peers *= lax.axis_size(name)
    groups = 1
    for name in FAR:
        groups *= lax.axis_size(name)
    core = lax.axis_index("core")
    weights = jnp.transpose(fine_qkv, (1, 0, 2))
    coarse_all = jnp.transpose(coarse_qkv, (1, 0, 2))
    picked = jnp.where(core == 0, coarse_all[:, :, :HEAD_DIM], coarse_all[:, :, HEAD_DIM:])
    blank = jnp.zeros((D, HEAD_DIM), BF)
    coarse_in = jnp.concatenate([picked[0], blank, picked[1], picked[2]], axis=1)
    picked_out = jnp.where(core == 0, coarse_out[:HEAD_DIM], coarse_out[HEAD_DIM:])
    coarse_back = jnp.pad(picked_out, ((HEAD_DIM, PAIR), (0, 0)))

    t1, t2, t3, t4 = (shifted_by(tokens, steps) for steps in (1, 2, 3, 4))
    t5 = shifted_by(tokens[ROWS - EXTRA :], 5)
    anchor = (lax.axis_index(LINE) * ROWS).astype(jnp.int32).reshape(1)

    query, key, value, q_factor, k_factor, probs, attended, hidden, message, coarse_grad = (
        fine_forward(anchor, t5, t4, t3, t2, t1, tokens, cotangent, weights, fine_out, peers)
    )
    gathered = exchanged(message, GROUP)
    coarse_send, coarse_factor = coarse_project(gathered, coarse_in, coarse_back, groups)
    group_rows = coarse_factor.shape[0]
    everyone = exchanged(coarse_send, FAR).reshape(groups * group_rows, 2 * PAIR)
    own_start = (lax.axis_index(FAR) * group_rows).astype(jnp.int32).reshape(1)
    partial = coarse_attention(own_start, everyone, coarse_factor, coarse_in, coarse_back)
    returned = exchanged(partial, GROUP)
    spread, state = coarse_finish(returned, message[0], coarse_grad)
    after = shifted_by(spread[0:1], -1)
    output = (
        hidden.astype(F32) + jnp.repeat(state.astype(BF), POOL, axis=0).astype(F32)
    ).astype(BF)
    h4, h3, h2, h1, own, hidden_grad = fine_backward(
        cotangent, spread, after, fine_out, weights, query, key, value, q_factor, k_factor, probs,
        attended,
    )
    arrived = [shifted_by(rows, -steps) for rows, steps in ((h1, 1), (h2, 2), (h3, 3), (h4, 4))]
    return (output, fine_finish(own, arrived, hidden_grad, tokens))


def solution(mesh):
    sizes = (4, 4, 2, 2, 4)
    fine_mesh = Mesh(mesh.devices.reshape(sizes), LINE)
    placed = (
        P(LINE, None),
        P(LINE, None),
        P(),
        P(),
        P(None, None, ("z_lo", "x")),
        P(("z_lo", "x"), None),
    )
    return jax.shard_map(
        per_device,
        mesh=fine_mesh,
        in_specs=placed,
        out_specs=(P(LINE, None), P(LINE, None)),
        check_vma=False,
    )
```

```python
import jax
import jax.numpy as jnp
from jax import lax
from jax.experimental import pallas as pl
from jax.experimental.pallas import tpu as pltpu
from jax.sharding import Mesh
from jax.sharding import PartitionSpec as P

D = 1024
HEADS = 16
HEAD_DIM = 64
WINDOW = 512
POOL = 16
EPS = 1e-06

LINE = ("y", "z_hi", "core", "z_lo", "x")
GROUP = ("core", "z_lo", "x")
FAR = ("y", "z_hi")

ROWS = 128
HALO = WINDOW
OWN_KEYS = HALO + ROWS
EXTRA = 16
ALL_KEYS = OWN_KEYS + EXTRA
QUERIES = EXTRA + ROWS
PAIR = 2 * HEAD_DIM
COARSE = ROWS // POOL
SCALE = HEAD_DIM ** (-0.5)
NEG = -1e30
VMEM_MIB = 32

BF = jnp.bfloat16
F32 = jnp.float32


def shifted_by(value, steps):
    count = 1
    for name in LINE:
        count *= lax.axis_size(name)
    first, last = (max(0, -steps), min(count, count - steps))
    return lax.ppermute(value, LINE, [(source, source + steps) for source in range(first, last)])


def exchanged(pieces, axes):
    return lax.all_to_all(pieces, axes, 0, 0, tiled=True)


def last_last(left, right):
    return lax.dot_general(left, right, (((1,), (1,)), ((), ())), preferred_element_type=F32)


def first_first(left, right):
    return lax.dot_general(left, right, (((0,), (0,)), ((), ())), preferred_element_type=F32)


def plain(left, right):
    return jnp.dot(left, right, preferred_element_type=F32)


def low_lanes():
    return lax.broadcasted_iota(jnp.int32, (1, PAIR), 1) < HEAD_DIM


def pair_sums(values, low):
    low_sum = jnp.sum(jnp.where(low, values, 0.0), axis=-1, keepdims=True)
    high_sum = jnp.sum(jnp.where(low, 0.0, values), axis=-1, keepdims=True)
    return jnp.where(low, low_sum, high_sum)


def pair_norm(values, low):
    factor = lax.rsqrt(pair_sums(values * values, low) * (1.0 / HEAD_DIM) + EPS)
    return values * factor, factor


def pair_norm_back(grad, unit, factor, low):
    return factor * (grad - unit * (pair_sums(unit * grad, low) * (1.0 / HEAD_DIM)))


def row_norm(rows):
    factor = lax.rsqrt(jnp.mean(rows * rows, axis=-1, keepdims=True) + EPS)
    return rows * factor, factor


def row_norm_back(grad, normed, factor):
    return factor * (grad - normed * jnp.mean(normed * grad, axis=-1, keepdims=True))


def fine_forward_kernel(
    place_ref, tail_ref, slots_ref, own_ref, cot_ref, w_ref, out_w_ref,
    q_ref, k_ref, v_ref, qf_ref, kf_ref, p_ref, att_ref, hid_ref, send_ref, cg_ref,
    normed, bias, acc,
):
    step = pl.program_id(0)
    anchor = place_ref[0]
    column_at = place_ref[1]
    low = low_lanes()
    slots = slots_ref.shape[0]
    nearest = lax.rem(column_at + (slots - 1), slots)

    @pl.when(step == 0)
    def _():
        for slot in range(slots):
            at = slot * ROWS
            normed[at : at + ROWS, :] = row_norm(slots_ref[slot].astype(F32))[0].astype(BF)
        normed[HALO:OWN_KEYS, :] = row_norm(own_ref[...].astype(F32))[0].astype(BF)
        normed[OWN_KEYS:, :] = row_norm(tail_ref[...].astype(F32))[0].astype(BF)
        row = lax.broadcasted_iota(jnp.int32, (2 * QUERIES, ALL_KEYS), 0)
        query_pos = jnp.where(row < QUERIES, row, row - QUERIES) - EXTRA
        column = lax.broadcasted_iota(jnp.int32, (2 * QUERIES, ALL_KEYS), 1)
        halo_pos = column - jnp.where(column >= column_at * ROWS, column_at * ROWS + HALO, column_at * ROWS)
        key_pos = jnp.where(
            column < HALO,
            halo_pos,
            jnp.where(column < OWN_KEYS, column - HALO, column - (OWN_KEYS + HALO + EXTRA)),
        )
        gap = query_pos - key_pos
        allowed = (gap >= 0) & (gap < WINDOW) & (anchor + key_pos >= 0)
        bias[...] = jnp.where(allowed, 0.0, NEG)
        acc[...] = jnp.zeros_like(acc)

    width = q_ref.shape[1]
    extra_at = pl.multiple_of(nearest * ROWS + (ROWS - EXTRA), EXTRA)
    query_rows = jnp.concatenate([normed[pl.ds(extra_at, EXTRA), :], normed[HALO:OWN_KEYS, :]], axis=0)
    queries = plain(query_rows, w_ref[0])
    both = plain(normed[...], jnp.concatenate([w_ref[1], w_ref[2]], axis=1))
    mixed = []
    for at in range(0, width, PAIR):
        here = slice(at, at + PAIR)
        query, q_factor = pair_norm(queries[:, here], low)
        key, k_factor = pair_norm(both[:, here], low)
        value = both[:, width + at : width + at + PAIR]
        key_b = key.astype(BF)
        q_ref[:, here] = query[EXTRA:].astype(BF)
        k_ref[:, here] = key_b[:OWN_KEYS]
        v_ref[:, here] = value[:OWN_KEYS].astype(BF)
        qf_ref[:, here] = q_factor[EXTRA:]
        kf_ref[:, here] = k_factor[:OWN_KEYS]
        scaled = query * SCALE
        stacked = jnp.concatenate([jnp.where(low, scaled, 0.0), jnp.where(low, 0.0, scaled)], axis=0)
        numer = jnp.exp(last_last(stacked.astype(BF), key_b) + bias[...])
        total = jnp.sum(numer, axis=-1, keepdims=True)
        prob = (numer * (1.0 / jnp.where(total > 0.0, total, 1.0))).astype(BF)
        p_ref[at // HEAD_DIM] = prob[EXTRA:QUERIES, :OWN_KEYS]
        p_ref[at // HEAD_DIM + 1] = prob[QUERIES + EXTRA :, :OWN_KEYS]
        twice = plain(prob, value.astype(BF))
        attended = jnp.where(low, twice[:QUERIES], twice[QUERIES:])
        attended = attended.astype(BF)
        att_ref[:, here] = attended[EXTRA:]
        mixed.append(attended)
    acc[...] += plain(jnp.concatenate(mixed, axis=1), out_w_ref[...])

    @pl.when(step == pl.num_programs(0) - 1)
    def _():
        before = slots_ref[nearest, ROWS - EXTRA :, :].astype(F32) + acc[:EXTRA, :]
        before = jnp.where(anchor > 0, before, 0.0).astype(BF)
        own = (own_ref[...].astype(F32) + acc[EXTRA:, :]).astype(BF)
        hid_ref[...] = own
        chunk = lax.broadcasted_iota(jnp.int32, (COARSE, QUERIES), 0) * POOL
        row = lax.broadcasted_iota(jnp.int32, (COARSE, QUERIES), 1)
        member = jnp.where((row > chunk) & (row <= chunk + POOL), 1.0, 0.0).astype(BF)
        pooled = plain(member, jnp.concatenate([before, own], axis=0)) * (1.0 / POOL)
        chunk = lax.broadcasted_iota(jnp.int32, (COARSE, ROWS), 0) * POOL
        row = lax.broadcasted_iota(jnp.int32, (COARSE, ROWS), 1)
        member = jnp.where((row >= chunk) & (row < chunk + POOL), 1.0, 0.0).astype(BF)
        coarse_grad = plain(member, cot_ref[...])
        cg_ref[...] = coarse_grad
        message = jnp.concatenate([pooled, coarse_grad], axis=0).astype(BF)
        for peer in range(send_ref.shape[0]):
            send_ref[peer] = message


def coarse_project_kernel(got_ref, in_w_ref, out_w_ref, send_ref, factor_ref):
    low = low_lanes()
    rows = got_ref[...].astype(F32)
    count = rows.shape[0] * COARSE
    pooled = rows[:, :COARSE, :].reshape(count, D)
    coarse_grad = rows[:, COARSE:, :].reshape(count, D)
    normed = row_norm(pooled)[0].astype(BF)
    raw = plain(normed, in_w_ref[...]) + last_last(coarse_grad.astype(BF), out_w_ref[...])
    units, factors = [], []
    for tile in (raw[:, :PAIR], raw[:, PAIR:]):
        unit, factor = pair_norm(tile, low)
        units.append(jnp.where(low, unit, tile))
        factors.append(factor)
    message = jnp.concatenate(units, axis=1).astype(BF)
    factor_ref[...] = jnp.concatenate(factors, axis=1)
    for peer in range(send_ref.shape[0]):
        send_ref[peer] = message


def coarse_attention_kernel(start_ref, got_ref, factor_ref, in_w_ref, out_w_ref, send_ref, own_grad):
    low = low_lanes()
    own_start = pl.multiple_of(start_ref[0], ROWS)
    length = got_ref.shape[0]
    block = 512
    own_left = got_ref[pl.ds(own_start, ROWS), :PAIR]
    own_right = got_ref[pl.ds(own_start, ROWS), PAIR:]
    own_grad[...] = jnp.zeros_like(own_grad)

    def masked_halves(tile):
        wide = tile.astype(F32)
        return (
            jnp.where(low, wide * SCALE, 0.0).astype(BF),
            jnp.where(low, 0.0, wide).astype(BF),
        )

    def lane_partials(values):
        total = values[:, :PAIR]
        for at in range(PAIR, values.shape[1], PAIR):
            total = total + values[:, at : at + PAIR]
        return total

    def one_block(index, carry):
        first = pl.multiple_of(index * block, block)
        query, grad = masked_halves(got_ref[pl.ds(first, block), :PAIR])
        stacked = jnp.concatenate([query, grad], axis=0)

        def scored(keys):
            both = last_last(stacked, keys)
            return jnp.exp(both[:block]), both[block:]

        def one_chunk(at, sums):
            total, product = sums
            numer, prob_grad = scored(got_ref[pl.ds(pl.multiple_of(at * block, block), block), PAIR:])
            return total + lane_partials(numer), product + lane_partials(numer * prob_grad)

        nothing = jnp.zeros((block, PAIR), F32)
        total, product = lax.fori_loop(0, index, one_chunk, (nothing, nothing))
        numer, prob_grad = scored(got_ref[pl.ds(first, block), PAIR:])
        query_at = lax.broadcasted_iota(jnp.int32, (block, 1), 0)
        numer = jnp.where(lax.broadcasted_iota(jnp.int32, (1, block), 1) <= query_at, numer, 0.0)
        total = jnp.sum(total + lane_partials(numer), axis=-1, keepdims=True)
        product = jnp.sum(product + lane_partials(numer * prob_grad), axis=-1, keepdims=True)
        inverse = 1.0 / total
        delta = product * inverse
        own_pos = own_start + lax.broadcasted_iota(jnp.int32, (1, ROWS), 1)
        numer, prob_grad = scored(own_right)
        numer = jnp.where(own_pos <= query_at + first, numer, 0.0)
        prob = numer * inverse
        score_grad = (prob * (prob_grad - delta)).astype(BF)
        own_grad[...] += first_first(
            jnp.concatenate([score_grad, prob.astype(BF)], axis=0), stacked
        )
        return carry

    lax.fori_loop(own_start // block, length // block, one_block, 0)

    query, grad = masked_halves(own_left)
    query_pos = own_start + lax.broadcasted_iota(jnp.int32, (ROWS, 1), 0)
    key_pos = lax.broadcasted_iota(jnp.int32, (1, length), 1)
    keys = got_ref[:, PAIR:]
    key_scaled, value = masked_halves(keys)
    numer = jnp.where(key_pos <= query_pos, jnp.exp(last_last(query, keys)), 0.0)
    prob_grad = last_last(grad, keys)
    inverse = 1.0 / jnp.sum(numer, axis=-1, keepdims=True)
    delta = jnp.sum(numer * prob_grad, axis=-1, keepdims=True) * inverse
    prob = numer * inverse
    score_grad = (prob * (prob_grad - delta)).astype(BF)
    mine = plain(score_grad, key_scaled) + plain(prob.astype(BF), value)

    parts = []
    for tile, unit, factor in (
        (mine, own_left, factor_ref[:, :PAIR]),
        (own_grad[...], own_right, factor_ref[:, PAIR:]),
    ):
        back = pair_norm_back(tile, unit.astype(F32), factor, low)
        parts.append(jnp.where(low, back, tile))
    parts = jnp.concatenate(parts, axis=1).astype(BF)
    peers = send_ref.shape[0]
    normed_grad = last_last(parts, in_w_ref[...]).reshape(peers, COARSE, D)
    mixed = plain(parts, out_w_ref[...]).reshape(peers, COARSE, D)
    send_ref[...] = jnp.concatenate([normed_grad, mixed], axis=1).astype(BF)


def coarse_finish_kernel(got_ref, message_ref, cg_ref, spread_ref, first_ref, state_ref):
    summed = jnp.sum(got_ref[...].astype(F32), axis=0)
    pooled = message_ref[0].astype(F32)[:COARSE]
    normed, factor = row_norm(pooled)
    pooled_grad = cg_ref[...] + row_norm_back(summed[:COARSE], normed, factor)
    spread = pooled_grad * (1.0 / POOL)
    spread_ref[...] = spread
    first_ref[...] = spread[:1]
    state_ref[...] = pooled + summed[COARSE:]


def fine_backward_kernel(
    cot_ref, spread_ref, next_ref, out_w_ref, w_ref, q_ref, k_ref, v_ref, qf_ref, kf_ref, p_ref,
    att_ref,
    halo_ref, own_ref, hg_ref, hidden_grad, acc,
):
    step = pl.program_id(0)
    low = low_lanes()

    @pl.when(step == 0)
    def _():
        block = (lax.broadcasted_iota(jnp.int32, (ROWS, 1), 0) + (POOL - 1)) // POOL
        added = jnp.zeros((ROWS, D), F32)
        for at in range(COARSE):
            added = jnp.where(block == at, spread_ref[at : at + 1, :], added)
        added = jnp.where(block == COARSE, next_ref[0:1, :], added)
        total = cot_ref[...].astype(F32) + added
        hg_ref[...] = total
        hidden_grad[...] = total.astype(BF)
        acc[...] = jnp.zeros_like(acc)

    width = q_ref.shape[1]
    att_grads = last_last(hidden_grad[...], out_w_ref[...]).astype(BF).astype(F32)
    query_grads, key_grads, value_grads = [], [], []
    for at in range(0, width, PAIR):
        here = slice(at, at + PAIR)
        att_grad = att_grads[:, here]
        delta_all = att_grad * att_ref[:, here].astype(F32)
        value = v_ref[:, here]
        key_wide = k_ref[:, here].astype(F32)
        query_wide = q_ref[:, here].astype(F32)
        grad = jnp.concatenate(
            [jnp.where(low, att_grad, 0.0), jnp.where(low, 0.0, att_grad)], axis=0
        ).astype(BF)
        delta = jnp.sum(
            jnp.concatenate([jnp.where(low, delta_all, 0.0), jnp.where(low, 0.0, delta_all)], axis=0),
            axis=-1,
            keepdims=True,
        )
        scaled = query_wide * SCALE
        query = jnp.concatenate(
            [jnp.where(low, scaled, 0.0), jnp.where(low, 0.0, scaled)], axis=0
        ).astype(BF)
        first = at // HEAD_DIM
        prob = p_ref[first : first + 2].reshape(2 * ROWS, OWN_KEYS)
        score_grad = (prob.astype(F32) * (last_last(grad, value) - delta)).astype(BF)
        twice = plain(score_grad, (key_wide * SCALE).astype(BF))
        query_grad = jnp.where(low, twice[:ROWS], twice[ROWS:])
        key_grad = first_first(score_grad, query)
        value_grad = first_first(prob, grad)
        query_grads.append(pair_norm_back(query_grad, query_wide, qf_ref[:, here], low).astype(BF))
        key_grads.append(pair_norm_back(key_grad, key_wide, kf_ref[:, here], low).astype(BF))
        value_grads.append(value_grad.astype(BF))
    both = jnp.concatenate(key_grads + value_grads, axis=1)
    acc[...] += last_last(both, jnp.concatenate([w_ref[1], w_ref[2]], axis=1))
    acc[HALO:, :] += last_last(jnp.concatenate(query_grads, axis=1), w_ref[0])

    @pl.when(step == pl.num_programs(0) - 1)
    def _():
        for slot in range(halo_ref.shape[0]):
            halo_ref[slot] = acc[slot * ROWS : (slot + 1) * ROWS, :].astype(BF)
        own_ref[...] = acc[HALO:, :]


def halo_sum_kernel(place_ref, got_ref, back_ref):
    column_at = place_ref[1]
    total = got_ref[0].astype(F32)
    for slot in range(1, got_ref.shape[0]):
        total = total + jnp.where(column_at >= slot, got_ref[slot].astype(F32), 0.0)
    back_ref[...] = total.astype(BF)


def fine_finish_kernel(place_ref, own_ref, got_ref, arrived_ref, hg_ref, tokens_ref, out_ref):
    column_at = place_ref[1]
    total = own_ref[...] + arrived_ref[...].astype(F32)
    for slot in range(1, got_ref.shape[0]):
        total = total + jnp.where(column_at < slot, got_ref[slot].astype(F32), 0.0)
    normed, factor = row_norm(tokens_ref[...].astype(F32))
    out_ref[...] = (hg_ref[...] + row_norm_back(total, normed, factor)).astype(BF)


def whole(shape):
    return pl.BlockSpec(shape, lambda *_: (0,) * len(shape))


def columns(rows, width):
    return pl.BlockSpec((rows, width), lambda p: (0, p))


def shaped(shape, kind):
    return jax.ShapeDtypeStruct(shape, kind)


def params(mib):
    return pltpu.CompilerParams(vmem_limit_bytes=mib << 20)


def cost(flops, moved, exps=0):
    return pl.CostEstimate(flops=flops, bytes_accessed=moved, transcendentals=exps)


SCALAR = pl.BlockSpec(memory_space=pltpu.SMEM)
IN_VMEM = pl.BlockSpec(memory_space=pltpu.VMEM)
FORWARD_WIDTH = 2 * PAIR
BACKWARD_WIDTH = 2 * PAIR


def in_hbm(x):
    return pltpu.with_memory_space_constraint(x, pltpu.HBM)


def fine_forward(place, tail, slots, tokens, cotangent, weights, fine_out, peers):
    width = FORWARD_WIDTH
    return pl.pallas_call(
        fine_forward_kernel,
        grid=(D // width,),
        in_specs=[SCALAR, whole((EXTRA, D)), whole(slots.shape)]
        + [whole((ROWS, D))] * 2
        + [
            pl.BlockSpec((3, D, width), lambda p: (0, 0, p)),
            pl.BlockSpec((width, D), lambda p: (p, 0)),
        ],
        out_specs=[
            columns(ROWS, width),
            columns(OWN_KEYS, width),
            columns(OWN_KEYS, width),
            columns(ROWS, width),
            columns(OWN_KEYS, width),
            pl.BlockSpec((width // HEAD_DIM, ROWS, OWN_KEYS), lambda p: (p, 0, 0)),
            columns(ROWS, width),
            whole((ROWS, D)),
            whole((peers, 2 * COARSE, D)),
            whole((COARSE, D)),
        ],
        out_shape=[
            pltpu.HBM((ROWS, D), BF),
            pltpu.HBM((OWN_KEYS, D), BF),
            pltpu.HBM((OWN_KEYS, D), BF),
            pltpu.HBM((ROWS, D), F32),
            pltpu.HBM((OWN_KEYS, D), F32),
            pltpu.HBM((HEADS, ROWS, OWN_KEYS), BF),
            pltpu.HBM((ROWS, D), BF),
            pltpu.HBM((ROWS, D), BF),
            shaped((peers, 2 * COARSE, D), BF),
            shaped((COARSE, D), F32),
        ],
        scratch_shapes=[
            pltpu.VMEM((ALL_KEYS, D), BF),
            pltpu.VMEM((2 * QUERIES, ALL_KEYS), F32),
            pltpu.VMEM((QUERIES, D), F32),
        ],
        compiler_params=params(VMEM_MIB),
        cost_estimate=cost(4_500_000_000, 20_000_000, 1_600_000),
        name="fine_forward",
    )(
        place, tail, slots, in_hbm(tokens), in_hbm(cotangent), in_hbm(weights), in_hbm(fine_out)
    )


def coarse_project(gathered, coarse_in, coarse_back, groups):
    rows = gathered.shape[0] * COARSE
    return pl.pallas_call(
        coarse_project_kernel,
        out_shape=[shaped((groups, rows, 2 * PAIR), BF), shaped((rows, 2 * PAIR), F32)],
        compiler_params=params(VMEM_MIB),
        cost_estimate=cost(140_000_000, 3_000_000),
        name="coarse_project",
    )(gathered, coarse_in, coarse_back)


def coarse_attention(own_start, everyone, factor, coarse_in, coarse_back):
    rows = factor.shape[0]
    return pl.pallas_call(
        coarse_attention_kernel,
        in_specs=[SCALAR] + [IN_VMEM] * 4,
        out_shape=shaped((rows // COARSE, 2 * COARSE, D), BF),
        scratch_shapes=[pltpu.VMEM((rows, PAIR), F32)],
        compiler_params=params(VMEM_MIB),
        cost_estimate=cost(1_500_000_000, 3_000_000, 3_000_000),
        name="coarse_attention",
    )(own_start, everyone, factor, coarse_in, coarse_back)


def coarse_finish(returned, message, coarse_grad):
    return pl.pallas_call(
        coarse_finish_kernel,
        grid=(1,),
        in_specs=[whole(returned.shape), whole((1, 2 * COARSE, D)), whole((COARSE, D))],
        out_specs=[whole((COARSE, D)), whole((1, D)), whole((COARSE, D))],
        out_shape=[shaped((COARSE, D), F32), shaped((1, D), F32), shaped((COARSE, D), F32)],
        compiler_params=params(VMEM_MIB),
        cost_estimate=cost(1_000_000, 1_000_000),
        name="coarse_finish",
    )(returned, message, coarse_grad)


def fine_backward(
    cotangent, spread, after, fine_out, weights, query, key, value, q_factor, k_factor, probs,
    attended,
):
    width = BACKWARD_WIDTH
    return pl.pallas_call(
        fine_backward_kernel,
        grid=(D // width,),
        in_specs=[
            whole((ROWS, D)),
            whole((COARSE, D)),
            whole((1, D)),
            pl.BlockSpec((width, D), lambda p: (p, 0)),
            pl.BlockSpec((3, D, width), lambda p: (0, 0, p)),
            columns(ROWS, width),
            columns(OWN_KEYS, width),
            columns(OWN_KEYS, width),
            columns(ROWS, width),
            columns(OWN_KEYS, width),
            pl.BlockSpec((width // HEAD_DIM, ROWS, OWN_KEYS), lambda p: (p, 0, 0)),
            columns(ROWS, width),
        ],
        out_specs=[whole((HALO // ROWS, ROWS, D)), whole((ROWS, D)), whole((ROWS, D))],
        out_shape=[shaped((HALO // ROWS, ROWS, D), BF)] + [shaped((ROWS, D), F32)] * 2,
        scratch_shapes=[pltpu.VMEM((ROWS, D), BF), pltpu.VMEM((OWN_KEYS, D), F32)],
        compiler_params=params(VMEM_MIB),
        cost_estimate=cost(5_000_000_000, 20_000_000),
        name="fine_backward",
    )(
        in_hbm(cotangent), spread, after,
        *(in_hbm(x) for x in (fine_out, weights, query, key, value, q_factor, k_factor, probs)),
        in_hbm(attended),
    )


def halo_sum(place, got):
    return pl.pallas_call(
        halo_sum_kernel,
        in_specs=[SCALAR, IN_VMEM],
        out_shape=shaped((ROWS, D), BF),
        compiler_params=params(VMEM_MIB),
        cost_estimate=cost(1_000_000, 1_500_000),
        name="halo_sum",
    )(place, got)


def fine_finish(place, own, got, arrived, hidden_grad, tokens):
    return pl.pallas_call(
        fine_finish_kernel,
        in_specs=[SCALAR] + [IN_VMEM] * 5,
        out_shape=shaped((ROWS, D), BF),
        compiler_params=params(VMEM_MIB),
        cost_estimate=cost(1_000_000, 3_000_000),
        name="fine_finish",
    )(place, own, got, arrived, hidden_grad, tokens)


def per_device(tokens, cotangent, fine_qkv, fine_out, coarse_qkv, coarse_out):
    peers = 1
    for name in GROUP:
        peers *= lax.axis_size(name)
    groups = 1
    for name in FAR:
        groups *= lax.axis_size(name)
    core = lax.axis_index("core")
    weights = jnp.transpose(fine_qkv, (1, 0, 2))
    coarse_all = jnp.transpose(coarse_qkv, (1, 0, 2))
    picked = jnp.where(core == 0, coarse_all[:, :, :HEAD_DIM], coarse_all[:, :, HEAD_DIM:])
    blank = jnp.zeros((D, HEAD_DIM), BF)
    coarse_in = jnp.concatenate([picked[0], blank, picked[1], picked[2]], axis=1)
    picked_out = jnp.where(core == 0, coarse_out[:HEAD_DIM], coarse_out[HEAD_DIM:])
    coarse_back = jnp.pad(picked_out, ((HEAD_DIM, PAIR), (0, 0)))

    column_at = lax.axis_index("x")
    columns_along = lax.axis_size("x")
    tail = shifted_by(tokens[ROWS - EXTRA :], columns_along + 1)
    row_before = shifted_by(tokens, columns_along)
    later = (jnp.arange(columns_along) > column_at)[:, None, None]
    slots = exchanged(jnp.where(later, tokens[None], row_before[None]), "x")
    place = jnp.stack([lax.axis_index(LINE) * ROWS, column_at]).astype(jnp.int32)

    query, key, value, q_factor, k_factor, probs, attended, hidden, message, coarse_grad = (
        fine_forward(place, tail, slots, tokens, cotangent, weights, fine_out, peers)
    )
    gathered = exchanged(message, GROUP)
    coarse_send, coarse_factor = coarse_project(gathered, coarse_in, coarse_back, groups)
    group_rows = coarse_factor.shape[0]
    everyone = exchanged(coarse_send, FAR).reshape(groups * group_rows, 2 * PAIR)
    own_start = (lax.axis_index(FAR) * group_rows).astype(jnp.int32).reshape(1)
    partial = coarse_attention(own_start, everyone, coarse_factor, coarse_in, coarse_back)
    returned = exchanged(partial, GROUP)
    spread, first, state = coarse_finish(returned, message, coarse_grad)
    after = shifted_by(first, -1)
    output = (
        hidden.astype(F32) + jnp.repeat(state.astype(BF), POOL, axis=0).astype(F32)
    ).astype(BF)
    halo, own, hidden_grad = fine_backward(
        cotangent, spread, after, fine_out, weights, query, key, value, q_factor, k_factor, probs,
        attended,
    )
    got = exchanged(halo, "x")
    arrived = shifted_by(halo_sum(place, got), -columns_along)
    return (output, fine_finish(place, own, got, arrived, hidden_grad, tokens))


def solution(mesh):
    sizes = (4, 4, 2, 2, 4)
    fine_mesh = Mesh(mesh.devices.reshape(sizes), LINE)
    placed = (
        P(LINE, None),
        P(LINE, None),
        P(),
        P(),
        P(None, None, ("z_lo", "x")),
        P(("z_lo", "x"), None),
    )
    return jax.shard_map(
        per_device,
        mesh=fine_mesh,
        in_specs=placed,
        out_specs=(P(LINE, None), P(LINE, None)),
        check_vma=False,
    )
```

```python
import jax
import jax.numpy as jnp
from jax import lax
from jax.experimental import pallas as pl
from jax.experimental.pallas import tpu as pltpu
from jax.sharding import Mesh
from jax.sharding import PartitionSpec as P

D = 1024
HEADS = 16
HEAD_DIM = 64
WINDOW = 512
POOL = 16
EPS = 1e-06

LINE = ("y", "z_hi", "core", "z_lo", "x")
GROUP = ("core", "z_lo", "x")
FAR = ("y", "z_hi")

ROWS = 128
HALO = WINDOW
OWN_KEYS = HALO + ROWS
EXTRA = 16
ALL_KEYS = OWN_KEYS + EXTRA
QUERIES = EXTRA + ROWS
PAIR = 2 * HEAD_DIM
COARSE = ROWS // POOL
SCALE = HEAD_DIM ** (-0.5)
NEG = -1e30
VMEM_MIB = 32

BF = jnp.bfloat16
F32 = jnp.float32


def shifted_by(value, steps):
    count = 1
    for name in LINE:
        count *= lax.axis_size(name)
    first, last = (max(0, -steps), min(count, count - steps))
    return lax.ppermute(value, LINE, [(source, source + steps) for source in range(first, last)])


def exchanged(pieces, axes):
    return lax.all_to_all(pieces, axes, 0, 0, tiled=True)


def last_last(left, right):
    return lax.dot_general(left, right, (((1,), (1,)), ((), ())), preferred_element_type=F32)


def first_first(left, right):
    return lax.dot_general(left, right, (((0,), (0,)), ((), ())), preferred_element_type=F32)


def plain(left, right):
    return jnp.dot(left, right, preferred_element_type=F32)


def low_lanes():
    return lax.broadcasted_iota(jnp.int32, (1, PAIR), 1) < HEAD_DIM


def pair_sums(values, low):
    low_sum = jnp.sum(jnp.where(low, values, 0.0), axis=-1, keepdims=True)
    high_sum = jnp.sum(jnp.where(low, 0.0, values), axis=-1, keepdims=True)
    return jnp.where(low, low_sum, high_sum)


def pair_norm(values, low):
    factor = lax.rsqrt(pair_sums(values * values, low) * (1.0 / HEAD_DIM) + EPS)
    return values * factor, factor


def pair_norm_back(grad, unit, factor, low):
    return factor * (grad - unit * (pair_sums(unit * grad, low) * (1.0 / HEAD_DIM)))


def row_norm(rows):
    factor = lax.rsqrt(jnp.mean(rows * rows, axis=-1, keepdims=True) + EPS)
    return rows * factor, factor


def row_norm_back(grad, normed, factor):
    return factor * (grad - normed * jnp.mean(normed * grad, axis=-1, keepdims=True))


def fine_forward_kernel(
    place_ref, tail_ref, slots_ref, own_ref, cot_ref, w_ref, out_w_ref,
    q_ref, k_ref, v_ref, qf_ref, kf_ref, p_ref, att_ref, hid_ref, send_ref, cg_ref,
    normed, bias, acc,
):
    step = pl.program_id(0)
    anchor = place_ref[0]
    column_at = place_ref[1]
    low = low_lanes()
    slots = slots_ref.shape[0]
    nearest = lax.rem(column_at + (slots - 1), slots)

    @pl.when(step == 0)
    def _():
        for slot in range(slots):
            at = slot * ROWS
            normed[at : at + ROWS, :] = row_norm(slots_ref[slot].astype(F32))[0].astype(BF)
        normed[HALO:OWN_KEYS, :] = row_norm(own_ref[...].astype(F32))[0].astype(BF)
        normed[OWN_KEYS:, :] = row_norm(tail_ref[...].astype(F32))[0].astype(BF)
        row = lax.broadcasted_iota(jnp.int32, (2 * QUERIES, ALL_KEYS), 0)
        query_pos = jnp.where(row < QUERIES, row, row - QUERIES) - EXTRA
        column = lax.broadcasted_iota(jnp.int32, (2 * QUERIES, ALL_KEYS), 1)
        halo_pos = column - jnp.where(column >= column_at * ROWS, column_at * ROWS + HALO, column_at * ROWS)
        key_pos = jnp.where(
            column < HALO,
            halo_pos,
            jnp.where(column < OWN_KEYS, column - HALO, column - (OWN_KEYS + HALO + EXTRA)),
        )
        gap = query_pos - key_pos
        allowed = (gap >= 0) & (gap < WINDOW) & (anchor + key_pos >= 0)
        bias[...] = jnp.where(allowed, 0.0, NEG)
        acc[...] = jnp.zeros_like(acc)

    width = q_ref.shape[1]
    extra_at = pl.multiple_of(nearest * ROWS + (ROWS - EXTRA), EXTRA)
    query_rows = jnp.concatenate([normed[pl.ds(extra_at, EXTRA), :], normed[HALO:OWN_KEYS, :]], axis=0)
    queries = plain(query_rows, w_ref[0])
    both = plain(normed[...], jnp.concatenate([w_ref[1], w_ref[2]], axis=1))
    mixed = []
    for at in range(0, width, PAIR):
        here = slice(at, at + PAIR)
        query, q_factor = pair_norm(queries[:, here], low)
        key, k_factor = pair_norm(both[:, here], low)
        value = both[:, width + at : width + at + PAIR]
        key_b = key.astype(BF)
        q_ref[:, here] = query[EXTRA:].astype(BF)
        k_ref[:, here] = key_b[:OWN_KEYS]
        v_ref[:, here] = value[:OWN_KEYS].astype(BF)
        qf_ref[:, here] = q_factor[EXTRA:]
        kf_ref[:, here] = k_factor[:OWN_KEYS]
        scaled = query * SCALE
        stacked = jnp.concatenate([jnp.where(low, scaled, 0.0), jnp.where(low, 0.0, scaled)], axis=0)
        numer = jnp.exp(last_last(stacked.astype(BF), key_b) + bias[...])
        total = jnp.sum(numer, axis=-1, keepdims=True)
        prob = (numer * (1.0 / jnp.where(total > 0.0, total, 1.0))).astype(BF)
        p_ref[at // HEAD_DIM] = prob[EXTRA:QUERIES, :OWN_KEYS]
        p_ref[at // HEAD_DIM + 1] = prob[QUERIES + EXTRA :, :OWN_KEYS]
        twice = plain(prob, value.astype(BF))
        attended = jnp.where(low, twice[:QUERIES], twice[QUERIES:])
        attended = attended.astype(BF)
        att_ref[:, here] = attended[EXTRA:]
        mixed.append(attended)
    acc[...] += plain(jnp.concatenate(mixed, axis=1), out_w_ref[...])

    @pl.when(step == pl.num_programs(0) - 1)
    def _():
        before = slots_ref[nearest, ROWS - EXTRA :, :].astype(F32) + acc[:EXTRA, :]
        before = jnp.where(anchor > 0, before, 0.0).astype(BF)
        own = (own_ref[...].astype(F32) + acc[EXTRA:, :]).astype(BF)
        hid_ref[...] = own
        chunk = lax.broadcasted_iota(jnp.int32, (COARSE, QUERIES), 0) * POOL
        row = lax.broadcasted_iota(jnp.int32, (COARSE, QUERIES), 1)
        member = jnp.where((row > chunk) & (row <= chunk + POOL), 1.0, 0.0).astype(BF)
        pooled = plain(member, jnp.concatenate([before, own], axis=0)) * (1.0 / POOL)
        chunk = lax.broadcasted_iota(jnp.int32, (COARSE, ROWS), 0) * POOL
        row = lax.broadcasted_iota(jnp.int32, (COARSE, ROWS), 1)
        member = jnp.where((row >= chunk) & (row < chunk + POOL), 1.0, 0.0).astype(BF)
        coarse_grad = plain(member, cot_ref[...])
        cg_ref[...] = coarse_grad
        message = jnp.concatenate([pooled, coarse_grad], axis=0).astype(BF)
        for peer in range(send_ref.shape[0]):
            send_ref[peer] = message


def coarse_project_kernel(got_ref, in_w_ref, out_w_ref, send_ref, factor_ref):
    low = low_lanes()
    rows = got_ref[...].astype(F32)
    count = rows.shape[0] * COARSE
    pooled = rows[:, :COARSE, :].reshape(count, D)
    coarse_grad = rows[:, COARSE:, :].reshape(count, D)
    normed = row_norm(pooled)[0].astype(BF)
    raw = plain(normed, in_w_ref[...]) + last_last(coarse_grad.astype(BF), out_w_ref[...])
    units, factors = [], []
    for tile in (raw[:, :PAIR], raw[:, PAIR:]):
        unit, factor = pair_norm(tile, low)
        units.append(jnp.where(low, unit, tile))
        factors.append(factor)
    message = jnp.concatenate(units, axis=1).astype(BF)
    factor_ref[...] = jnp.concatenate(factors, axis=1)
    for peer in range(send_ref.shape[0]):
        send_ref[peer] = message


def coarse_attention_kernel(start_ref, got_ref, factor_ref, in_w_ref, out_w_ref, send_ref, own_grad):
    low = low_lanes()
    own_start = pl.multiple_of(start_ref[0], ROWS)
    length = got_ref.shape[0]
    block = 512
    own_left = got_ref[pl.ds(own_start, ROWS), :PAIR]
    own_right = got_ref[pl.ds(own_start, ROWS), PAIR:]
    own_grad[...] = jnp.zeros_like(own_grad)

    def masked_halves(tile):
        wide = tile.astype(F32)
        return (
            jnp.where(low, wide * SCALE, 0.0).astype(BF),
            jnp.where(low, 0.0, wide).astype(BF),
        )

    def lane_partials(values):
        total = values[:, :PAIR]
        for at in range(PAIR, values.shape[1], PAIR):
            total = total + values[:, at : at + PAIR]
        return total

    def one_block(index, carry):
        first = pl.multiple_of(index * block, block)
        query, grad = masked_halves(got_ref[pl.ds(first, block), :PAIR])
        stacked = jnp.concatenate([query, grad], axis=0)

        def scored(keys):
            both = last_last(stacked, keys)
            return jnp.exp(both[:block]), both[block:]

        def one_chunk(at, sums):
            total, product = sums
            numer, prob_grad = scored(got_ref[pl.ds(pl.multiple_of(at * block, block), block), PAIR:])
            return total + lane_partials(numer), product + lane_partials(numer * prob_grad)

        nothing = jnp.zeros((block, PAIR), F32)
        total, product = lax.fori_loop(0, index, one_chunk, (nothing, nothing))
        numer, prob_grad = scored(got_ref[pl.ds(first, block), PAIR:])
        query_at = lax.broadcasted_iota(jnp.int32, (block, 1), 0)
        numer = jnp.where(lax.broadcasted_iota(jnp.int32, (1, block), 1) <= query_at, numer, 0.0)
        total = jnp.sum(total + lane_partials(numer), axis=-1, keepdims=True)
        product = jnp.sum(product + lane_partials(numer * prob_grad), axis=-1, keepdims=True)
        inverse = 1.0 / total
        delta = product * inverse
        own_pos = own_start + lax.broadcasted_iota(jnp.int32, (1, ROWS), 1)
        numer, prob_grad = scored(own_right)
        numer = jnp.where(own_pos <= query_at + first, numer, 0.0)
        prob = numer * inverse
        score_grad = (prob * (prob_grad - delta)).astype(BF)
        own_grad[...] += first_first(
            jnp.concatenate([score_grad, prob.astype(BF)], axis=0), stacked
        )
        return carry

    lax.fori_loop(own_start // block, length // block, one_block, 0)

    query, grad = masked_halves(own_left)
    query_pos = own_start + lax.broadcasted_iota(jnp.int32, (ROWS, 1), 0)
    key_pos = lax.broadcasted_iota(jnp.int32, (1, length), 1)
    keys = got_ref[:, PAIR:]
    key_scaled, value = masked_halves(keys)
    numer = jnp.where(key_pos <= query_pos, jnp.exp(last_last(query, keys)), 0.0)
    prob_grad = last_last(grad, keys)
    inverse = 1.0 / jnp.sum(numer, axis=-1, keepdims=True)
    delta = jnp.sum(numer * prob_grad, axis=-1, keepdims=True) * inverse
    prob = numer * inverse
    score_grad = (prob * (prob_grad - delta)).astype(BF)
    mine = plain(score_grad, key_scaled) + plain(prob.astype(BF), value)

    parts = []
    for tile, unit, factor in (
        (mine, own_left, factor_ref[:, :PAIR]),
        (own_grad[...], own_right, factor_ref[:, PAIR:]),
    ):
        back = pair_norm_back(tile, unit.astype(F32), factor, low)
        parts.append(jnp.where(low, back, tile))
    parts = jnp.concatenate(parts, axis=1).astype(BF)
    peers = send_ref.shape[0]
    normed_grad = last_last(parts, in_w_ref[...]).reshape(peers, COARSE, D)
    mixed = plain(parts, out_w_ref[...]).reshape(peers, COARSE, D)
    send_ref[...] = jnp.concatenate([normed_grad, mixed], axis=1).astype(BF)


def coarse_finish_kernel(got_ref, message_ref, cg_ref, spread_ref, first_ref, state_ref):
    summed = jnp.sum(got_ref[...].astype(F32), axis=0)
    pooled = message_ref[0].astype(F32)[:COARSE]
    normed, factor = row_norm(pooled)
    pooled_grad = cg_ref[...] + row_norm_back(summed[:COARSE], normed, factor)
    spread = pooled_grad * (1.0 / POOL)
    spread_ref[...] = spread
    first_ref[...] = spread[:1]
    state_ref[...] = pooled + summed[COARSE:]


def fine_backward_kernel(
    cot_ref, spread_ref, next_ref, out_w_ref, w_ref, q_ref, k_ref, v_ref, qf_ref, kf_ref, p_ref,
    att_ref,
    halo_ref, own_ref, hg_ref, hidden_grad, acc,
):
    step = pl.program_id(0)
    low = low_lanes()

    @pl.when(step == 0)
    def _():
        block = (lax.broadcasted_iota(jnp.int32, (ROWS, 1), 0) + (POOL - 1)) // POOL
        added = jnp.zeros((ROWS, D), F32)
        for at in range(COARSE):
            added = jnp.where(block == at, spread_ref[at : at + 1, :], added)
        added = jnp.where(block == COARSE, next_ref[0:1, :], added)
        total = cot_ref[...].astype(F32) + added
        hg_ref[...] = total
        hidden_grad[...] = total.astype(BF)
        acc[...] = jnp.zeros_like(acc)

    width = q_ref.shape[1]
    att_grads = last_last(hidden_grad[...], out_w_ref[...]).astype(BF).astype(F32)
    query_grads, key_grads, value_grads = [], [], []
    for at in range(0, width, PAIR):
        here = slice(at, at + PAIR)
        att_grad = att_grads[:, here]
        delta_all = att_grad * att_ref[:, here].astype(F32)
        value = v_ref[:, here]
        key_wide = k_ref[:, here].astype(F32)
        query_wide = q_ref[:, here].astype(F32)
        grad = jnp.concatenate(
            [jnp.where(low, att_grad, 0.0), jnp.where(low, 0.0, att_grad)], axis=0
        ).astype(BF)
        delta = jnp.sum(
            jnp.concatenate([jnp.where(low, delta_all, 0.0), jnp.where(low, 0.0, delta_all)], axis=0),
            axis=-1,
            keepdims=True,
        )
        scaled = query_wide * SCALE
        query = jnp.concatenate(
            [jnp.where(low, scaled, 0.0), jnp.where(low, 0.0, scaled)], axis=0
        ).astype(BF)
        first = at // HEAD_DIM
        prob = p_ref[first : first + 2].reshape(2 * ROWS, OWN_KEYS)
        score_grad = (prob.astype(F32) * (last_last(grad, value) - delta)).astype(BF)
        twice = plain(score_grad, (key_wide * SCALE).astype(BF))
        query_grad = jnp.where(low, twice[:ROWS], twice[ROWS:])
        key_grad = first_first(score_grad, query)
        value_grad = first_first(prob, grad)
        query_grads.append(pair_norm_back(query_grad, query_wide, qf_ref[:, here], low).astype(BF))
        key_grads.append(pair_norm_back(key_grad, key_wide, kf_ref[:, here], low).astype(BF))
        value_grads.append(value_grad.astype(BF))
    both = jnp.concatenate(key_grads + value_grads, axis=1)
    acc[...] += last_last(both, jnp.concatenate([w_ref[1], w_ref[2]], axis=1))
    acc[HALO:, :] += last_last(jnp.concatenate(query_grads, axis=1), w_ref[0])

    @pl.when(step == pl.num_programs(0) - 1)
    def _():
        for slot in range(halo_ref.shape[0]):
            halo_ref[slot] = acc[slot * ROWS : (slot + 1) * ROWS, :].astype(BF)
        own_ref[...] = acc[HALO:, :]


def halo_send_kernel(place_ref, own_ref, before_ref, send_ref):
    column_at = place_ref[1]
    for slot in range(send_ref.shape[0]):
        send_ref[slot] = jnp.where(column_at < slot, own_ref[...], before_ref[...])


def repeated_kernel(block_ref, send_ref):
    for peer in range(send_ref.shape[0]):
        send_ref[peer] = block_ref[...]


def halo_sum_kernel(place_ref, got_ref, back_ref):
    column_at = place_ref[1]
    total = got_ref[0].astype(F32)
    for slot in range(1, got_ref.shape[0]):
        total = total + jnp.where(column_at >= slot, got_ref[slot].astype(F32), 0.0)
    back_ref[...] = total.astype(BF)


def fine_finish_kernel(place_ref, own_ref, got_ref, arrived_ref, hg_ref, tokens_ref, out_ref):
    column_at = place_ref[1]
    total = own_ref[...] + arrived_ref[...].astype(F32)
    for slot in range(1, got_ref.shape[0]):
        total = total + jnp.where(column_at < slot, got_ref[slot].astype(F32), 0.0)
    normed, factor = row_norm(tokens_ref[...].astype(F32))
    out_ref[...] = (hg_ref[...] + row_norm_back(total, normed, factor)).astype(BF)


def whole(shape):
    return pl.BlockSpec(shape, lambda *_: (0,) * len(shape))


def columns(rows, width):
    return pl.BlockSpec((rows, width), lambda p: (0, p))


def shaped(shape, kind):
    return jax.ShapeDtypeStruct(shape, kind)


def params(mib):
    return pltpu.CompilerParams(vmem_limit_bytes=mib << 20)


def cost(flops, moved, exps=0):
    return pl.CostEstimate(flops=flops, bytes_accessed=moved, transcendentals=exps)


SCALAR = pl.BlockSpec(memory_space=pltpu.SMEM)
IN_VMEM = pl.BlockSpec(memory_space=pltpu.VMEM)
FORWARD_WIDTH = 2 * PAIR
BACKWARD_WIDTH = 2 * PAIR


def in_hbm(x):
    return pltpu.with_memory_space_constraint(x, pltpu.HBM)


def fine_forward(place, tail, slots, tokens, cotangent, weights, fine_out, peers):
    width = FORWARD_WIDTH
    return pl.pallas_call(
        fine_forward_kernel,
        grid=(D // width,),
        in_specs=[SCALAR, whole((EXTRA, D)), whole(slots.shape)]
        + [whole((ROWS, D))] * 2
        + [
            pl.BlockSpec((3, D, width), lambda p: (0, 0, p)),
            pl.BlockSpec((width, D), lambda p: (p, 0)),
        ],
        out_specs=[
            columns(ROWS, width),
            columns(OWN_KEYS, width),
            columns(OWN_KEYS, width),
            columns(ROWS, width),
            columns(OWN_KEYS, width),
            pl.BlockSpec((width // HEAD_DIM, ROWS, OWN_KEYS), lambda p: (p, 0, 0)),
            columns(ROWS, width),
            whole((ROWS, D)),
            whole((peers, 2 * COARSE, D)),
            whole((COARSE, D)),
        ],
        out_shape=[
            pltpu.HBM((ROWS, D), BF),
            pltpu.HBM((OWN_KEYS, D), BF),
            pltpu.HBM((OWN_KEYS, D), BF),
            pltpu.HBM((ROWS, D), F32),
            pltpu.HBM((OWN_KEYS, D), F32),
            pltpu.HBM((HEADS, ROWS, OWN_KEYS), BF),
            pltpu.HBM((ROWS, D), BF),
            pltpu.HBM((ROWS, D), BF),
            shaped((peers, 2 * COARSE, D), BF),
            shaped((COARSE, D), F32),
        ],
        scratch_shapes=[
            pltpu.VMEM((ALL_KEYS, D), BF),
            pltpu.VMEM((2 * QUERIES, ALL_KEYS), F32),
            pltpu.VMEM((QUERIES, D), F32),
        ],
        compiler_params=params(VMEM_MIB),
        cost_estimate=cost(4_500_000_000, 20_000_000, 1_600_000),
        name="fine_forward",
    )(
        place, tail, slots, in_hbm(tokens), in_hbm(cotangent), in_hbm(weights), in_hbm(fine_out)
    )


def coarse_project(gathered, coarse_in, coarse_back, groups):
    rows = gathered.shape[0] * COARSE
    return pl.pallas_call(
        coarse_project_kernel,
        out_shape=[shaped((groups, rows, 2 * PAIR), BF), shaped((rows, 2 * PAIR), F32)],
        compiler_params=params(VMEM_MIB),
        cost_estimate=cost(140_000_000, 3_000_000),
        name="coarse_project",
    )(gathered, coarse_in, coarse_back)


def coarse_attention(own_start, everyone, factor, coarse_in, coarse_back):
    rows = factor.shape[0]
    return pl.pallas_call(
        coarse_attention_kernel,
        in_specs=[SCALAR] + [IN_VMEM] * 4,
        out_shape=shaped((rows // COARSE, 2 * COARSE, D), BF),
        scratch_shapes=[pltpu.VMEM((rows, PAIR), F32)],
        compiler_params=params(VMEM_MIB),
        cost_estimate=cost(1_500_000_000, 3_000_000, 3_000_000),
        name="coarse_attention",
    )(own_start, everyone, factor, coarse_in, coarse_back)


def coarse_finish(returned, message, coarse_grad):
    return pl.pallas_call(
        coarse_finish_kernel,
        grid=(1,),
        in_specs=[whole(returned.shape), whole((1, 2 * COARSE, D)), whole((COARSE, D))],
        out_specs=[whole((COARSE, D)), whole((1, D)), whole((COARSE, D))],
        out_shape=[shaped((COARSE, D), F32), shaped((1, D), F32), shaped((COARSE, D), F32)],
        compiler_params=params(VMEM_MIB),
        cost_estimate=cost(1_000_000, 1_000_000),
        name="coarse_finish",
    )(returned, message, coarse_grad)


def fine_backward(
    cotangent, spread, after, fine_out, weights, query, key, value, q_factor, k_factor, probs,
    attended,
):
    width = BACKWARD_WIDTH
    return pl.pallas_call(
        fine_backward_kernel,
        grid=(D // width,),
        in_specs=[
            whole((ROWS, D)),
            whole((COARSE, D)),
            whole((1, D)),
            pl.BlockSpec((width, D), lambda p: (p, 0)),
            pl.BlockSpec((3, D, width), lambda p: (0, 0, p)),
            columns(ROWS, width),
            columns(OWN_KEYS, width),
            columns(OWN_KEYS, width),
            columns(ROWS, width),
            columns(OWN_KEYS, width),
            pl.BlockSpec((width // HEAD_DIM, ROWS, OWN_KEYS), lambda p: (p, 0, 0)),
            columns(ROWS, width),
        ],
        out_specs=[whole((HALO // ROWS, ROWS, D)), whole((ROWS, D)), whole((ROWS, D))],
        out_shape=[shaped((HALO // ROWS, ROWS, D), BF)] + [shaped((ROWS, D), F32)] * 2,
        scratch_shapes=[pltpu.VMEM((ROWS, D), BF), pltpu.VMEM((OWN_KEYS, D), F32)],
        compiler_params=params(VMEM_MIB),
        cost_estimate=cost(5_000_000_000, 20_000_000),
        name="fine_backward",
    )(
        in_hbm(cotangent), spread, after,
        *(in_hbm(x) for x in (fine_out, weights, query, key, value, q_factor, k_factor, probs)),
        in_hbm(attended),
    )


def halo_send(place, own, before, count):
    return pl.pallas_call(
        halo_send_kernel,
        in_specs=[SCALAR] + [IN_VMEM] * 2,
        out_shape=shaped((count, ROWS, D), BF),
        compiler_params=params(VMEM_MIB),
        cost_estimate=cost(1_000_000, 1_500_000),
        name="halo_send",
    )(place, own, before)


def repeated(block, count):
    return pl.pallas_call(
        repeated_kernel,
        out_shape=shaped((count, *block.shape), BF),
        compiler_params=params(VMEM_MIB),
        cost_estimate=cost(1_000_000, 1_300_000),
        name="repeated",
    )(block)


def halo_sum(place, got):
    return pl.pallas_call(
        halo_sum_kernel,
        in_specs=[SCALAR, IN_VMEM],
        out_shape=shaped((ROWS, D), BF),
        compiler_params=params(VMEM_MIB),
        cost_estimate=cost(1_000_000, 1_500_000),
        name="halo_sum",
    )(place, got)


def fine_finish(place, own, got, arrived, hidden_grad, tokens):
    return pl.pallas_call(
        fine_finish_kernel,
        in_specs=[SCALAR] + [IN_VMEM] * 5,
        out_shape=shaped((ROWS, D), BF),
        compiler_params=params(VMEM_MIB),
        cost_estimate=cost(1_000_000, 3_000_000),
        name="fine_finish",
    )(place, own, got, arrived, hidden_grad, tokens)


def per_device(tokens, cotangent, fine_qkv, fine_out, coarse_qkv, coarse_out):
    peers = 1
    for name in GROUP:
        peers *= lax.axis_size(name)
    groups = 1
    for name in FAR:
        groups *= lax.axis_size(name)
    core = lax.axis_index("core")
    weights = jnp.transpose(fine_qkv, (1, 0, 2))
    coarse_all = jnp.transpose(coarse_qkv, (1, 0, 2))
    picked = jnp.where(core == 0, coarse_all[:, :, :HEAD_DIM], coarse_all[:, :, HEAD_DIM:])
    blank = jnp.zeros((D, HEAD_DIM), BF)
    coarse_in = jnp.concatenate([picked[0], blank, picked[1], picked[2]], axis=1)
    picked_out = jnp.where(core == 0, coarse_out[:HEAD_DIM], coarse_out[HEAD_DIM:])
    coarse_back = jnp.pad(picked_out, ((HEAD_DIM, PAIR), (0, 0)))

    column_at = lax.axis_index("x")
    columns_along = lax.axis_size("x")
    tail = shifted_by(tokens[ROWS - EXTRA :], columns_along + 1)
    row_before = shifted_by(tokens, columns_along)
    tail, row_before = lax.optimization_barrier((tail, row_before))
    place = jnp.stack([lax.axis_index(LINE) * ROWS, column_at]).astype(jnp.int32)
    slots = exchanged(halo_send(place, tokens, row_before, columns_along), "x")

    query, key, value, q_factor, k_factor, probs, attended, hidden, message, coarse_grad = (
        fine_forward(place, tail, slots, tokens, cotangent, weights, fine_out, peers)
    )
    gathered = exchanged(message, GROUP)
    near, further = lax.axis_size("z_hi"), lax.axis_size("y")
    coarse_send, coarse_factor = coarse_project(gathered, coarse_in, coarse_back, near)
    group_rows = coarse_factor.shape[0]
    nearby = exchanged(coarse_send, "z_hi").reshape(near * group_rows, 2 * PAIR)
    everyone = exchanged(repeated(nearby, further), "y").reshape(groups * group_rows, 2 * PAIR)
    own_start = (lax.axis_index(FAR) * group_rows).astype(jnp.int32).reshape(1)
    partial = coarse_attention(own_start, everyone, coarse_factor, coarse_in, coarse_back)
    returned = exchanged(partial, GROUP)
    spread, first, state = coarse_finish(returned, message, coarse_grad)
    after = shifted_by(first, -1)
    output = (
        hidden.astype(F32) + jnp.repeat(state.astype(BF), POOL, axis=0).astype(F32)
    ).astype(BF)
    halo, own, hidden_grad = fine_backward(
        cotangent, spread, after, fine_out, weights, query, key, value, q_factor, k_factor, probs,
        attended,
    )
    got = exchanged(halo, "x")
    arrived = shifted_by(halo_sum(place, got), -columns_along)
    return (output, fine_finish(place, own, got, arrived, hidden_grad, tokens))


def solution(mesh):
    sizes = (4, 4, 2, 2, 4)
    fine_mesh = Mesh(mesh.devices.reshape(sizes), LINE)
    placed = (
        P(LINE, None),
        P(LINE, None),
        P(),
        P(),
        P(None, None, ("z_lo", "x")),
        P(("z_lo", "x"), None),
    )
    return jax.shard_map(
        per_device,
        mesh=fine_mesh,
        in_specs=placed,
        out_specs=(P(LINE, None), P(LINE, None)),
        check_vma=False,
    )
```

```python
import jax
import jax.numpy as jnp
from jax import lax
from jax.experimental import pallas as pl
from jax.experimental.pallas import tpu as pltpu
from jax.sharding import Mesh
from jax.sharding import PartitionSpec as P

D = 1024
HEADS = 16
HEAD_DIM = 64
WINDOW = 512
POOL = 16
EPS = 1e-06

LINE = ("y", "z_hi", "core", "z_lo", "x")
GROUP = ("core", "z_lo", "x")
FAR = ("y", "z_hi")

ROWS = 128
HALO = WINDOW
OWN_KEYS = HALO + ROWS
EXTRA = 16
ALL_KEYS = OWN_KEYS + EXTRA
QUERIES = EXTRA + ROWS
PAIR = 2 * HEAD_DIM
COARSE = ROWS // POOL
SCALE = HEAD_DIM ** (-0.5)
NEG = -1e30
VMEM_MIB = 16

BF = jnp.bfloat16
F32 = jnp.float32


def shifted_by(value, steps):
    count = 1
    for name in LINE:
        count *= lax.axis_size(name)
    first, last = (max(0, -steps), min(count, count - steps))
    return lax.ppermute(value, LINE, [(source, source + steps) for source in range(first, last)])


def exchanged(pieces, axes):
    return lax.all_to_all(pieces, axes, 0, 0, tiled=True)


def last_last(left, right):
    return lax.dot_general(left, right, (((1,), (1,)), ((), ())), preferred_element_type=F32)


def first_first(left, right):
    return lax.dot_general(left, right, (((0,), (0,)), ((), ())), preferred_element_type=F32)


def plain(left, right):
    return jnp.dot(left, right, preferred_element_type=F32)


def low_lanes():
    return lax.broadcasted_iota(jnp.int32, (1, PAIR), 1) < HEAD_DIM


def pair_sums(values, low):
    low_sum = jnp.sum(jnp.where(low, values, 0.0), axis=-1, keepdims=True)
    high_sum = jnp.sum(jnp.where(low, 0.0, values), axis=-1, keepdims=True)
    return jnp.where(low, low_sum, high_sum)


def pair_norm(values, low):
    factor = lax.rsqrt(pair_sums(values * values, low) * (1.0 / HEAD_DIM) + EPS)
    return values * factor, factor


def pair_norm_back(grad, unit, factor, low):
    return factor * (grad - unit * (pair_sums(unit * grad, low) * (1.0 / HEAD_DIM)))


def row_norm(rows):
    factor = lax.rsqrt(jnp.mean(rows * rows, axis=-1, keepdims=True) + EPS)
    return rows * factor, factor


def row_norm_back(grad, normed, factor):
    return factor * (grad - normed * jnp.mean(normed * grad, axis=-1, keepdims=True))


def fine_prepare_kernel(
    place_ref, own_hbm, cot_hbm, w_hbm, out_w_hbm,
    own_ref, w_ref, out_w_ref, q_ref, k_ref, v_ref, qf_ref, kf_ref, bias_ref, cg_ref,
    cot, copied,
):
    anchor = place_ref[0]
    column_at = place_ref[1]
    low = low_lanes()
    copies = [
        pltpu.make_async_copy(source, target, copied.at[at])
        for at, (source, target) in enumerate(
            ((own_hbm, own_ref), (cot_hbm, cot), (w_hbm, w_ref), (out_w_hbm, out_w_ref))
        )
    ]
    for copy in copies:
        copy.start()

    row = lax.broadcasted_iota(jnp.int32, (2 * QUERIES, ALL_KEYS), 0)
    query_pos = jnp.where(row < QUERIES, row, row - QUERIES) - EXTRA
    column = lax.broadcasted_iota(jnp.int32, (2 * QUERIES, ALL_KEYS), 1)
    turned = column_at * ROWS
    halo_pos = column - jnp.where(column >= turned, turned + HALO, turned)
    key_pos = jnp.where(
        column < HALO,
        halo_pos,
        jnp.where(column < OWN_KEYS, column - HALO, column - (OWN_KEYS + HALO + EXTRA)),
    )
    gap = query_pos - key_pos
    allowed = (gap >= 0) & (gap < WINDOW) & (anchor + key_pos >= 0)
    bias_ref[...] = jnp.where(allowed, 0.0, NEG)

    copies[0].wait()
    normed = row_norm(own_ref[...].astype(F32))[0].astype(BF)
    copies[1].wait()
    chunk = lax.broadcasted_iota(jnp.int32, (COARSE, ROWS), 0) * POOL
    row = lax.broadcasted_iota(jnp.int32, (COARSE, ROWS), 1)
    member = jnp.where((row >= chunk) & (row < chunk + POOL), 1.0, 0.0).astype(BF)
    cg_ref[...] = plain(member, cot[...])
    copies[2].wait()
    for at in range(0, D, WIDTH):
        here = slice(at, at + WIDTH)
        queries = plain(normed, w_ref[0, :, here])
        keys = plain(normed, w_ref[1, :, here])
        v_ref[:, here] = plain(normed, w_ref[2, :, here]).astype(BF)
        for part in range(0, WIDTH, PAIR):
            inner = slice(part, part + PAIR)
            outer = slice(at + part, at + part + PAIR)
            query, q_factor = pair_norm(queries[:, inner], low)
            key, k_factor = pair_norm(keys[:, inner], low)
            q_ref[:, outer] = query.astype(BF)
            k_ref[:, outer] = key.astype(BF)
            qf_ref[:, outer] = q_factor
            kf_ref[:, outer] = k_factor
    copies[3].wait()


def fine_forward_kernel(
    place_ref, tail_ref, slots_ref, own_ref, w_ref, out_w_ref, own_q_ref, own_k_ref, own_v_ref,
    own_kf_ref, bias, cg_ref,
    k_ref, v_ref, kf_ref, p_ref, att_ref, hid_ref, send_ref,
    normed, acc,
):
    anchor = place_ref[0]
    column_at = place_ref[1]
    low = low_lanes()
    slots = slots_ref.shape[0]
    nearest = lax.rem(column_at + (slots - 1), slots)
    for slot in range(slots):
        at = slot * ROWS
        normed[at : at + ROWS, :] = row_norm(slots_ref[slot].astype(F32))[0].astype(BF)
    normed[HALO:, :] = row_norm(tail_ref[...].astype(F32))[0].astype(BF)
    acc[...] = jnp.zeros_like(acc)
    extra_at = pl.multiple_of(nearest * ROWS + (ROWS - EXTRA), EXTRA)

    def one_step(step, carry):
        first = pl.multiple_of(step * WIDTH, WIDTH)
        here = pl.ds(first, WIDTH)
        extra = plain(normed[pl.ds(extra_at, EXTRA), :], w_ref[0, :, here])
        both = plain(
            normed[...], jnp.concatenate([w_ref[1, :, here], w_ref[2, :, here]], axis=1)
        )
        own_q, own_k, own_v = own_q_ref[:, here], own_k_ref[:, here], own_v_ref[:, here]
        own_kf = own_kf_ref[:, here]
        mixed = []
        for part in range(0, WIDTH, PAIR):
            inner = slice(part, part + PAIR)
            outer = pl.ds(pl.multiple_of(first + part, PAIR), PAIR)
            key, k_factor = pair_norm(both[:, inner], low)
            key = key.astype(BF)
            value = both[:, WIDTH + part : WIDTH + part + PAIR].astype(BF)
            k_ref[:HALO, outer] = key[:HALO]
            k_ref[HALO:, outer] = own_k[:, inner]
            v_ref[:HALO, outer] = value[:HALO]
            v_ref[HALO:, outer] = own_v[:, inner]
            kf_ref[:HALO, outer] = k_factor[:HALO]
            kf_ref[HALO:, outer] = own_kf[:, inner]
            key = jnp.concatenate([key[:HALO], own_k[:, inner], key[HALO:]], axis=0)
            value = jnp.concatenate([value[:HALO], own_v[:, inner], value[HALO:]], axis=0)
            before = pair_norm(extra[:, inner], low)[0].astype(BF).astype(F32)
            scaled = jnp.concatenate([before, own_q[:, inner].astype(F32)], axis=0) * SCALE
            stacked = jnp.concatenate(
                [jnp.where(low, scaled, 0.0), jnp.where(low, 0.0, scaled)], axis=0
            )
            numer = jnp.exp(last_last(stacked.astype(BF), key) + bias[...])
            total = jnp.sum(numer, axis=-1, keepdims=True)
            prob = (numer * (1.0 / jnp.where(total > 0.0, total, 1.0))).astype(BF)
            head = (first + part) // HEAD_DIM
            p_ref[head] = prob[EXTRA:QUERIES, :OWN_KEYS]
            p_ref[head + 1] = prob[QUERIES + EXTRA :, :OWN_KEYS]
            twice = plain(prob, value)
            attended = jnp.where(low, twice[:QUERIES], twice[QUERIES:]).astype(BF)
            att_ref[:, outer] = attended[EXTRA:]
            mixed.append(attended)
        acc[...] += plain(jnp.concatenate(mixed, axis=1), out_w_ref[here, :])
        return carry

    lax.fori_loop(0, D // WIDTH, one_step, 0)
    before = slots_ref[nearest, ROWS - EXTRA :, :].astype(F32) + acc[:EXTRA, :]
    before = jnp.where(anchor > 0, before, 0.0).astype(BF)
    own = (own_ref[...].astype(F32) + acc[EXTRA:, :]).astype(BF)
    hid_ref[...] = own
    chunk = lax.broadcasted_iota(jnp.int32, (COARSE, QUERIES), 0) * POOL
    row = lax.broadcasted_iota(jnp.int32, (COARSE, QUERIES), 1)
    member = jnp.where((row > chunk) & (row <= chunk + POOL), 1.0, 0.0).astype(BF)
    pooled = plain(member, jnp.concatenate([before, own], axis=0)) * (1.0 / POOL)
    message = jnp.concatenate([pooled, cg_ref[...]], axis=0).astype(BF)
    for peer in range(send_ref.shape[0]):
        send_ref[peer] = message


def coarse_prepare_kernel(core_ref, w_ref, back_ref, in_ref, out_ref):
    low = low_lanes()
    second = core_ref[0] > 0
    parts = [w_ref[at].astype(F32) for at in range(3)]
    turned = [pltpu.roll(part, HEAD_DIM, 1) for part in parts]
    query = jnp.where(second, turned[0], parts[0])
    key = jnp.where(second, turned[1], parts[1])
    value = jnp.where(second, parts[2], turned[2])
    in_ref[:, :PAIR] = jnp.where(low, query, 0.0).astype(BF)
    in_ref[:, PAIR:] = jnp.where(low, key, value).astype(BF)
    out_ref[...] = jnp.zeros_like(out_ref)
    out_ref[HEAD_DIM:PAIR, :] = jnp.where(second, back_ref[HEAD_DIM:, :], back_ref[:HEAD_DIM, :])


def coarse_project_kernel(got_ref, in_w_ref, out_w_ref, send_ref, factor_ref):
    low = low_lanes()
    rows = got_ref[...].astype(F32)
    count = rows.shape[0] * COARSE
    pooled = rows[:, :COARSE, :].reshape(count, D)
    coarse_grad = rows[:, COARSE:, :].reshape(count, D)
    normed = row_norm(pooled)[0].astype(BF)
    raw = plain(normed, in_w_ref[...]) + last_last(coarse_grad.astype(BF), out_w_ref[...])
    units, factors = [], []
    for tile in (raw[:, :PAIR], raw[:, PAIR:]):
        unit, factor = pair_norm(tile, low)
        units.append(jnp.where(low, unit, tile))
        factors.append(factor)
    message = jnp.concatenate(units, axis=1).astype(BF)
    factor_ref[...] = jnp.concatenate(factors, axis=1)
    for peer in range(send_ref.shape[0]):
        send_ref[peer] = message


def coarse_attention_kernel(place_ref, got_ref, factor_ref, in_w_ref, out_w_ref, send_ref, own_grad):
    low = low_lanes()
    own_start = pl.multiple_of(place_ref[2], ROWS)
    length = got_ref.shape[0]
    block = 512
    own_left = got_ref[pl.ds(own_start, ROWS), :PAIR]
    own_right = got_ref[pl.ds(own_start, ROWS), PAIR:]
    own_grad[...] = jnp.zeros_like(own_grad)

    def masked_halves(tile):
        wide = tile.astype(F32)
        return (
            jnp.where(low, wide * SCALE, 0.0).astype(BF),
            jnp.where(low, 0.0, wide).astype(BF),
        )

    def lane_partials(values):
        total = values[:, :PAIR]
        for at in range(PAIR, values.shape[1], PAIR):
            total = total + values[:, at : at + PAIR]
        return total

    def one_block(index, carry):
        first = pl.multiple_of(index * block, block)
        query, grad = masked_halves(got_ref[pl.ds(first, block), :PAIR])
        stacked = jnp.concatenate([query, grad], axis=0)

        def scored(keys):
            both = last_last(stacked, keys)
            return jnp.exp(both[:block]), both[block:]

        def one_chunk(at, sums):
            total, product = sums
            numer, prob_grad = scored(got_ref[pl.ds(pl.multiple_of(at * block, block), block), PAIR:])
            return total + lane_partials(numer), product + lane_partials(numer * prob_grad)

        nothing = jnp.zeros((block, PAIR), F32)
        total, product = lax.fori_loop(0, index, one_chunk, (nothing, nothing))
        numer, prob_grad = scored(got_ref[pl.ds(first, block), PAIR:])
        query_at = lax.broadcasted_iota(jnp.int32, (block, 1), 0)
        numer = jnp.where(lax.broadcasted_iota(jnp.int32, (1, block), 1) <= query_at, numer, 0.0)
        total = jnp.sum(total + lane_partials(numer), axis=-1, keepdims=True)
        product = jnp.sum(product + lane_partials(numer * prob_grad), axis=-1, keepdims=True)
        inverse = 1.0 / total
        delta = product * inverse
        own_pos = own_start + lax.broadcasted_iota(jnp.int32, (1, ROWS), 1)
        numer, prob_grad = scored(own_right)
        numer = jnp.where(own_pos <= query_at + first, numer, 0.0)
        prob = numer * inverse
        score_grad = (prob * (prob_grad - delta)).astype(BF)
        own_grad[...] += first_first(
            jnp.concatenate([score_grad, prob.astype(BF)], axis=0), stacked
        )
        return carry

    lax.fori_loop(own_start // block, length // block, one_block, 0)

    query, grad = masked_halves(own_left)
    query_pos = own_start + lax.broadcasted_iota(jnp.int32, (ROWS, 1), 0)
    key_pos = lax.broadcasted_iota(jnp.int32, (1, length), 1)
    keys = got_ref[:, PAIR:]
    key_scaled, value = masked_halves(keys)
    numer = jnp.where(key_pos <= query_pos, jnp.exp(last_last(query, keys)), 0.0)
    prob_grad = last_last(grad, keys)
    inverse = 1.0 / jnp.sum(numer, axis=-1, keepdims=True)
    delta = jnp.sum(numer * prob_grad, axis=-1, keepdims=True) * inverse
    prob = numer * inverse
    score_grad = (prob * (prob_grad - delta)).astype(BF)
    mine = plain(score_grad, key_scaled) + plain(prob.astype(BF), value)

    parts = []
    for tile, unit, factor in (
        (mine, own_left, factor_ref[:, :PAIR]),
        (own_grad[...], own_right, factor_ref[:, PAIR:]),
    ):
        back = pair_norm_back(tile, unit.astype(F32), factor, low)
        parts.append(jnp.where(low, back, tile))
    parts = jnp.concatenate(parts, axis=1).astype(BF)
    peers = send_ref.shape[0]
    normed_grad = last_last(parts, in_w_ref[...]).reshape(peers, COARSE, D)
    mixed = plain(parts, out_w_ref[...]).reshape(peers, COARSE, D)
    send_ref[...] = jnp.concatenate([normed_grad, mixed], axis=1).astype(BF)


def coarse_finish_kernel(got_ref, message_ref, cg_ref, spread_ref, first_ref, state_ref):
    summed = jnp.sum(got_ref[...].astype(F32), axis=0)
    pooled = message_ref[0].astype(F32)[:COARSE]
    normed, factor = row_norm(pooled)
    pooled_grad = cg_ref[...] + row_norm_back(summed[:COARSE], normed, factor)
    spread = pooled_grad * (1.0 / POOL)
    spread_ref[...] = spread
    first_ref[...] = spread[:1]
    state_ref[...] = pooled + summed[COARSE:]


def fine_backward_kernel(
    cot_ref, spread_ref, next_ref, out_w_ref, w_ref, q_ref, k_ref, v_ref, qf_ref, kf_ref, p_ref,
    att_ref,
    halo_ref, own_ref, hg_ref, hidden_grad, acc,
):
    low = low_lanes()
    block = (lax.broadcasted_iota(jnp.int32, (ROWS, 1), 0) + (POOL - 1)) // POOL
    added = jnp.zeros((ROWS, D), F32)
    for at in range(COARSE):
        added = jnp.where(block == at, spread_ref[at : at + 1, :], added)
    added = jnp.where(block == COARSE, next_ref[0:1, :], added)
    total = cot_ref[...].astype(F32) + added
    hg_ref[...] = total
    hidden_grad[...] = total.astype(BF)
    acc[...] = jnp.zeros_like(acc)

    def one_step(step, carry):
        first = pl.multiple_of(step * WIDTH, WIDTH)
        here = pl.ds(first, WIDTH)
        att_grads = last_last(hidden_grad[...], out_w_ref[here, :]).astype(BF).astype(F32)
        query_grads, key_grads, value_grads = [], [], []
        for part in range(0, WIDTH, PAIR):
            outer = pl.ds(pl.multiple_of(first + part, PAIR), PAIR)
            att_grad = att_grads[:, part : part + PAIR]
            delta_all = att_grad * att_ref[:, outer].astype(F32)
            value = v_ref[:, outer]
            key_wide = k_ref[:, outer].astype(F32)
            query_wide = q_ref[:, outer].astype(F32)
            grad = jnp.concatenate(
                [jnp.where(low, att_grad, 0.0), jnp.where(low, 0.0, att_grad)], axis=0
            ).astype(BF)
            delta = jnp.sum(
                jnp.concatenate(
                    [jnp.where(low, delta_all, 0.0), jnp.where(low, 0.0, delta_all)], axis=0
                ),
                axis=-1,
                keepdims=True,
            )
            scaled = query_wide * SCALE
            query = jnp.concatenate(
                [jnp.where(low, scaled, 0.0), jnp.where(low, 0.0, scaled)], axis=0
            ).astype(BF)
            head = (first + part) // HEAD_DIM
            prob = p_ref[pl.ds(head, 2)].reshape(2 * ROWS, OWN_KEYS)
            score_grad = (prob.astype(F32) * (last_last(grad, value) - delta)).astype(BF)
            twice = plain(score_grad, (key_wide * SCALE).astype(BF))
            query_grad = jnp.where(low, twice[:ROWS], twice[ROWS:])
            key_grad = first_first(score_grad, query)
            value_grad = first_first(prob, grad)
            query_grads.append(pair_norm_back(query_grad, query_wide, qf_ref[:, outer], low).astype(BF))
            key_grads.append(pair_norm_back(key_grad, key_wide, kf_ref[:, outer], low).astype(BF))
            value_grads.append(value_grad.astype(BF))
        both = jnp.concatenate(key_grads + value_grads, axis=1)
        acc[...] += last_last(
            both, jnp.concatenate([w_ref[1, :, here], w_ref[2, :, here]], axis=1)
        )
        acc[HALO:, :] += last_last(jnp.concatenate(query_grads, axis=1), w_ref[0, :, here])
        return carry

    lax.fori_loop(0, D // WIDTH, one_step, 0)
    for slot in range(halo_ref.shape[0]):
        halo_ref[slot] = acc[slot * ROWS : (slot + 1) * ROWS, :].astype(BF)
    own_ref[...] = acc[HALO:, :]


def halo_send_kernel(place_ref, own_ref, before_ref, send_ref):
    send_ref[0] = jnp.where(place_ref[1] < pl.program_id(0), own_ref[...], before_ref[...])


def repeated_kernel(block_ref, send_ref):
    for peer in range(send_ref.shape[0]):
        send_ref[peer] = block_ref[...]


def halo_sum_kernel(place_ref, got_ref, back_ref):
    column_at = place_ref[1]
    total = got_ref[0].astype(F32)
    for slot in range(1, got_ref.shape[0]):
        total = total + jnp.where(column_at >= slot, got_ref[slot].astype(F32), 0.0)
    back_ref[...] = total.astype(BF)


def fine_finish_kernel(place_ref, own_ref, got_ref, arrived_ref, hg_ref, tokens_ref, out_ref):
    column_at = place_ref[1]
    total = own_ref[...] + arrived_ref[...].astype(F32)
    for slot in range(1, got_ref.shape[0]):
        total = total + jnp.where(column_at < slot, got_ref[slot].astype(F32), 0.0)
    normed, factor = row_norm(tokens_ref[...].astype(F32))
    out_ref[...] = (hg_ref[...] + row_norm_back(total, normed, factor)).astype(BF)


def whole(shape):
    return pl.BlockSpec(shape, lambda *_: (0,) * len(shape))


def columns(rows, width):
    return pl.BlockSpec((rows, width), lambda p: (0, p))


def shaped(shape, kind):
    return jax.ShapeDtypeStruct(shape, kind)


def params(mib):
    return pltpu.CompilerParams(vmem_limit_bytes=mib << 20)


def cost(flops, moved, exps=0):
    return pl.CostEstimate(flops=flops, bytes_accessed=moved, transcendentals=exps)


SCALAR = pl.BlockSpec(memory_space=pltpu.SMEM)
IN_VMEM = pl.BlockSpec(memory_space=pltpu.VMEM)
WIDTH = 2 * PAIR


def in_hbm(x):
    return pltpu.with_memory_space_constraint(x, pltpu.HBM)


def fine_prepare(place, tokens, cotangent, weights, fine_out):
    anywhere = pl.BlockSpec(memory_space=pltpu.HBM)
    return pl.pallas_call(
        fine_prepare_kernel,
        in_specs=[SCALAR] + [anywhere] * 4,
        out_specs=[IN_VMEM] * 10,
        out_shape=[
            pltpu.VMEM((ROWS, D), BF),
            pltpu.VMEM((3, D, D), BF),
            pltpu.VMEM((D, D), BF),
            pltpu.VMEM((ROWS, D), BF),
            pltpu.VMEM((ROWS, D), BF),
            pltpu.VMEM((ROWS, D), BF),
            pltpu.VMEM((ROWS, D), F32),
            pltpu.VMEM((ROWS, D), F32),
            pltpu.VMEM((2 * QUERIES, ALL_KEYS), F32),
            pltpu.VMEM((COARSE, D), F32),
        ],
        scratch_shapes=[pltpu.VMEM((ROWS, D), BF), pltpu.SemaphoreType.DMA((4,))],
        compiler_params=params(16),
        cost_estimate=cost(900_000_000, 17_000_000),
        name="fine_prepare",
    )(place, *(in_hbm(x) for x in (tokens, cotangent, weights, fine_out)))


def fine_forward(place, tail, slots, own, weights, fine_out, own_q, own_k, own_v, own_kf, bias, cg, peers):
    return pl.pallas_call(
        fine_forward_kernel,
        in_specs=[SCALAR] + [IN_VMEM] * 11,
        out_specs=[IN_VMEM] * 7,
        out_shape=[
            pltpu.VMEM((OWN_KEYS, D), BF),
            pltpu.VMEM((OWN_KEYS, D), BF),
            pltpu.VMEM((OWN_KEYS, D), F32),
            pltpu.VMEM((HEADS, ROWS, OWN_KEYS), BF),
            pltpu.VMEM((ROWS, D), BF),
            shaped((ROWS, D), BF),
            shaped((peers, 2 * COARSE, D), BF),
        ],
        scratch_shapes=[pltpu.VMEM((HALO + EXTRA, D), BF), pltpu.VMEM((QUERIES, D), F32)],
        compiler_params=params(16),
        cost_estimate=cost(4_500_000_000, 20_000_000, 1_600_000),
        name="fine_forward",
    )(place, tail, slots, own, weights, fine_out, own_q, own_k, own_v, own_kf, bias, cg)


def coarse_prepare(core, weights, back):
    return pl.pallas_call(
        coarse_prepare_kernel,
        in_specs=[SCALAR, IN_VMEM, IN_VMEM],
        out_specs=[IN_VMEM] * 2,
        out_shape=[shaped((D, 2 * PAIR), BF), shaped((2 * PAIR, D), BF)],
        compiler_params=params(8),
        cost_estimate=cost(1_000_000, 2_500_000),
        name="coarse_prepare",
    )(core, weights, back)


def coarse_project(gathered, coarse_in, coarse_back, groups):
    rows = gathered.shape[0] * COARSE
    return pl.pallas_call(
        coarse_project_kernel,
        out_shape=[shaped((groups, rows, 2 * PAIR), BF), shaped((rows, 2 * PAIR), F32)],
        compiler_params=params(VMEM_MIB),
        cost_estimate=cost(140_000_000, 3_000_000),
        name="coarse_project",
    )(gathered, coarse_in, coarse_back)


def coarse_attention(place, everyone, factor, coarse_in, coarse_back):
    rows = factor.shape[0]
    return pl.pallas_call(
        coarse_attention_kernel,
        in_specs=[SCALAR] + [IN_VMEM] * 4,
        out_shape=shaped((rows // COARSE, 2 * COARSE, D), BF),
        scratch_shapes=[pltpu.VMEM((rows, PAIR), F32)],
        compiler_params=params(VMEM_MIB),
        cost_estimate=cost(1_500_000_000, 3_000_000, 3_000_000),
        name="coarse_attention",
    )(place, everyone, factor, coarse_in, coarse_back)


def coarse_finish(returned, message, coarse_grad):
    return pl.pallas_call(
        coarse_finish_kernel,
        grid=(1,),
        in_specs=[whole(returned.shape), whole((1, 2 * COARSE, D)), whole((COARSE, D))],
        out_specs=[whole((COARSE, D)), whole((1, D)), whole((COARSE, D))],
        out_shape=[shaped((COARSE, D), F32), shaped((1, D), F32), shaped((COARSE, D), F32)],
        compiler_params=params(VMEM_MIB),
        cost_estimate=cost(1_000_000, 1_000_000),
        name="coarse_finish",
    )(returned, message, coarse_grad)


def fine_backward(
    cotangent, spread, after, fine_out, weights, query, key, value, q_factor, k_factor, probs,
    attended,
):
    return pl.pallas_call(
        fine_backward_kernel,
        in_specs=[IN_VMEM] * 12,
        out_specs=[IN_VMEM] * 3,
        out_shape=[shaped((HALO // ROWS, ROWS, D), BF)] + [shaped((ROWS, D), F32)] * 2,
        scratch_shapes=[pltpu.VMEM((ROWS, D), BF), pltpu.VMEM((OWN_KEYS, D), F32)],
        compiler_params=params(16),
        cost_estimate=cost(5_000_000_000, 20_000_000),
        name="fine_backward",
    )(
        cotangent, spread, after, fine_out, weights, query, key, value, q_factor, k_factor, probs,
        attended,
    )


def halo_send(place, own, before, count):
    return pl.pallas_call(
        halo_send_kernel,
        grid=(count,),
        in_specs=[SCALAR, whole((ROWS, D)), whole((ROWS, D))],
        out_specs=pl.BlockSpec((1, ROWS, D), lambda p: (p, 0, 0)),
        out_shape=shaped((count, ROWS, D), BF),
        compiler_params=params(8),
        cost_estimate=cost(1_000_000, 1_500_000),
        name="halo_send",
    )(place, own, before)


def repeated(block, count):
    return pl.pallas_call(
        repeated_kernel,
        out_shape=shaped((count, *block.shape), BF),
        compiler_params=params(VMEM_MIB),
        cost_estimate=cost(1_000_000, 1_300_000),
        name="repeated",
    )(block)


def halo_sum(place, got):
    return pl.pallas_call(
        halo_sum_kernel,
        in_specs=[SCALAR, IN_VMEM],
        out_shape=shaped((ROWS, D), BF),
        compiler_params=params(VMEM_MIB),
        cost_estimate=cost(1_000_000, 1_500_000),
        name="halo_sum",
    )(place, got)


def fine_finish(place, own, got, arrived, hidden_grad, tokens):
    return pl.pallas_call(
        fine_finish_kernel,
        in_specs=[SCALAR] + [IN_VMEM] * 5,
        out_shape=shaped((ROWS, D), BF),
        compiler_params=params(VMEM_MIB),
        cost_estimate=cost(1_000_000, 3_000_000),
        name="fine_finish",
    )(place, own, got, arrived, hidden_grad, tokens)


def per_device(tokens, cotangent, fine_qkv, fine_out, coarse_qkv, coarse_out):
    peers = 1
    for name in GROUP:
        peers *= lax.axis_size(name)
    groups = 1
    for name in FAR:
        groups *= lax.axis_size(name)
    weights = jnp.transpose(fine_qkv, (1, 0, 2))
    core = lax.axis_index("core").astype(jnp.int32).reshape(1)
    column_at = lax.axis_index("x")
    columns_along = lax.axis_size("x")
    tail = shifted_by(tokens[ROWS - EXTRA :], columns_along + 1)
    row_before = shifted_by(tokens, columns_along)
    group_start = lax.axis_index(FAR) * (peers * COARSE)
    place = jnp.stack([lax.axis_index(LINE) * ROWS, column_at, group_start]).astype(jnp.int32)
    prepared = fine_prepare(place, tokens, cotangent, weights, fine_out)
    coarse_weights = coarse_prepare(core, jnp.transpose(coarse_qkv, (1, 0, 2)), coarse_out)
    tail, row_before, prepared, coarse_weights, place = lax.optimization_barrier(
        (tail, row_before, prepared, coarse_weights, place)
    )
    own, weights, fine_out, query, own_key, own_value, q_factor, own_k_factor, bias, coarse_grad = prepared
    coarse_in, coarse_back = coarse_weights
    slots = exchanged(halo_send(place, own, row_before, columns_along), "x")
    key, value, k_factor, probs, attended, hidden, message = fine_forward(
        place, tail, slots, own, weights, fine_out, query, own_key, own_value, own_k_factor, bias,
        coarse_grad, peers,
    )
    gathered = exchanged(message, GROUP)
    near, further = lax.axis_size("z_hi"), lax.axis_size("y")
    coarse_send, coarse_factor = coarse_project(gathered, coarse_in, coarse_back, near)
    group_rows = coarse_factor.shape[0]
    nearby = exchanged(coarse_send, "z_hi").reshape(near * group_rows, 2 * PAIR)
    everyone = exchanged(repeated(nearby, further), "y").reshape(groups * group_rows, 2 * PAIR)
    partial = coarse_attention(place, everyone, coarse_factor, coarse_in, coarse_back)
    returned = exchanged(partial, GROUP)
    spread, first, state = coarse_finish(returned, message, coarse_grad)
    after = shifted_by(first, -1)
    output = (
        hidden.astype(F32) + jnp.repeat(state.astype(BF), POOL, axis=0).astype(F32)
    ).astype(BF)
    halo, own_grad, hidden_grad = fine_backward(
        cotangent, spread, after, fine_out, weights, query, key, value, q_factor, k_factor, probs,
        attended,
    )
    got = exchanged(halo, "x")
    arrived = shifted_by(halo_sum(place, got), -columns_along)
    return (output, fine_finish(place, own_grad, got, arrived, hidden_grad, own))


def solution(mesh):
    sizes = (4, 4, 2, 2, 4)
    fine_mesh = Mesh(mesh.devices.reshape(sizes), LINE)
    placed = (
        P(LINE, None),
        P(LINE, None),
        P(),
        P(),
        P(None, None, ("z_lo", "x")),
        P(("z_lo", "x"), None),
    )
    return jax.shard_map(
        per_device,
        mesh=fine_mesh,
        in_specs=placed,
        out_specs=(P(LINE, None), P(LINE, None)),
        check_vma=False,
    )
```

```python
import jax
import jax.numpy as jnp
from jax import lax
from jax.experimental import pallas as pl
from jax.experimental.pallas import tpu as pltpu
from jax.sharding import Mesh
from jax.sharding import PartitionSpec as P

D = 1024
HEADS = 16
HEAD_DIM = 64
WINDOW = 512
POOL = 16
EPS = 1e-06

LINE = ("y", "z_hi", "core", "z_lo", "x")
GROUP = ("core", "z_lo", "x")
FAR = ("y", "z_hi")

ROWS = 128
HALO = WINDOW
OWN_KEYS = HALO + ROWS
EXTRA = 16
ALL_KEYS = OWN_KEYS + EXTRA
QUERIES = EXTRA + ROWS
PAIR = 2 * HEAD_DIM
COARSE = ROWS // POOL
SCALE = HEAD_DIM ** (-0.5)
NEG = -1e30
VMEM_MIB = 16

BF = jnp.bfloat16
F32 = jnp.float32


def shifted_by(value, steps):
    count = 1
    for name in LINE:
        count *= lax.axis_size(name)
    first, last = (max(0, -steps), min(count, count - steps))
    return lax.ppermute(value, LINE, [(source, source + steps) for source in range(first, last)])


def exchanged(pieces, axes):
    return lax.all_to_all(pieces, axes, 0, 0, tiled=True)


def last_last(left, right):
    return lax.dot_general(left, right, (((1,), (1,)), ((), ())), preferred_element_type=F32)


def first_first(left, right):
    return lax.dot_general(left, right, (((0,), (0,)), ((), ())), preferred_element_type=F32)


def plain(left, right):
    return jnp.dot(left, right, preferred_element_type=F32)


def low_lanes():
    return lax.broadcasted_iota(jnp.int32, (1, PAIR), 1) < HEAD_DIM


def pair_sums(values, low):
    low_sum = jnp.sum(jnp.where(low, values, 0.0), axis=-1, keepdims=True)
    high_sum = jnp.sum(jnp.where(low, 0.0, values), axis=-1, keepdims=True)
    return jnp.where(low, low_sum, high_sum)


def pair_norm(values, low):
    factor = lax.rsqrt(pair_sums(values * values, low) * (1.0 / HEAD_DIM) + EPS)
    return values * factor, factor


def pair_norm_back(grad, unit, factor, low):
    return factor * (grad - unit * (pair_sums(unit * grad, low) * (1.0 / HEAD_DIM)))


def row_norm(rows):
    factor = lax.rsqrt(jnp.mean(rows * rows, axis=-1, keepdims=True) + EPS)
    return rows * factor, factor


def row_norm_back(grad, normed, factor):
    return factor * (grad - normed * jnp.mean(normed * grad, axis=-1, keepdims=True))


def fine_prepare_kernel(
    place_ref, own_hbm, cot_hbm, w_hbm, out_w_hbm,
    own_ref, w_ref, out_w_ref, q_ref, k_ref, v_ref, qf_ref, kf_ref, bias_ref, cg_ref,
    cot, copied,
):
    anchor = place_ref[0]
    column_at = place_ref[1]
    low = low_lanes()
    copies = [
        pltpu.make_async_copy(source, target, copied.at[at])
        for at, (source, target) in enumerate(
            ((own_hbm, own_ref), (cot_hbm, cot), (w_hbm, w_ref), (out_w_hbm, out_w_ref))
        )
    ]
    for copy in copies:
        copy.start()

    row = lax.broadcasted_iota(jnp.int32, (2 * QUERIES, ALL_KEYS), 0)
    query_pos = jnp.where(row < QUERIES, row, row - QUERIES) - EXTRA
    column = lax.broadcasted_iota(jnp.int32, (2 * QUERIES, ALL_KEYS), 1)
    turned = column_at * ROWS
    halo_pos = column - jnp.where(column >= turned, turned + HALO, turned)
    key_pos = jnp.where(
        column < HALO,
        halo_pos,
        jnp.where(column < OWN_KEYS, column - HALO, column - (OWN_KEYS + HALO + EXTRA)),
    )
    gap = query_pos - key_pos
    allowed = (gap >= 0) & (gap < WINDOW) & (anchor + key_pos >= 0)
    bias_ref[...] = jnp.where(allowed, 0.0, NEG)

    copies[0].wait()
    normed = row_norm(own_ref[...].astype(F32))[0].astype(BF)
    copies[1].wait()
    chunk = lax.broadcasted_iota(jnp.int32, (COARSE, ROWS), 0) * POOL
    row = lax.broadcasted_iota(jnp.int32, (COARSE, ROWS), 1)
    member = jnp.where((row >= chunk) & (row < chunk + POOL), 1.0, 0.0).astype(BF)
    cg_ref[...] = plain(member, cot[...])
    copies[2].wait()
    for at in range(0, D, WIDTH):
        here = slice(at, at + WIDTH)
        queries = plain(normed, w_ref[0, :, here])
        keys = plain(normed, w_ref[1, :, here])
        v_ref[:, here] = plain(normed, w_ref[2, :, here]).astype(BF)
        for part in range(0, WIDTH, PAIR):
            inner = slice(part, part + PAIR)
            outer = slice(at + part, at + part + PAIR)
            query, q_factor = pair_norm(queries[:, inner], low)
            key, k_factor = pair_norm(keys[:, inner], low)
            q_ref[:, outer] = query.astype(BF)
            k_ref[:, outer] = key.astype(BF)
            qf_ref[:, outer] = q_factor
            kf_ref[:, outer] = k_factor
    copies[3].wait()


def fine_forward_kernel(
    place_ref, tail_ref, slots_ref, own_ref, w_ref, out_w_ref, own_q_ref, own_k_ref, own_v_ref,
    own_kf_ref, bias, cg_ref,
    k_ref, v_ref, kf_ref, p_ref, att_ref, hid_ref, send_ref,
    normed, acc,
):
    anchor = place_ref[0]
    column_at = place_ref[1]
    low = low_lanes()
    slots = slots_ref.shape[0]
    nearest = lax.rem(column_at + (slots - 1), slots)
    for slot in range(slots):
        at = slot * ROWS
        normed[at : at + ROWS, :] = row_norm(slots_ref[slot].astype(F32))[0].astype(BF)
    normed[HALO:, :] = row_norm(tail_ref[...].astype(F32))[0].astype(BF)
    acc[...] = jnp.zeros_like(acc)
    extra_at = pl.multiple_of(nearest * ROWS + (ROWS - EXTRA), EXTRA)

    def one_step(step, carry):
        first = pl.multiple_of(step * WIDTH, WIDTH)
        here = pl.ds(first, WIDTH)
        extra = plain(normed[pl.ds(extra_at, EXTRA), :], w_ref[0, :, here])
        both = plain(
            normed[...], jnp.concatenate([w_ref[1, :, here], w_ref[2, :, here]], axis=1)
        )
        own_q, own_k, own_v = own_q_ref[:, here], own_k_ref[:, here], own_v_ref[:, here]
        own_kf = own_kf_ref[:, here]
        mixed = []
        for part in range(0, WIDTH, PAIR):
            inner = slice(part, part + PAIR)
            outer = pl.ds(pl.multiple_of(first + part, PAIR), PAIR)
            key, k_factor = pair_norm(both[:, inner], low)
            key = key.astype(BF)
            value = both[:, WIDTH + part : WIDTH + part + PAIR].astype(BF)
            k_ref[:HALO, outer] = key[:HALO]
            k_ref[HALO:, outer] = own_k[:, inner]
            v_ref[:HALO, outer] = value[:HALO]
            v_ref[HALO:, outer] = own_v[:, inner]
            kf_ref[:HALO, outer] = k_factor[:HALO]
            kf_ref[HALO:, outer] = own_kf[:, inner]
            key = jnp.concatenate([key[:HALO], own_k[:, inner], key[HALO:]], axis=0)
            value = jnp.concatenate([value[:HALO], own_v[:, inner], value[HALO:]], axis=0)
            before = pair_norm(extra[:, inner], low)[0].astype(BF).astype(F32)
            scaled = jnp.concatenate([before, own_q[:, inner].astype(F32)], axis=0) * SCALE
            stacked = jnp.concatenate(
                [jnp.where(low, scaled, 0.0), jnp.where(low, 0.0, scaled)], axis=0
            )
            numer = jnp.exp(last_last(stacked.astype(BF), key) + bias[...])
            total = jnp.sum(numer, axis=-1, keepdims=True)
            prob = (numer * (1.0 / jnp.where(total > 0.0, total, 1.0))).astype(BF)
            head = (first + part) // HEAD_DIM
            p_ref[head] = prob[EXTRA:QUERIES, :OWN_KEYS]
            p_ref[head + 1] = prob[QUERIES + EXTRA :, :OWN_KEYS]
            twice = plain(prob, value)
            attended = jnp.where(low, twice[:QUERIES], twice[QUERIES:]).astype(BF)
            att_ref[:, outer] = attended[EXTRA:]
            mixed.append(attended)
        acc[...] += plain(jnp.concatenate(mixed, axis=1), out_w_ref[here, :])
        return carry

    lax.fori_loop(0, D // WIDTH, one_step, 0, unroll=True)
    before = slots_ref[nearest, ROWS - EXTRA :, :].astype(F32) + acc[:EXTRA, :]
    before = jnp.where(anchor > 0, before, 0.0).astype(BF)
    own = (own_ref[...].astype(F32) + acc[EXTRA:, :]).astype(BF)
    hid_ref[...] = own
    chunk = lax.broadcasted_iota(jnp.int32, (COARSE, QUERIES), 0) * POOL
    row = lax.broadcasted_iota(jnp.int32, (COARSE, QUERIES), 1)
    member = jnp.where((row > chunk) & (row <= chunk + POOL), 1.0, 0.0).astype(BF)
    pooled = plain(member, jnp.concatenate([before, own], axis=0)) * (1.0 / POOL)
    message = jnp.concatenate([pooled, cg_ref[...]], axis=0).astype(BF)
    for peer in range(send_ref.shape[0]):
        send_ref[peer] = message


def coarse_prepare_kernel(core_ref, w_ref, back_ref, in_ref, out_ref):
    low = low_lanes()
    second = core_ref[0] > 0
    parts = [w_ref[at].astype(F32) for at in range(3)]
    turned = [pltpu.roll(part, HEAD_DIM, 1) for part in parts]
    query = jnp.where(second, turned[0], parts[0])
    key = jnp.where(second, turned[1], parts[1])
    value = jnp.where(second, parts[2], turned[2])
    in_ref[:, :PAIR] = jnp.where(low, query, 0.0).astype(BF)
    in_ref[:, PAIR:] = jnp.where(low, key, value).astype(BF)
    out_ref[...] = jnp.zeros_like(out_ref)
    out_ref[HEAD_DIM:PAIR, :] = jnp.where(second, back_ref[HEAD_DIM:, :], back_ref[:HEAD_DIM, :])


def coarse_project_kernel(got_ref, in_w_ref, out_w_ref, send_ref, factor_ref):
    low = low_lanes()
    rows = got_ref[...].astype(F32)
    count = rows.shape[0] * COARSE
    pooled = rows[:, :COARSE, :].reshape(count, D)
    coarse_grad = rows[:, COARSE:, :].reshape(count, D)
    normed = row_norm(pooled)[0].astype(BF)
    raw = plain(normed, in_w_ref[...]) + last_last(coarse_grad.astype(BF), out_w_ref[...])
    units, factors = [], []
    for tile in (raw[:, :PAIR], raw[:, PAIR:]):
        unit, factor = pair_norm(tile, low)
        units.append(jnp.where(low, unit, tile))
        factors.append(factor)
    message = jnp.concatenate(units, axis=1).astype(BF)
    factor_ref[...] = jnp.concatenate(factors, axis=1)
    for peer in range(send_ref.shape[0]):
        send_ref[peer] = message


def coarse_attention_kernel(place_ref, got_ref, factor_ref, in_w_ref, out_w_ref, send_ref, own_grad):
    low = low_lanes()
    own_start = pl.multiple_of(place_ref[2], ROWS)
    length = got_ref.shape[0]
    block = 512
    own_left = got_ref[pl.ds(own_start, ROWS), :PAIR]
    own_right = got_ref[pl.ds(own_start, ROWS), PAIR:]
    own_grad[...] = jnp.zeros_like(own_grad)

    def masked_halves(tile):
        wide = tile.astype(F32)
        return (
            jnp.where(low, wide * SCALE, 0.0).astype(BF),
            jnp.where(low, 0.0, wide).astype(BF),
        )

    def lane_partials(values):
        total = values[:, :PAIR]
        for at in range(PAIR, values.shape[1], PAIR):
            total = total + values[:, at : at + PAIR]
        return total

    def one_block(index):
        first = index * block
        query, grad = masked_halves(got_ref[first : first + block, :PAIR])
        stacked = jnp.concatenate([query, grad], axis=0)

        def scored(keys):
            both = last_last(stacked, keys)
            return jnp.exp(both[:block]), both[block:]

        query_at = lax.broadcasted_iota(jnp.int32, (block, 1), 0)
        total = product = None
        for at in range(index + 1):
            numer, prob_grad = scored(got_ref[at * block : (at + 1) * block, PAIR:])
            if at == index:
                key_at = lax.broadcasted_iota(jnp.int32, (1, block), 1)
                numer = jnp.where(key_at <= query_at, numer, 0.0)
            sums = lane_partials(numer), lane_partials(numer * prob_grad)
            total, product = sums if at == 0 else (total + sums[0], product + sums[1])
        inverse = 1.0 / jnp.sum(total, axis=-1, keepdims=True)
        delta = jnp.sum(product, axis=-1, keepdims=True) * inverse
        own_pos = own_start + lax.broadcasted_iota(jnp.int32, (1, ROWS), 1)
        numer, prob_grad = scored(own_right)
        numer = jnp.where(own_pos <= query_at + first, numer, 0.0)
        prob = numer * inverse
        score_grad = (prob * (prob_grad - delta)).astype(BF)
        own_grad[...] += first_first(
            jnp.concatenate([score_grad, prob.astype(BF)], axis=0), stacked
        )

    for index in range(length // block):
        pl.when(own_start < (index + 1) * block)(lambda index=index: one_block(index))

    query, grad = masked_halves(own_left)
    stacked = jnp.concatenate([query, grad], axis=0)
    query_pos = own_start + lax.broadcasted_iota(jnp.int32, (ROWS, 1), 0)

    def own_chunk(at):
        key_start = pl.multiple_of(at * block, block)
        keys = got_ref[pl.ds(key_start, block), PAIR:]
        both = last_last(stacked, keys)
        key_pos = key_start + lax.broadcasted_iota(jnp.int32, (1, block), 1)
        return keys, jnp.where(key_pos <= query_pos, jnp.exp(both[:ROWS]), 0.0), both[ROWS:]

    def own_sums(at, sums):
        numer, prob_grad = own_chunk(at)[1:]
        return sums[0] + lane_partials(numer), sums[1] + lane_partials(numer * prob_grad)

    nothing = jnp.zeros((ROWS, PAIR), F32)
    chunks = own_start // block + 1
    total, product = lax.fori_loop(0, chunks, own_sums, (nothing, nothing))
    inverse = 1.0 / jnp.sum(total, axis=-1, keepdims=True)
    delta = jnp.sum(product, axis=-1, keepdims=True) * inverse

    def own_results(at, mine):
        keys, numer, prob_grad = own_chunk(at)
        key_scaled, value = masked_halves(keys)
        prob = numer * inverse
        score_grad = (prob * (prob_grad - delta)).astype(BF)
        return mine + plain(score_grad, key_scaled) + plain(prob.astype(BF), value)

    mine = lax.fori_loop(0, chunks, own_results, nothing)

    parts = []
    for tile, unit, factor in (
        (mine, own_left, factor_ref[:, :PAIR]),
        (own_grad[...], own_right, factor_ref[:, PAIR:]),
    ):
        back = pair_norm_back(tile, unit.astype(F32), factor, low)
        parts.append(jnp.where(low, back, tile))
    parts = jnp.concatenate(parts, axis=1).astype(BF)
    peers = send_ref.shape[0]
    normed_grad = last_last(parts, in_w_ref[...]).reshape(peers, COARSE, D)
    mixed = plain(parts, out_w_ref[...]).reshape(peers, COARSE, D)
    send_ref[...] = jnp.concatenate([normed_grad, mixed], axis=1).astype(BF)


def coarse_finish_kernel(got_ref, message_ref, cg_ref, spread_ref, first_ref, state_ref):
    summed = jnp.sum(got_ref[...].astype(F32), axis=0)
    pooled = message_ref[0].astype(F32)[:COARSE]
    normed, factor = row_norm(pooled)
    pooled_grad = cg_ref[...] + row_norm_back(summed[:COARSE], normed, factor)
    spread = pooled_grad * (1.0 / POOL)
    spread_ref[...] = spread
    first_ref[...] = spread[:1]
    state_ref[...] = pooled + summed[COARSE:]


def fine_backward_kernel(
    cot_ref, spread_ref, next_ref, out_w_ref, w_ref, q_ref, k_ref, v_ref, qf_ref, kf_ref, p_ref,
    att_ref,
    halo_ref, own_ref, hg_ref, hidden_grad, acc,
):
    low = low_lanes()
    block = (lax.broadcasted_iota(jnp.int32, (ROWS, 1), 0) + (POOL - 1)) // POOL
    added = jnp.zeros((ROWS, D), F32)
    for at in range(COARSE):
        added = jnp.where(block == at, spread_ref[at : at + 1, :], added)
    added = jnp.where(block == COARSE, next_ref[0:1, :], added)
    total = cot_ref[...].astype(F32) + added
    hg_ref[...] = total
    hidden_grad[...] = total.astype(BF)
    acc[...] = jnp.zeros_like(acc)

    def one_step(step, carry):
        first = pl.multiple_of(step * WIDTH, WIDTH)
        here = pl.ds(first, WIDTH)
        att_grads = last_last(hidden_grad[...], out_w_ref[here, :]).astype(BF).astype(F32)
        query_grads, key_grads, value_grads = [], [], []
        for part in range(0, WIDTH, PAIR):
            outer = pl.ds(pl.multiple_of(first + part, PAIR), PAIR)
            att_grad = att_grads[:, part : part + PAIR]
            delta_all = att_grad * att_ref[:, outer].astype(F32)
            value = v_ref[:, outer]
            key_wide = k_ref[:, outer].astype(F32)
            query_wide = q_ref[:, outer].astype(F32)
            grad = jnp.concatenate(
                [jnp.where(low, att_grad, 0.0), jnp.where(low, 0.0, att_grad)], axis=0
            ).astype(BF)
            delta = jnp.sum(
                jnp.concatenate(
                    [jnp.where(low, delta_all, 0.0), jnp.where(low, 0.0, delta_all)], axis=0
                ),
                axis=-1,
                keepdims=True,
            )
            scaled = query_wide * SCALE
            query = jnp.concatenate(
                [jnp.where(low, scaled, 0.0), jnp.where(low, 0.0, scaled)], axis=0
            ).astype(BF)
            head = (first + part) // HEAD_DIM
            prob = p_ref[pl.ds(head, 2)].reshape(2 * ROWS, OWN_KEYS)
            score_grad = (prob.astype(F32) * (last_last(grad, value) - delta)).astype(BF)
            twice = plain(score_grad, (key_wide * SCALE).astype(BF))
            query_grad = jnp.where(low, twice[:ROWS], twice[ROWS:])
            key_grad = first_first(score_grad, query)
            value_grad = first_first(prob, grad)
            query_grads.append(pair_norm_back(query_grad, query_wide, qf_ref[:, outer], low).astype(BF))
            key_grads.append(pair_norm_back(key_grad, key_wide, kf_ref[:, outer], low).astype(BF))
            value_grads.append(value_grad.astype(BF))
        both = jnp.concatenate(key_grads + value_grads, axis=1)
        acc[...] += last_last(
            both, jnp.concatenate([w_ref[1, :, here], w_ref[2, :, here]], axis=1)
        )
        acc[HALO:, :] += last_last(jnp.concatenate(query_grads, axis=1), w_ref[0, :, here])
        return carry

    lax.fori_loop(0, D // WIDTH, one_step, 0, unroll=True)
    for slot in range(halo_ref.shape[0]):
        halo_ref[slot] = acc[slot * ROWS : (slot + 1) * ROWS, :].astype(BF)
    own_ref[...] = acc[HALO:, :]


def halo_send_kernel(place_ref, own_ref, before_ref, send_ref):
    send_ref[0] = jnp.where(place_ref[1] < pl.program_id(0), own_ref[...], before_ref[...])


def repeated_kernel(block_ref, send_ref):
    for peer in range(send_ref.shape[0]):
        send_ref[peer] = block_ref[...]


def halo_sum_kernel(place_ref, got_ref, back_ref):
    column_at = place_ref[1]
    total = got_ref[0].astype(F32)
    for slot in range(1, got_ref.shape[0]):
        total = total + jnp.where(column_at >= slot, got_ref[slot].astype(F32), 0.0)
    back_ref[...] = total.astype(BF)


def halo_keep_kernel(place_ref, own_ref, got_ref, kept_ref):
    column_at = place_ref[1]
    total = own_ref[...]
    for slot in range(1, got_ref.shape[0]):
        total = total + jnp.where(column_at < slot, got_ref[slot].astype(F32), 0.0)
    kept_ref[...] = total


def fine_finish_kernel(kept_ref, arrived_ref, hg_ref, tokens_ref, out_ref):
    total = kept_ref[...] + arrived_ref[...].astype(F32)
    normed, factor = row_norm(tokens_ref[...].astype(F32))
    out_ref[...] = (hg_ref[...] + row_norm_back(total, normed, factor)).astype(BF)


def whole(shape):
    return pl.BlockSpec(shape, lambda *_: (0,) * len(shape))


def columns(rows, width):
    return pl.BlockSpec((rows, width), lambda p: (0, p))


def shaped(shape, kind):
    return jax.ShapeDtypeStruct(shape, kind)


def params(mib):
    return pltpu.CompilerParams(vmem_limit_bytes=mib << 20)


def cost(flops, moved, exps=0):
    return pl.CostEstimate(flops=flops, bytes_accessed=moved, transcendentals=exps)


SCALAR = pl.BlockSpec(memory_space=pltpu.SMEM)
IN_VMEM = pl.BlockSpec(memory_space=pltpu.VMEM)
WIDTH = 2 * PAIR


def in_hbm(x):
    return pltpu.with_memory_space_constraint(x, pltpu.HBM)


def fine_prepare(place, tokens, cotangent, weights, fine_out):
    anywhere = pl.BlockSpec(memory_space=pltpu.HBM)
    return pl.pallas_call(
        fine_prepare_kernel,
        in_specs=[SCALAR] + [anywhere] * 4,
        out_specs=[IN_VMEM] * 10,
        out_shape=[
            pltpu.VMEM((ROWS, D), BF),
            pltpu.VMEM((3, D, D), BF),
            pltpu.VMEM((D, D), BF),
            pltpu.VMEM((ROWS, D), BF),
            pltpu.VMEM((ROWS, D), BF),
            pltpu.VMEM((ROWS, D), BF),
            pltpu.VMEM((ROWS, D), F32),
            pltpu.VMEM((ROWS, D), F32),
            pltpu.VMEM((2 * QUERIES, ALL_KEYS), F32),
            pltpu.VMEM((COARSE, D), F32),
        ],
        scratch_shapes=[pltpu.VMEM((ROWS, D), BF), pltpu.SemaphoreType.DMA((4,))],
        compiler_params=params(16),
        cost_estimate=cost(900_000_000, 17_000_000),
        name="fine_prepare",
    )(place, *(in_hbm(x) for x in (tokens, cotangent, weights, fine_out)))


def fine_forward(place, tail, slots, own, weights, fine_out, own_q, own_k, own_v, own_kf, bias, cg, peers):
    return pl.pallas_call(
        fine_forward_kernel,
        in_specs=[SCALAR] + [IN_VMEM] * 11,
        out_specs=[IN_VMEM] * 7,
        out_shape=[
            pltpu.VMEM((OWN_KEYS, D), BF),
            pltpu.VMEM((OWN_KEYS, D), BF),
            pltpu.VMEM((OWN_KEYS, D), F32),
            pltpu.VMEM((HEADS, ROWS, OWN_KEYS), BF),
            pltpu.VMEM((ROWS, D), BF),
            shaped((ROWS, D), BF),
            shaped((peers, 2 * COARSE, D), BF),
        ],
        scratch_shapes=[pltpu.VMEM((HALO + EXTRA, D), BF), pltpu.VMEM((QUERIES, D), F32)],
        compiler_params=params(16),
        cost_estimate=cost(4_500_000_000, 20_000_000, 1_600_000),
        name="fine_forward",
    )(place, tail, slots, own, weights, fine_out, own_q, own_k, own_v, own_kf, bias, cg)


def coarse_prepare(core, weights, back):
    return pl.pallas_call(
        coarse_prepare_kernel,
        in_specs=[SCALAR, IN_VMEM, IN_VMEM],
        out_specs=[IN_VMEM] * 2,
        out_shape=[shaped((D, 2 * PAIR), BF), shaped((2 * PAIR, D), BF)],
        compiler_params=params(8),
        cost_estimate=cost(1_000_000, 2_500_000),
        name="coarse_prepare",
    )(core, weights, back)


def coarse_project(gathered, coarse_in, coarse_back, groups):
    rows = gathered.shape[0] * COARSE
    return pl.pallas_call(
        coarse_project_kernel,
        out_shape=[shaped((groups, rows, 2 * PAIR), BF), shaped((rows, 2 * PAIR), F32)],
        compiler_params=params(VMEM_MIB),
        cost_estimate=cost(140_000_000, 3_000_000),
        name="coarse_project",
    )(gathered, coarse_in, coarse_back)


def coarse_attention(place, everyone, factor, coarse_in, coarse_back):
    rows = factor.shape[0]
    return pl.pallas_call(
        coarse_attention_kernel,
        in_specs=[SCALAR] + [IN_VMEM] * 4,
        out_shape=shaped((rows // COARSE, 2 * COARSE, D), BF),
        scratch_shapes=[pltpu.VMEM((rows, PAIR), F32)],
        compiler_params=params(VMEM_MIB),
        cost_estimate=cost(1_500_000_000, 3_000_000, 3_000_000),
        name="coarse_attention",
    )(place, everyone, factor, coarse_in, coarse_back)


def coarse_finish(returned, message, coarse_grad):
    return pl.pallas_call(
        coarse_finish_kernel,
        grid=(1,),
        in_specs=[whole(returned.shape), whole((1, 2 * COARSE, D)), whole((COARSE, D))],
        out_specs=[whole((COARSE, D)), whole((1, D)), whole((COARSE, D))],
        out_shape=[shaped((COARSE, D), F32), shaped((1, D), F32), shaped((COARSE, D), F32)],
        compiler_params=params(VMEM_MIB),
        cost_estimate=cost(1_000_000, 1_000_000),
        name="coarse_finish",
    )(returned, message, coarse_grad)


def fine_backward(
    cotangent, spread, after, fine_out, weights, query, key, value, q_factor, k_factor, probs,
    attended,
):
    return pl.pallas_call(
        fine_backward_kernel,
        in_specs=[IN_VMEM] * 12,
        out_specs=[IN_VMEM] * 3,
        out_shape=[shaped((HALO // ROWS, ROWS, D), BF)] + [shaped((ROWS, D), F32)] * 2,
        scratch_shapes=[pltpu.VMEM((ROWS, D), BF), pltpu.VMEM((OWN_KEYS, D), F32)],
        compiler_params=params(16),
        cost_estimate=cost(5_000_000_000, 20_000_000),
        name="fine_backward",
    )(
        cotangent, spread, after, fine_out, weights, query, key, value, q_factor, k_factor, probs,
        attended,
    )


def halo_send(place, own, before, count):
    return pl.pallas_call(
        halo_send_kernel,
        grid=(count,),
        in_specs=[SCALAR, whole((ROWS, D)), whole((ROWS, D))],
        out_specs=pl.BlockSpec((1, ROWS, D), lambda p: (p, 0, 0)),
        out_shape=shaped((count, ROWS, D), BF),
        compiler_params=params(8),
        cost_estimate=cost(1_000_000, 1_500_000),
        name="halo_send",
    )(place, own, before)


def repeated(block, count):
    return pl.pallas_call(
        repeated_kernel,
        out_shape=shaped((count, *block.shape), BF),
        compiler_params=params(VMEM_MIB),
        cost_estimate=cost(1_000_000, 1_300_000),
        name="repeated",
    )(block)


def halo_sum(place, got):
    return pl.pallas_call(
        halo_sum_kernel,
        in_specs=[SCALAR, IN_VMEM],
        out_shape=shaped((ROWS, D), BF),
        compiler_params=params(VMEM_MIB),
        cost_estimate=cost(1_000_000, 1_500_000),
        name="halo_sum",
    )(place, got)


def halo_keep(place, own, got):
    return pl.pallas_call(
        halo_keep_kernel,
        in_specs=[SCALAR, IN_VMEM, IN_VMEM],
        out_shape=shaped((ROWS, D), F32),
        compiler_params=params(VMEM_MIB),
        cost_estimate=cost(1_000_000, 1_500_000),
        name="halo_keep",
    )(place, own, got)


def fine_finish(kept, arrived, hidden_grad, tokens):
    return pl.pallas_call(
        fine_finish_kernel,
        out_shape=shaped((ROWS, D), BF),
        compiler_params=params(VMEM_MIB),
        cost_estimate=cost(1_000_000, 3_000_000),
        name="fine_finish",
    )(kept, arrived, hidden_grad, tokens)


def per_device(tokens, cotangent, fine_qkv, fine_out, coarse_qkv, coarse_out):
    peers = 1
    for name in GROUP:
        peers *= lax.axis_size(name)
    groups = 1
    for name in FAR:
        groups *= lax.axis_size(name)
    weights = jnp.transpose(fine_qkv, (1, 0, 2))
    core = lax.axis_index("core").astype(jnp.int32).reshape(1)
    column_at = lax.axis_index("x")
    columns_along = lax.axis_size("x")
    tail = shifted_by(tokens[ROWS - EXTRA :], columns_along + 1)
    row_before = shifted_by(tokens, columns_along)
    group_start = lax.axis_index(FAR) * (peers * COARSE)
    place = jnp.stack([lax.axis_index(LINE) * ROWS, column_at, group_start]).astype(jnp.int32)
    prepared = fine_prepare(place, tokens, cotangent, weights, fine_out)
    coarse_weights = coarse_prepare(core, jnp.transpose(coarse_qkv, (1, 0, 2)), coarse_out)
    tail, row_before, prepared, coarse_weights, place = lax.optimization_barrier(
        (tail, row_before, prepared, coarse_weights, place)
    )
    own, weights, fine_out, query, own_key, own_value, q_factor, own_k_factor, bias, coarse_grad = prepared
    coarse_in, coarse_back = coarse_weights
    slots = exchanged(halo_send(place, own, row_before, columns_along), "x")
    key, value, k_factor, probs, attended, hidden, message = fine_forward(
        place, tail, slots, own, weights, fine_out, query, own_key, own_value, own_k_factor, bias,
        coarse_grad, peers,
    )
    gathered = exchanged(message, GROUP)
    near, further = lax.axis_size("z_hi"), lax.axis_size("y")
    coarse_send, coarse_factor = coarse_project(gathered, coarse_in, coarse_back, near)
    group_rows = coarse_factor.shape[0]
    nearby = exchanged(coarse_send, "z_hi").reshape(near * group_rows, 2 * PAIR)
    everyone = exchanged(repeated(nearby, further), "y").reshape(groups * group_rows, 2 * PAIR)
    partial = coarse_attention(place, everyone, coarse_factor, coarse_in, coarse_back)
    returned = exchanged(partial, GROUP)
    spread, first, state = coarse_finish(returned, message, coarse_grad)
    after = shifted_by(first, -1)
    output = (
        hidden.astype(F32) + jnp.repeat(state.astype(BF), POOL, axis=0).astype(F32)
    ).astype(BF)
    halo, own_grad, hidden_grad = fine_backward(
        cotangent, spread, after, fine_out, weights, query, key, value, q_factor, k_factor, probs,
        attended,
    )
    got = exchanged(halo, "x")
    arrived = shifted_by(halo_sum(place, got), -columns_along)
    kept = halo_keep(place, own_grad, got)
    return (output, fine_finish(kept, arrived, hidden_grad, own))


def solution(mesh):
    sizes = (4, 4, 2, 2, 4)
    fine_mesh = Mesh(mesh.devices.reshape(sizes), LINE)
    placed = (
        P(LINE, None),
        P(LINE, None),
        P(),
        P(),
        P(None, None, ("z_lo", "x")),
        P(("z_lo", "x"), None),
    )
    return jax.shard_map(
        per_device,
        mesh=fine_mesh,
        in_specs=placed,
        out_specs=(P(LINE, None), P(LINE, None)),
        check_vma=False,
    )
```

```python
import jax
import jax.numpy as jnp
from jax import lax
from jax.experimental import pallas as pl
from jax.experimental.pallas import tpu as pltpu
from jax.sharding import Mesh
from jax.sharding import PartitionSpec as P

D = 1024
HEADS = 16
HEAD_DIM = 64
WINDOW = 512
POOL = 16
EPS = 1e-06

LINE = ("y", "z_hi", "core", "z_lo", "x")
GROUP = ("core", "z_lo", "x")
FAR = ("y", "z_hi")

ROWS = 128
HALO = WINDOW
OWN_KEYS = HALO + ROWS
EXTRA = 16
ALL_KEYS = OWN_KEYS + EXTRA
QUERIES = EXTRA + ROWS
PAIR = 2 * HEAD_DIM
COARSE = ROWS // POOL
SCALE = HEAD_DIM ** (-0.5)
NEG = -1e30
VMEM_MIB = 16

BF = jnp.bfloat16
F32 = jnp.float32


def shifted_by(value, steps):
    count = 1
    for name in LINE:
        count *= lax.axis_size(name)
    first, last = (max(0, -steps), min(count, count - steps))
    return lax.ppermute(value, LINE, [(source, source + steps) for source in range(first, last)])


def exchanged(pieces, axes):
    return lax.all_to_all(pieces, axes, 0, 0, tiled=True)


def last_last(left, right):
    return lax.dot_general(left, right, (((1,), (1,)), ((), ())), preferred_element_type=F32)


def first_first(left, right):
    return lax.dot_general(left, right, (((0,), (0,)), ((), ())), preferred_element_type=F32)


def plain(left, right):
    return jnp.dot(left, right, preferred_element_type=F32)


def low_lanes():
    return lax.broadcasted_iota(jnp.int32, (1, PAIR), 1) < HEAD_DIM


def pair_sums(values, low):
    low_sum = jnp.sum(jnp.where(low, values, 0.0), axis=-1, keepdims=True)
    high_sum = jnp.sum(jnp.where(low, 0.0, values), axis=-1, keepdims=True)
    return jnp.where(low, low_sum, high_sum)


def pair_norm(values, low):
    factor = lax.rsqrt(pair_sums(values * values, low) * (1.0 / HEAD_DIM) + EPS)
    return values * factor, factor


def pair_norm_back(grad, unit, factor, low):
    return factor * (grad - unit * (pair_sums(unit * grad, low) * (1.0 / HEAD_DIM)))


def row_norm(rows):
    factor = lax.rsqrt(jnp.mean(rows * rows, axis=-1, keepdims=True) + EPS)
    return rows * factor, factor


def row_norm_back(grad, normed, factor):
    return factor * (grad - normed * jnp.mean(normed * grad, axis=-1, keepdims=True))


def fine_prepare_kernel(
    place_ref, own_hbm, cot_hbm, w_hbm, out_w_hbm,
    own_ref, w_ref, out_w_ref, q_ref, k_ref, v_ref, qf_ref, kf_ref, bias_ref, cg_ref,
    cot, copied,
):
    anchor = place_ref[0]
    column_at = place_ref[1]
    low = low_lanes()
    copies = [
        pltpu.make_async_copy(source, target, copied.at[at])
        for at, (source, target) in enumerate(
            ((own_hbm, own_ref), (cot_hbm, cot), (w_hbm, w_ref), (out_w_hbm, out_w_ref))
        )
    ]
    for copy in copies:
        copy.start()

    row = lax.broadcasted_iota(jnp.int32, (2 * QUERIES, ALL_KEYS), 0)
    query_pos = jnp.where(row < QUERIES, row, row - QUERIES) - EXTRA
    column = lax.broadcasted_iota(jnp.int32, (2 * QUERIES, ALL_KEYS), 1)
    turned = column_at * ROWS
    halo_pos = column - jnp.where(column >= turned, turned + HALO, turned)
    key_pos = jnp.where(
        column < HALO,
        halo_pos,
        jnp.where(column < OWN_KEYS, column - HALO, column - (OWN_KEYS + HALO + EXTRA)),
    )
    gap = query_pos - key_pos
    allowed = (gap >= 0) & (gap < WINDOW) & (anchor + key_pos >= 0)
    bias_ref[...] = jnp.where(allowed, 0.0, NEG)

    copies[0].wait()
    normed = row_norm(own_ref[...].astype(F32))[0].astype(BF)
    copies[1].wait()
    chunk = lax.broadcasted_iota(jnp.int32, (COARSE, ROWS), 0) * POOL
    row = lax.broadcasted_iota(jnp.int32, (COARSE, ROWS), 1)
    member = jnp.where((row >= chunk) & (row < chunk + POOL), 1.0, 0.0).astype(BF)
    cg_ref[...] = plain(member, cot[...])
    copies[2].wait()
    for at in range(0, D, WIDTH):
        here = slice(at, at + WIDTH)
        queries = plain(normed, w_ref[0, :, here])
        keys = plain(normed, w_ref[1, :, here])
        v_ref[:, here] = plain(normed, w_ref[2, :, here]).astype(BF)
        for part in range(0, WIDTH, PAIR):
            inner = slice(part, part + PAIR)
            outer = slice(at + part, at + part + PAIR)
            query, q_factor = pair_norm(queries[:, inner], low)
            key, k_factor = pair_norm(keys[:, inner], low)
            q_ref[:, outer] = query.astype(BF)
            k_ref[:, outer] = key.astype(BF)
            qf_ref[:, outer] = q_factor
            kf_ref[:, outer] = k_factor
    copies[3].wait()


def fine_forward_kernel(
    place_ref, tail_ref, slots_ref, own_ref, w_ref, out_w_ref, own_q_ref, own_k_ref, own_v_ref,
    own_kf_ref, bias, cg_ref,
    k_ref, v_ref, kf_ref, p_ref, att_ref, hid_ref, send_ref,
    normed, acc,
):
    anchor = place_ref[0]
    column_at = place_ref[1]
    low = low_lanes()
    slots = slots_ref.shape[0]
    nearest = lax.rem(column_at + (slots - 1), slots)
    for slot in range(slots):
        at = slot * ROWS
        normed[at : at + ROWS, :] = row_norm(slots_ref[slot].astype(F32))[0].astype(BF)
    normed[HALO:, :] = row_norm(tail_ref[...].astype(F32))[0].astype(BF)
    acc[...] = jnp.zeros_like(acc)
    extra_at = pl.multiple_of(nearest * ROWS + (ROWS - EXTRA), EXTRA)

    def one_step(step, carry):
        first = pl.multiple_of(step * WIDTH, WIDTH)
        here = pl.ds(first, WIDTH)
        extra = plain(normed[pl.ds(extra_at, EXTRA), :], w_ref[0, :, here])
        both = plain(
            normed[...], jnp.concatenate([w_ref[1, :, here], w_ref[2, :, here]], axis=1)
        )
        own_q, own_k, own_v = own_q_ref[:, here], own_k_ref[:, here], own_v_ref[:, here]
        own_kf = own_kf_ref[:, here]
        mixed = []
        for part in range(0, WIDTH, PAIR):
            inner = slice(part, part + PAIR)
            outer = pl.ds(pl.multiple_of(first + part, PAIR), PAIR)
            key, k_factor = pair_norm(both[:, inner], low)
            key = key.astype(BF)
            value = both[:, WIDTH + part : WIDTH + part + PAIR].astype(BF)
            k_ref[:HALO, outer] = key[:HALO]
            k_ref[HALO:, outer] = own_k[:, inner]
            v_ref[:HALO, outer] = value[:HALO]
            v_ref[HALO:, outer] = own_v[:, inner]
            kf_ref[:HALO, outer] = k_factor[:HALO]
            kf_ref[HALO:, outer] = own_kf[:, inner]
            key = jnp.concatenate([key[:HALO], own_k[:, inner], key[HALO:]], axis=0)
            value = jnp.concatenate([value[:HALO], own_v[:, inner], value[HALO:]], axis=0)
            before = pair_norm(extra[:, inner], low)[0].astype(BF).astype(F32)
            scaled = jnp.concatenate([before, own_q[:, inner].astype(F32)], axis=0) * SCALE
            stacked = jnp.concatenate(
                [jnp.where(low, scaled, 0.0), jnp.where(low, 0.0, scaled)], axis=0
            )
            numer = jnp.exp(last_last(stacked.astype(BF), key) + bias[...])
            total = jnp.sum(numer, axis=-1, keepdims=True)
            prob = (numer * (1.0 / jnp.where(total > 0.0, total, 1.0))).astype(BF)
            head = (first + part) // HEAD_DIM
            p_ref[head] = prob[EXTRA:QUERIES, :OWN_KEYS]
            p_ref[head + 1] = prob[QUERIES + EXTRA :, :OWN_KEYS]
            twice = plain(prob, value)
            attended = jnp.where(low, twice[:QUERIES], twice[QUERIES:]).astype(BF)
            att_ref[:, outer] = attended[EXTRA:]
            mixed.append(attended)
        acc[...] += plain(jnp.concatenate(mixed, axis=1), out_w_ref[here, :])
        return carry

    lax.fori_loop(0, D // WIDTH, one_step, 0, unroll=True)
    before = slots_ref[nearest, ROWS - EXTRA :, :].astype(F32) + acc[:EXTRA, :]
    before = jnp.where(anchor > 0, before, 0.0).astype(BF)
    own = (own_ref[...].astype(F32) + acc[EXTRA:, :]).astype(BF)
    hid_ref[...] = own
    chunk = lax.broadcasted_iota(jnp.int32, (COARSE, QUERIES), 0) * POOL
    row = lax.broadcasted_iota(jnp.int32, (COARSE, QUERIES), 1)
    member = jnp.where((row > chunk) & (row <= chunk + POOL), 1.0, 0.0).astype(BF)
    pooled = plain(member, jnp.concatenate([before, own], axis=0)) * (1.0 / POOL)
    message = jnp.concatenate([pooled, cg_ref[...]], axis=0).astype(BF)
    for peer in range(send_ref.shape[0]):
        send_ref[peer] = message


def coarse_prepare_kernel(core_ref, w_ref, back_ref, in_ref, out_ref):
    low = low_lanes()
    second = core_ref[0] > 0
    parts = [w_ref[at].astype(F32) for at in range(3)]
    turned = [pltpu.roll(part, HEAD_DIM, 1) for part in parts]
    query = jnp.where(second, turned[0], parts[0])
    key = jnp.where(second, turned[1], parts[1])
    value = jnp.where(second, parts[2], turned[2])
    in_ref[:, :PAIR] = jnp.where(low, query, 0.0).astype(BF)
    in_ref[:, PAIR:] = jnp.where(low, key, value).astype(BF)
    out_ref[...] = jnp.zeros_like(out_ref)
    out_ref[HEAD_DIM:PAIR, :] = jnp.where(second, back_ref[HEAD_DIM:, :], back_ref[:HEAD_DIM, :])


def coarse_project_kernel(got_ref, in_w_ref, out_w_ref, send_ref, factor_ref):
    low = low_lanes()
    rows = got_ref[...].astype(F32)
    count = rows.shape[0] * COARSE
    pooled = rows[:, :COARSE, :].reshape(count, D)
    coarse_grad = rows[:, COARSE:, :].reshape(count, D)
    normed = row_norm(pooled)[0].astype(BF)
    raw = plain(normed, in_w_ref[...]) + last_last(coarse_grad.astype(BF), out_w_ref[...])
    units, factors = [], []
    for tile in (raw[:, :PAIR], raw[:, PAIR:]):
        unit, factor = pair_norm(tile, low)
        units.append(jnp.where(low, unit, tile))
        factors.append(factor)
    message = jnp.concatenate(units, axis=1).astype(BF)
    factor_ref[...] = jnp.concatenate(factors, axis=1)
    for peer in range(send_ref.shape[0]):
        send_ref[peer] = message


def coarse_attention_kernel(place_ref, got_ref, factor_ref, in_w_ref, out_w_ref, send_ref, own_grad):
    low = low_lanes()
    own_start = pl.multiple_of(place_ref[2], ROWS)
    length = got_ref.shape[0]
    block = 512
    own_left = got_ref[pl.ds(own_start, ROWS), :PAIR]
    own_right = got_ref[pl.ds(own_start, ROWS), PAIR:]
    own_grad[...] = jnp.zeros_like(own_grad)

    def masked_halves(tile):
        wide = tile.astype(F32)
        return (
            jnp.where(low, wide * SCALE, 0.0).astype(BF),
            jnp.where(low, 0.0, wide).astype(BF),
        )

    def lane_partials(values):
        total = values[:, :PAIR]
        for at in range(PAIR, values.shape[1], PAIR):
            total = total + values[:, at : at + PAIR]
        return total

    def one_block(index):
        first = index * block
        query, grad = masked_halves(got_ref[first : first + block, :PAIR])
        stacked = jnp.concatenate([query, grad], axis=0)

        def scored(keys):
            both = last_last(stacked, keys)
            return jnp.exp(both[:block]), both[block:]

        query_at = lax.broadcasted_iota(jnp.int32, (block, 1), 0)
        total = product = None
        for at in range(index + 1):
            numer, prob_grad = scored(got_ref[at * block : (at + 1) * block, PAIR:])
            if at == index:
                key_at = lax.broadcasted_iota(jnp.int32, (1, block), 1)
                numer = jnp.where(key_at <= query_at, numer, 0.0)
            sums = lane_partials(numer), lane_partials(numer * prob_grad)
            total, product = sums if at == 0 else (total + sums[0], product + sums[1])
        inverse = 1.0 / jnp.sum(total, axis=-1, keepdims=True)
        delta = jnp.sum(product, axis=-1, keepdims=True) * inverse
        own_pos = own_start + lax.broadcasted_iota(jnp.int32, (1, ROWS), 1)
        numer, prob_grad = scored(own_right)
        numer = jnp.where(own_pos <= query_at + first, numer, 0.0)
        prob = numer * inverse
        score_grad = (prob * (prob_grad - delta)).astype(BF)
        own_grad[...] += first_first(
            jnp.concatenate([score_grad, prob.astype(BF)], axis=0), stacked
        )

    for index in range(length // block):
        pl.when(own_start < (index + 1) * block)(lambda index=index: one_block(index))

    query, grad = masked_halves(own_left)
    stacked = jnp.concatenate([query, grad], axis=0)
    query_pos = own_start + lax.broadcasted_iota(jnp.int32, (ROWS, 1), 0)

    def own_chunk(at):
        key_start = pl.multiple_of(at * block, block)
        keys = got_ref[pl.ds(key_start, block), PAIR:]
        both = last_last(stacked, keys)
        key_pos = key_start + lax.broadcasted_iota(jnp.int32, (1, block), 1)
        return keys, jnp.where(key_pos <= query_pos, jnp.exp(both[:ROWS]), 0.0), both[ROWS:]

    def own_sums(at, sums):
        numer, prob_grad = own_chunk(at)[1:]
        return sums[0] + lane_partials(numer), sums[1] + lane_partials(numer * prob_grad)

    nothing = jnp.zeros((ROWS, PAIR), F32)
    chunks = own_start // block + 1
    total, product = lax.fori_loop(0, chunks, own_sums, (nothing, nothing))
    inverse = 1.0 / jnp.sum(total, axis=-1, keepdims=True)
    delta = jnp.sum(product, axis=-1, keepdims=True) * inverse

    def own_results(at, mine):
        keys, numer, prob_grad = own_chunk(at)
        key_scaled, value = masked_halves(keys)
        prob = numer * inverse
        score_grad = (prob * (prob_grad - delta)).astype(BF)
        return mine + plain(score_grad, key_scaled) + plain(prob.astype(BF), value)

    mine = lax.fori_loop(0, chunks, own_results, nothing)

    parts = []
    for tile, unit, factor in (
        (mine, own_left, factor_ref[:, :PAIR]),
        (own_grad[...], own_right, factor_ref[:, PAIR:]),
    ):
        back = pair_norm_back(tile, unit.astype(F32), factor, low)
        parts.append(jnp.where(low, back, tile))
    parts = jnp.concatenate(parts, axis=1).astype(BF)
    peers = send_ref.shape[0]
    normed_grad = last_last(parts, in_w_ref[...]).reshape(peers, COARSE, D)
    mixed = plain(parts, out_w_ref[...]).reshape(peers, COARSE, D)
    send_ref[...] = jnp.concatenate([normed_grad, mixed], axis=1).astype(BF)


def coarse_finish_kernel(got_ref, message_ref, cg_ref, spread_ref, first_ref, state_ref):
    summed = jnp.sum(got_ref[...].astype(F32), axis=0)
    pooled = message_ref[0].astype(F32)[:COARSE]
    normed, factor = row_norm(pooled)
    pooled_grad = cg_ref[...] + row_norm_back(summed[:COARSE], normed, factor)
    spread = pooled_grad * (1.0 / POOL)
    spread_ref[...] = spread
    first_ref[...] = spread[:1]
    state_ref[...] = pooled + summed[COARSE:]


def fine_backward_kernel(
    place_ref, cot_ref, spread_ref, next_ref, out_w_ref, w_ref, q_ref, k_ref, v_ref, qf_ref, kf_ref, p_ref,
    att_ref,
    back1, back2, back3, back4, own_ref, hg_ref, hidden_grad, acc,
):
    low = low_lanes()
    block = (lax.broadcasted_iota(jnp.int32, (ROWS, 1), 0) + (POOL - 1)) // POOL
    added = jnp.zeros((ROWS, D), F32)
    for at in range(COARSE):
        added = jnp.where(block == at, spread_ref[at : at + 1, :], added)
    added = jnp.where(block == COARSE, next_ref[0:1, :], added)
    total = cot_ref[...].astype(F32) + added
    hg_ref[...] = total
    hidden_grad[...] = total.astype(BF)
    acc[...] = jnp.zeros_like(acc)

    def one_step(step, carry):
        first = pl.multiple_of(step * WIDTH, WIDTH)
        here = pl.ds(first, WIDTH)
        att_grads = last_last(hidden_grad[...], out_w_ref[here, :]).astype(BF).astype(F32)
        query_grads, key_grads, value_grads = [], [], []
        for part in range(0, WIDTH, PAIR):
            outer = pl.ds(pl.multiple_of(first + part, PAIR), PAIR)
            att_grad = att_grads[:, part : part + PAIR]
            delta_all = att_grad * att_ref[:, outer].astype(F32)
            value = v_ref[:, outer]
            key_wide = k_ref[:, outer].astype(F32)
            query_wide = q_ref[:, outer].astype(F32)
            grad = jnp.concatenate(
                [jnp.where(low, att_grad, 0.0), jnp.where(low, 0.0, att_grad)], axis=0
            ).astype(BF)
            delta = jnp.sum(
                jnp.concatenate(
                    [jnp.where(low, delta_all, 0.0), jnp.where(low, 0.0, delta_all)], axis=0
                ),
                axis=-1,
                keepdims=True,
            )
            scaled = query_wide * SCALE
            query = jnp.concatenate(
                [jnp.where(low, scaled, 0.0), jnp.where(low, 0.0, scaled)], axis=0
            ).astype(BF)
            head = (first + part) // HEAD_DIM
            prob = p_ref[pl.ds(head, 2)].reshape(2 * ROWS, OWN_KEYS)
            score_grad = (prob.astype(F32) * (last_last(grad, value) - delta)).astype(BF)
            twice = plain(score_grad, (key_wide * SCALE).astype(BF))
            query_grad = jnp.where(low, twice[:ROWS], twice[ROWS:])
            key_grad = first_first(score_grad, query)
            value_grad = first_first(prob, grad)
            query_grads.append(pair_norm_back(query_grad, query_wide, qf_ref[:, outer], low).astype(BF))
            key_grads.append(pair_norm_back(key_grad, key_wide, kf_ref[:, outer], low).astype(BF))
            value_grads.append(value_grad.astype(BF))
        both = jnp.concatenate(key_grads + value_grads, axis=1)
        acc[...] += last_last(
            both, jnp.concatenate([w_ref[1, :, here], w_ref[2, :, here]], axis=1)
        )
        acc[HALO:, :] += last_last(jnp.concatenate(query_grads, axis=1), w_ref[0, :, here])
        return carry

    lax.fori_loop(0, D // WIDTH, one_step, 0, unroll=True)
    backs = (back1, back2, back3, back4)
    for distance, ref in enumerate(backs, 1):
        slot = lax.rem(place_ref[1] + (len(backs) - distance), len(backs))
        ref[...] = acc[pl.ds(pl.multiple_of(slot * ROWS, ROWS), ROWS), :].astype(BF)
    own_ref[...] = acc[HALO:, :]


def halo_send_kernel(place_ref, own_ref, before_ref, send_ref):
    send_ref[0] = jnp.where(place_ref[1] < pl.program_id(0), own_ref[...], before_ref[...])


def repeated_kernel(block_ref, send_ref):
    for peer in range(send_ref.shape[0]):
        send_ref[peer] = block_ref[...]


def fine_finish_kernel(own_ref, a1, a2, a3, a4, hg_ref, tokens_ref, out_ref):
    total = own_ref[...]
    for ref in (a1, a2, a3, a4):
        total = total + ref[...].astype(F32)
    normed, factor = row_norm(tokens_ref[...].astype(F32))
    out_ref[...] = (hg_ref[...] + row_norm_back(total, normed, factor)).astype(BF)


def whole(shape):
    return pl.BlockSpec(shape, lambda *_: (0,) * len(shape))


def columns(rows, width):
    return pl.BlockSpec((rows, width), lambda p: (0, p))


def shaped(shape, kind):
    return jax.ShapeDtypeStruct(shape, kind)


def params(mib):
    return pltpu.CompilerParams(vmem_limit_bytes=mib << 20)


def cost(flops, moved, exps=0):
    return pl.CostEstimate(flops=flops, bytes_accessed=moved, transcendentals=exps)


SCALAR = pl.BlockSpec(memory_space=pltpu.SMEM)
IN_VMEM = pl.BlockSpec(memory_space=pltpu.VMEM)
WIDTH = 4 * PAIR


def in_hbm(x):
    return pltpu.with_memory_space_constraint(x, pltpu.HBM)


def fine_prepare(place, tokens, cotangent, weights, fine_out):
    anywhere = pl.BlockSpec(memory_space=pltpu.HBM)
    return pl.pallas_call(
        fine_prepare_kernel,
        in_specs=[SCALAR] + [anywhere] * 4,
        out_specs=[IN_VMEM] * 10,
        out_shape=[
            pltpu.VMEM((ROWS, D), BF),
            pltpu.VMEM((3, D, D), BF),
            pltpu.VMEM((D, D), BF),
            pltpu.VMEM((ROWS, D), BF),
            pltpu.VMEM((ROWS, D), BF),
            pltpu.VMEM((ROWS, D), BF),
            pltpu.VMEM((ROWS, D), F32),
            pltpu.VMEM((ROWS, D), F32),
            pltpu.VMEM((2 * QUERIES, ALL_KEYS), F32),
            pltpu.VMEM((COARSE, D), F32),
        ],
        scratch_shapes=[pltpu.VMEM((ROWS, D), BF), pltpu.SemaphoreType.DMA((4,))],
        compiler_params=params(16),
        cost_estimate=cost(900_000_000, 17_000_000),
        name="fine_prepare",
    )(place, *(in_hbm(x) for x in (tokens, cotangent, weights, fine_out)))


def fine_forward(place, tail, slots, own, weights, fine_out, own_q, own_k, own_v, own_kf, bias, cg, peers):
    return pl.pallas_call(
        fine_forward_kernel,
        in_specs=[SCALAR] + [IN_VMEM] * 11,
        out_specs=[IN_VMEM] * 7,
        out_shape=[
            pltpu.VMEM((OWN_KEYS, D), BF),
            pltpu.VMEM((OWN_KEYS, D), BF),
            pltpu.VMEM((OWN_KEYS, D), F32),
            pltpu.VMEM((HEADS, ROWS, OWN_KEYS), BF),
            pltpu.VMEM((ROWS, D), BF),
            shaped((ROWS, D), BF),
            shaped((peers, 2 * COARSE, D), BF),
        ],
        scratch_shapes=[pltpu.VMEM((HALO + EXTRA, D), BF), pltpu.VMEM((QUERIES, D), F32)],
        compiler_params=params(16),
        cost_estimate=cost(4_500_000_000, 20_000_000, 1_600_000),
        name="fine_forward",
    )(place, tail, slots, own, weights, fine_out, own_q, own_k, own_v, own_kf, bias, cg)


def coarse_prepare(core, weights, back):
    return pl.pallas_call(
        coarse_prepare_kernel,
        in_specs=[SCALAR, IN_VMEM, IN_VMEM],
        out_specs=[IN_VMEM] * 2,
        out_shape=[shaped((D, 2 * PAIR), BF), shaped((2 * PAIR, D), BF)],
        compiler_params=params(8),
        cost_estimate=cost(1_000_000, 2_500_000),
        name="coarse_prepare",
    )(core, weights, back)


def coarse_project(gathered, coarse_in, coarse_back, groups):
    rows = gathered.shape[0] * COARSE
    return pl.pallas_call(
        coarse_project_kernel,
        out_shape=[shaped((groups, rows, 2 * PAIR), BF), shaped((rows, 2 * PAIR), F32)],
        compiler_params=params(VMEM_MIB),
        cost_estimate=cost(140_000_000, 3_000_000),
        name="coarse_project",
    )(gathered, coarse_in, coarse_back)


def coarse_attention(place, everyone, factor, coarse_in, coarse_back):
    rows = factor.shape[0]
    return pl.pallas_call(
        coarse_attention_kernel,
        in_specs=[SCALAR] + [IN_VMEM] * 4,
        out_shape=shaped((rows // COARSE, 2 * COARSE, D), BF),
        scratch_shapes=[pltpu.VMEM((rows, PAIR), F32)],
        compiler_params=params(VMEM_MIB),
        cost_estimate=cost(1_500_000_000, 3_000_000, 3_000_000),
        name="coarse_attention",
    )(place, everyone, factor, coarse_in, coarse_back)


def coarse_finish(returned, message, coarse_grad):
    return pl.pallas_call(
        coarse_finish_kernel,
        grid=(1,),
        in_specs=[whole(returned.shape), whole((1, 2 * COARSE, D)), whole((COARSE, D))],
        out_specs=[whole((COARSE, D)), whole((1, D)), whole((COARSE, D))],
        out_shape=[shaped((COARSE, D), F32), shaped((1, D), F32), shaped((COARSE, D), F32)],
        compiler_params=params(VMEM_MIB),
        cost_estimate=cost(1_000_000, 1_000_000),
        name="coarse_finish",
    )(returned, message, coarse_grad)


def fine_backward(
    place, cotangent, spread, after, fine_out, weights, query, key, value, q_factor, k_factor, probs,
    attended,
):
    return pl.pallas_call(
        fine_backward_kernel,
        in_specs=[SCALAR] + [IN_VMEM] * 12,
        out_specs=[IN_VMEM] * 6,
        out_shape=[shaped((ROWS, D), BF)] * 4 + [shaped((ROWS, D), F32)] * 2,
        scratch_shapes=[pltpu.VMEM((ROWS, D), BF), pltpu.VMEM((OWN_KEYS, D), F32)],
        compiler_params=params(16),
        cost_estimate=cost(5_000_000_000, 20_000_000),
        name="fine_backward",
    )(
        place, cotangent, spread, after, fine_out, weights, query, key, value, q_factor, k_factor, probs,
        attended,
    )


def halo_send(place, own, before, count):
    return pl.pallas_call(
        halo_send_kernel,
        grid=(count,),
        in_specs=[SCALAR, whole((ROWS, D)), whole((ROWS, D))],
        out_specs=pl.BlockSpec((1, ROWS, D), lambda p: (p, 0, 0)),
        out_shape=shaped((count, ROWS, D), BF),
        compiler_params=params(8),
        cost_estimate=cost(1_000_000, 1_500_000),
        name="halo_send",
    )(place, own, before)


def repeated(block, count):
    return pl.pallas_call(
        repeated_kernel,
        out_shape=shaped((count, *block.shape), BF),
        compiler_params=params(VMEM_MIB),
        cost_estimate=cost(1_000_000, 1_300_000),
        name="repeated",
    )(block)


def fine_finish(own, arrived, hidden_grad, tokens):
    return pl.pallas_call(
        fine_finish_kernel,
        out_shape=shaped((ROWS, D), BF),
        compiler_params=params(VMEM_MIB),
        cost_estimate=cost(1_000_000, 3_000_000),
        name="fine_finish",
    )(own, *arrived, hidden_grad, tokens)


def per_device(tokens, cotangent, fine_qkv, fine_out, coarse_qkv, coarse_out):
    peers = 1
    for name in GROUP:
        peers *= lax.axis_size(name)
    groups = 1
    for name in FAR:
        groups *= lax.axis_size(name)
    weights = jnp.transpose(fine_qkv, (1, 0, 2))
    core = lax.axis_index("core").astype(jnp.int32).reshape(1)
    column_at = lax.axis_index("x")
    columns_along = lax.axis_size("x")
    tail = shifted_by(tokens[ROWS - EXTRA :], columns_along + 1)
    row_before = shifted_by(tokens, columns_along)
    group_start = lax.axis_index(FAR) * (peers * COARSE)
    place = jnp.stack([lax.axis_index(LINE) * ROWS, column_at, group_start]).astype(jnp.int32)
    prepared = fine_prepare(place, tokens, cotangent, weights, fine_out)
    coarse_weights = coarse_prepare(core, jnp.transpose(coarse_qkv, (1, 0, 2)), coarse_out)
    tail, row_before, prepared, coarse_weights, place = lax.optimization_barrier(
        (tail, row_before, prepared, coarse_weights, place)
    )
    own, weights, fine_out, query, own_key, own_value, q_factor, own_k_factor, bias, coarse_grad = prepared
    coarse_in, coarse_back = coarse_weights
    slots = exchanged(halo_send(place, own, row_before, columns_along), "x")
    key, value, k_factor, probs, attended, hidden, message = fine_forward(
        place, tail, slots, own, weights, fine_out, query, own_key, own_value, own_k_factor, bias,
        coarse_grad, peers,
    )
    gathered = exchanged(message, GROUP)
    near, further = lax.axis_size("z_hi"), lax.axis_size("y")
    coarse_send, coarse_factor = coarse_project(gathered, coarse_in, coarse_back, near)
    group_rows = coarse_factor.shape[0]
    nearby = exchanged(coarse_send, "z_hi").reshape(near * group_rows, 2 * PAIR)
    everyone = exchanged(repeated(nearby, further), "y").reshape(groups * group_rows, 2 * PAIR)
    partial = coarse_attention(place, everyone, coarse_factor, coarse_in, coarse_back)
    returned = exchanged(partial, GROUP)
    spread, first, state = coarse_finish(returned, message, coarse_grad)
    after = shifted_by(first, -1)
    output = (
        hidden.astype(F32) + jnp.repeat(state.astype(BF), POOL, axis=0).astype(F32)
    ).astype(BF)
    *backs, own_grad, hidden_grad = fine_backward(
        place, cotangent, spread, after, fine_out, weights, query, key, value, q_factor, k_factor, probs,
        attended,
    )
    arrived = [shifted_by(rows, -steps) for steps, rows in enumerate(backs, 1)]
    return (output, fine_finish(own_grad, arrived, hidden_grad, own))


def solution(mesh):
    sizes = (4, 4, 2, 2, 4)
    fine_mesh = Mesh(mesh.devices.reshape(sizes), LINE)
    placed = (
        P(LINE, None),
        P(LINE, None),
        P(),
        P(),
        P(None, None, ("z_lo", "x")),
        P(("z_lo", "x"), None),
    )
    return jax.shard_map(
        per_device,
        mesh=fine_mesh,
        in_specs=placed,
        out_specs=(P(LINE, None), P(LINE, None)),
        check_vma=False,
    )
```

```python
import jax
import jax.numpy as jnp
from jax import lax
from jax.experimental import pallas as pl
from jax.experimental.pallas import tpu as pltpu
from jax.sharding import Mesh
from jax.sharding import PartitionSpec as P

D = 1024
HEADS = 16
HEAD_DIM = 64
WINDOW = 512
POOL = 16
EPS = 1e-06

LINE = ("y", "z_hi", "core", "z_lo", "x")
GROUP = ("core", "z_lo", "x")
FAR = ("y", "z_hi")

ROWS = 128
HALO = WINDOW
OWN_KEYS = HALO + ROWS
EXTRA = 16
ALL_KEYS = OWN_KEYS + EXTRA
QUERIES = EXTRA + ROWS
PAIR = 2 * HEAD_DIM
COARSE = ROWS // POOL
SCALE = HEAD_DIM ** (-0.5)
NEG = -1e30
VMEM_MIB = 16

BF = jnp.bfloat16
F32 = jnp.float32


def shifted_by(value, steps):
    count = 1
    for name in LINE:
        count *= lax.axis_size(name)
    first, last = (max(0, -steps), min(count, count - steps))
    return lax.ppermute(value, LINE, [(source, source + steps) for source in range(first, last)])


def exchanged(pieces, axes):
    return lax.all_to_all(pieces, axes, 0, 0, tiled=True)


def last_last(left, right):
    return lax.dot_general(left, right, (((1,), (1,)), ((), ())), preferred_element_type=F32)


def first_first(left, right):
    return lax.dot_general(left, right, (((0,), (0,)), ((), ())), preferred_element_type=F32)


def plain(left, right):
    return jnp.dot(left, right, preferred_element_type=F32)


def low_lanes():
    return lax.broadcasted_iota(jnp.int32, (1, PAIR), 1) < HEAD_DIM


def pair_sums(values, low):
    low_sum = jnp.sum(jnp.where(low, values, 0.0), axis=-1, keepdims=True)
    high_sum = jnp.sum(jnp.where(low, 0.0, values), axis=-1, keepdims=True)
    return jnp.where(low, low_sum, high_sum)


def pair_norm(values, low):
    factor = lax.rsqrt(pair_sums(values * values, low) * (1.0 / HEAD_DIM) + EPS)
    return values * factor, factor


def pair_norm_back(grad, unit, factor, low):
    return factor * (grad - unit * (pair_sums(unit * grad, low) * (1.0 / HEAD_DIM)))


def row_norm(rows):
    factor = lax.rsqrt(jnp.mean(rows * rows, axis=-1, keepdims=True) + EPS)
    return rows * factor, factor


def row_norm_back(grad, normed, factor):
    return factor * (grad - normed * jnp.mean(normed * grad, axis=-1, keepdims=True))


def fine_prepare_kernel(
    place_ref, own_hbm, cot_hbm, w_hbm, out_w_hbm,
    own_ref, w_ref, out_w_ref, q_ref, k_ref, v_ref, qf_ref, kf_ref, bias_ref, cg_ref,
    cot, copied,
):
    anchor = place_ref[0]
    column_at = place_ref[1]
    low = low_lanes()
    copies = [
        pltpu.make_async_copy(source, target, copied.at[at])
        for at, (source, target) in enumerate(
            ((own_hbm, own_ref), (cot_hbm, cot), (w_hbm, w_ref), (out_w_hbm, out_w_ref))
        )
    ]
    for copy in copies:
        copy.start()

    row = lax.broadcasted_iota(jnp.int32, (2 * QUERIES, ALL_KEYS), 0)
    query_pos = jnp.where(row < QUERIES, row, row - QUERIES) - EXTRA
    column = lax.broadcasted_iota(jnp.int32, (2 * QUERIES, ALL_KEYS), 1)
    turned = column_at * ROWS
    halo_pos = column - jnp.where(column >= turned, turned + HALO, turned)
    key_pos = jnp.where(
        column < HALO,
        halo_pos,
        jnp.where(column < OWN_KEYS, column - HALO, column - (OWN_KEYS + HALO + EXTRA)),
    )
    gap = query_pos - key_pos
    allowed = (gap >= 0) & (gap < WINDOW) & (anchor + key_pos >= 0)
    bias_ref[...] = jnp.where(allowed, 0.0, NEG)

    copies[0].wait()
    normed = row_norm(own_ref[...].astype(F32))[0].astype(BF)
    copies[1].wait()
    chunk = lax.broadcasted_iota(jnp.int32, (COARSE, ROWS), 0) * POOL
    row = lax.broadcasted_iota(jnp.int32, (COARSE, ROWS), 1)
    member = jnp.where((row >= chunk) & (row < chunk + POOL), 1.0, 0.0).astype(BF)
    cg_ref[...] = plain(member, cot[...])
    copies[2].wait()
    for at in range(0, D, WIDTH):
        here = slice(at, at + WIDTH)
        queries = plain(normed, w_ref[0, :, here])
        keys = plain(normed, w_ref[1, :, here])
        v_ref[:, here] = plain(normed, w_ref[2, :, here]).astype(BF)
        for part in range(0, WIDTH, PAIR):
            inner = slice(part, part + PAIR)
            outer = slice(at + part, at + part + PAIR)
            query, q_factor = pair_norm(queries[:, inner], low)
            key, k_factor = pair_norm(keys[:, inner], low)
            q_ref[:, outer] = query.astype(BF)
            k_ref[:, outer] = key.astype(BF)
            qf_ref[:, outer] = q_factor
            kf_ref[:, outer] = k_factor
    copies[3].wait()


def fine_forward_kernel(
    place_ref, tail_ref, slots_ref, own_ref, w_ref, out_w_ref, own_q_ref, own_k_ref, own_v_ref,
    own_qf_ref, own_kf_ref, bias, cg_ref,
    q_ref, k_ref, v_ref, qf_ref, kf_ref, p_ref, att_ref, hid_ref, send_ref,
    normed, acc,
):
    anchor = place_ref[0]
    column_at = place_ref[1]
    low = low_lanes()
    slots = slots_ref.shape[0]
    nearest = lax.rem(column_at + (slots - 1), slots)
    for slot in range(slots):
        at = slot * ROWS
        normed[at : at + ROWS, :] = row_norm(slots_ref[slot].astype(F32))[0].astype(BF)
    normed[HALO:, :] = row_norm(tail_ref[...].astype(F32))[0].astype(BF)
    acc[...] = jnp.zeros_like(acc)
    extra_at = pl.multiple_of(nearest * ROWS + (ROWS - EXTRA), EXTRA)

    def one_step(step, carry):
        first = pl.multiple_of(step * WIDTH, WIDTH)
        here = pl.ds(first, WIDTH)
        extra = plain(normed[pl.ds(extra_at, EXTRA), :], w_ref[0, :, here])
        both = plain(
            normed[...], jnp.concatenate([w_ref[1, :, here], w_ref[2, :, here]], axis=1)
        )
        own_q, own_k, own_v = own_q_ref[:, here], own_k_ref[:, here], own_v_ref[:, here]
        own_kf = own_kf_ref[:, here]
        mixed = []
        for part in range(0, WIDTH, PAIR):
            inner = slice(part, part + PAIR)
            outer = pl.ds(pl.multiple_of(first + part, PAIR), PAIR)
            key, k_factor = pair_norm(both[:, inner], low)
            key = key.astype(BF)
            value = both[:, WIDTH + part : WIDTH + part + PAIR].astype(BF)
            key = jnp.concatenate([key[:HALO], own_k[:, inner], key[HALO:]], axis=0)
            value = jnp.concatenate([value[:HALO], own_v[:, inner], value[HALO:]], axis=0)
            k_ref[:, outer] = key
            v_ref[:, outer] = value
            kf_ref[:HALO, outer] = k_factor[:HALO]
            kf_ref[HALO:OWN_KEYS, outer] = own_kf[:, inner]
            kf_ref[OWN_KEYS:, outer] = k_factor[HALO:]
            before, before_factor = pair_norm(extra[:, inner], low)
            query = jnp.concatenate([before.astype(BF), own_q[:, inner]], axis=0)
            q_ref[:, outer] = query
            qf_ref[:EXTRA, outer] = before_factor
            qf_ref[EXTRA:, outer] = own_qf_ref[:, outer]
            scaled = query.astype(F32) * SCALE
            stacked = jnp.concatenate(
                [jnp.where(low, scaled, 0.0), jnp.where(low, 0.0, scaled)], axis=0
            )
            numer = jnp.exp(last_last(stacked.astype(BF), key) + bias[...])
            total = jnp.sum(numer, axis=-1, keepdims=True)
            prob = (numer * (1.0 / jnp.where(total > 0.0, total, 1.0))).astype(BF)
            head = (first + part) // HEAD_DIM
            p_ref[head] = prob[:QUERIES]
            p_ref[head + 1] = prob[QUERIES:]
            twice = plain(prob, value)
            attended = jnp.where(low, twice[:QUERIES], twice[QUERIES:]).astype(BF)
            att_ref[:, outer] = attended
            mixed.append(attended)
        acc[...] += plain(jnp.concatenate(mixed, axis=1), out_w_ref[here, :])
        return carry

    lax.fori_loop(0, D // WIDTH, one_step, 0, unroll=True)
    before = slots_ref[nearest, ROWS - EXTRA :, :].astype(F32) + acc[:EXTRA, :]
    before = jnp.where(anchor > 0, before, 0.0).astype(BF)
    own = (own_ref[...].astype(F32) + acc[EXTRA:, :]).astype(BF)
    hid_ref[...] = own
    chunk = lax.broadcasted_iota(jnp.int32, (COARSE, QUERIES), 0) * POOL
    row = lax.broadcasted_iota(jnp.int32, (COARSE, QUERIES), 1)
    member = jnp.where((row > chunk) & (row <= chunk + POOL), 1.0, 0.0).astype(BF)
    pooled = plain(member, jnp.concatenate([before, own], axis=0)) * (1.0 / POOL)
    message = jnp.concatenate([pooled, cg_ref[...]], axis=0).astype(BF)
    for peer in range(send_ref.shape[0]):
        send_ref[peer] = message


def coarse_prepare_kernel(core_ref, w_ref, back_ref, in_ref, out_ref):
    low = low_lanes()
    second = core_ref[0] > 0
    parts = [w_ref[at].astype(F32) for at in range(3)]
    turned = [pltpu.roll(part, HEAD_DIM, 1) for part in parts]
    query = jnp.where(second, turned[0], parts[0])
    key = jnp.where(second, turned[1], parts[1])
    value = jnp.where(second, parts[2], turned[2])
    in_ref[:, :PAIR] = jnp.where(low, query, 0.0).astype(BF)
    in_ref[:, PAIR:] = jnp.where(low, key, value).astype(BF)
    out_ref[...] = jnp.zeros_like(out_ref)
    out_ref[HEAD_DIM:PAIR, :] = jnp.where(second, back_ref[HEAD_DIM:, :], back_ref[:HEAD_DIM, :])


def coarse_project_kernel(got_ref, in_w_ref, out_w_ref, send_ref, factor_ref):
    low = low_lanes()
    rows = got_ref[...].astype(F32)
    count = rows.shape[0] * COARSE
    pooled = rows[:, :COARSE, :].reshape(count, D)
    coarse_grad = rows[:, COARSE:, :].reshape(count, D)
    normed = row_norm(pooled)[0].astype(BF)
    raw = plain(normed, in_w_ref[...]) + last_last(coarse_grad.astype(BF), out_w_ref[...])
    units, factors = [], []
    for tile in (raw[:, :PAIR], raw[:, PAIR:]):
        unit, factor = pair_norm(tile, low)
        units.append(jnp.where(low, unit, tile))
        factors.append(factor)
    message = jnp.concatenate(units, axis=1).astype(BF)
    factor_ref[...] = jnp.concatenate(factors, axis=1)
    for peer in range(send_ref.shape[0]):
        send_ref[peer] = message


def coarse_attention_kernel(place_ref, got_ref, factor_ref, in_w_ref, out_w_ref, send_ref, own_grad):
    low = low_lanes()
    own_start = pl.multiple_of(place_ref[2], ROWS)
    length = got_ref.shape[0]
    block = 512
    own_left = got_ref[pl.ds(own_start, ROWS), :PAIR]
    own_right = got_ref[pl.ds(own_start, ROWS), PAIR:]
    own_grad[...] = jnp.zeros_like(own_grad)

    def masked_halves(tile):
        wide = tile.astype(F32)
        return (
            jnp.where(low, wide * SCALE, 0.0).astype(BF),
            jnp.where(low, 0.0, wide).astype(BF),
        )

    def lane_partials(values):
        total = values[:, :PAIR]
        for at in range(PAIR, values.shape[1], PAIR):
            total = total + values[:, at : at + PAIR]
        return total

    def one_block(index):
        first = index * block
        query, grad = masked_halves(got_ref[first : first + block, :PAIR])
        stacked = jnp.concatenate([query, grad], axis=0)

        def scored(keys):
            both = last_last(stacked, keys)
            return jnp.exp(both[:block]), both[block:]

        query_at = lax.broadcasted_iota(jnp.int32, (block, 1), 0)
        total = product = None
        for at in range(index + 1):
            numer, prob_grad = scored(got_ref[at * block : (at + 1) * block, PAIR:])
            if at == index:
                key_at = lax.broadcasted_iota(jnp.int32, (1, block), 1)
                numer = jnp.where(key_at <= query_at, numer, 0.0)
            sums = lane_partials(numer), lane_partials(numer * prob_grad)
            total, product = sums if at == 0 else (total + sums[0], product + sums[1])
        inverse = 1.0 / jnp.sum(total, axis=-1, keepdims=True)
        delta = jnp.sum(product, axis=-1, keepdims=True) * inverse
        own_pos = own_start + lax.broadcasted_iota(jnp.int32, (1, ROWS), 1)
        numer, prob_grad = scored(own_right)
        numer = jnp.where(own_pos <= query_at + first, numer, 0.0)
        prob = numer * inverse
        score_grad = (prob * (prob_grad - delta)).astype(BF)
        own_grad[...] += first_first(
            jnp.concatenate([score_grad, prob.astype(BF)], axis=0), stacked
        )

    for index in range(length // block):
        pl.when(own_start < (index + 1) * block)(lambda index=index: one_block(index))

    query, grad = masked_halves(own_left)
    stacked = jnp.concatenate([query, grad], axis=0)
    query_pos = own_start + lax.broadcasted_iota(jnp.int32, (ROWS, 1), 0)

    def own_chunk(at):
        key_start = pl.multiple_of(at * block, block)
        keys = got_ref[pl.ds(key_start, block), PAIR:]
        both = last_last(stacked, keys)
        key_pos = key_start + lax.broadcasted_iota(jnp.int32, (1, block), 1)
        return keys, jnp.where(key_pos <= query_pos, jnp.exp(both[:ROWS]), 0.0), both[ROWS:]

    def own_sums(at, sums):
        numer, prob_grad = own_chunk(at)[1:]
        return sums[0] + lane_partials(numer), sums[1] + lane_partials(numer * prob_grad)

    nothing = jnp.zeros((ROWS, PAIR), F32)
    chunks = own_start // block + 1
    total, product = lax.fori_loop(0, chunks, own_sums, (nothing, nothing))
    inverse = 1.0 / jnp.sum(total, axis=-1, keepdims=True)
    delta = jnp.sum(product, axis=-1, keepdims=True) * inverse

    def own_results(at, mine):
        keys, numer, prob_grad = own_chunk(at)
        key_scaled, value = masked_halves(keys)
        prob = numer * inverse
        score_grad = (prob * (prob_grad - delta)).astype(BF)
        return mine + plain(score_grad, key_scaled) + plain(prob.astype(BF), value)

    mine = lax.fori_loop(0, chunks, own_results, nothing)

    parts = []
    for tile, unit, factor in (
        (mine, own_left, factor_ref[:, :PAIR]),
        (own_grad[...], own_right, factor_ref[:, PAIR:]),
    ):
        back = pair_norm_back(tile, unit.astype(F32), factor, low)
        parts.append(jnp.where(low, back, tile))
    parts = jnp.concatenate(parts, axis=1).astype(BF)
    peers = send_ref.shape[0]
    normed_grad = last_last(parts, in_w_ref[...]).reshape(peers, COARSE, D)
    mixed = plain(parts, out_w_ref[...]).reshape(peers, COARSE, D)
    send_ref[...] = jnp.concatenate([normed_grad, mixed], axis=1).astype(BF)


def coarse_finish_kernel(got_ref, message_ref, cg_ref, spread_ref, first_ref, state_ref):
    summed = jnp.sum(got_ref[...].astype(F32), axis=0)
    pooled = message_ref[0].astype(F32)[:COARSE]
    normed, factor = row_norm(pooled)
    pooled_grad = cg_ref[...] + row_norm_back(summed[:COARSE], normed, factor)
    spread = pooled_grad * (1.0 / POOL)
    spread_ref[...] = spread
    first_ref[...] = spread[:1]
    state_ref[...] = pooled + summed[COARSE:]


def fine_backward_kernel(
    place_ref, cot_ref, spread_ref, out_w_ref, w_ref, q_ref, k_ref, v_ref, qf_ref, kf_ref, p_ref,
    att_ref,
    back1, back2, back3, back4, tail_ref, own_ref, hg_ref, hidden_grad, acc,
):
    low = low_lanes()
    block = (lax.broadcasted_iota(jnp.int32, (ROWS, 1), 0) + (POOL - 1)) // POOL
    added = jnp.zeros((ROWS, D), F32)
    for at in range(COARSE):
        added = jnp.where(block == at, spread_ref[at : at + 1, :], added)
    total = cot_ref[...].astype(F32) + added
    hg_ref[...] = total
    counted = lax.broadcasted_iota(jnp.int32, (EXTRA, 1), 0) > EXTRA - POOL
    hidden_grad[:EXTRA, :] = jnp.where(counted, spread_ref[0:1, :], 0.0).astype(BF)
    hidden_grad[EXTRA:, :] = total.astype(BF)
    backs = (back1, back2, back3, back4)
    slots = len(backs)
    nearest = lax.rem(place_ref[1] + (slots - 1), slots)
    extra_at = pl.multiple_of(nearest * ROWS + (ROWS - EXTRA), EXTRA)
    acc[...] = jnp.zeros_like(acc)

    def one_step(step, carry):
        first = pl.multiple_of(step * WIDTH, WIDTH)
        here = pl.ds(first, WIDTH)
        att_grads = last_last(hidden_grad[...], out_w_ref[here, :]).astype(BF).astype(F32)
        query_grads, key_grads, value_grads = [], [], []
        for part in range(0, WIDTH, PAIR):
            outer = pl.ds(pl.multiple_of(first + part, PAIR), PAIR)
            att_grad = att_grads[:, part : part + PAIR]
            delta_all = att_grad * att_ref[:, outer].astype(F32)
            value = v_ref[:, outer]
            key_wide = k_ref[:, outer].astype(F32)
            query_wide = q_ref[:, outer].astype(F32)
            grad = jnp.concatenate(
                [jnp.where(low, att_grad, 0.0), jnp.where(low, 0.0, att_grad)], axis=0
            ).astype(BF)
            delta = jnp.sum(
                jnp.concatenate(
                    [jnp.where(low, delta_all, 0.0), jnp.where(low, 0.0, delta_all)], axis=0
                ),
                axis=-1,
                keepdims=True,
            )
            scaled = query_wide * SCALE
            query = jnp.concatenate(
                [jnp.where(low, scaled, 0.0), jnp.where(low, 0.0, scaled)], axis=0
            ).astype(BF)
            head = (first + part) // HEAD_DIM
            prob = p_ref[pl.ds(head, 2)].reshape(2 * QUERIES, ALL_KEYS)
            score_grad = (prob.astype(F32) * (last_last(grad, value) - delta)).astype(BF)
            twice = plain(score_grad, (key_wide * SCALE).astype(BF))
            query_grad = jnp.where(low, twice[:QUERIES], twice[QUERIES:])
            key_grad = first_first(score_grad, query)
            value_grad = first_first(prob, grad)
            query_grads.append(pair_norm_back(query_grad, query_wide, qf_ref[:, outer], low).astype(BF))
            key_grads.append(pair_norm_back(key_grad, key_wide, kf_ref[:, outer], low).astype(BF))
            value_grads.append(value_grad.astype(BF))
        both = jnp.concatenate(key_grads + value_grads, axis=1)
        acc[...] += last_last(
            both, jnp.concatenate([w_ref[1, :, here], w_ref[2, :, here]], axis=1)
        )
        from_query = last_last(jnp.concatenate(query_grads, axis=1), w_ref[0, :, here])
        acc[pl.ds(extra_at, EXTRA), :] += from_query[:EXTRA]
        acc[HALO:OWN_KEYS, :] += from_query[EXTRA:]
        return carry

    lax.fori_loop(0, D // WIDTH, one_step, 0, unroll=True)
    for distance, ref in enumerate(backs, 1):
        slot = lax.rem(place_ref[1] + (slots - distance), slots)
        ref[...] = acc[pl.ds(pl.multiple_of(slot * ROWS, ROWS), ROWS), :].astype(BF)
    tail_ref[...] = acc[OWN_KEYS:, :].astype(BF)
    own_ref[...] = acc[HALO:OWN_KEYS, :]


def halo_send_kernel(place_ref, own_ref, before_ref, send_ref):
    send_ref[0] = jnp.where(place_ref[1] < pl.program_id(0), own_ref[...], before_ref[...])


def repeated_kernel(block_ref, send_ref):
    for peer in range(send_ref.shape[0]):
        send_ref[peer] = block_ref[...]


def fine_finish_kernel(own_ref, a1, a2, a3, a4, tail_ref, next_ref, hg_ref, tokens_ref, out_ref):
    total = own_ref[...]
    for ref in (a1, a2, a3, a4):
        total = total + ref[...].astype(F32)
    split = ROWS - EXTRA
    total = jnp.concatenate([total[:split], total[split:] + tail_ref[...].astype(F32)], axis=0)
    normed, factor = row_norm(tokens_ref[...].astype(F32))
    after = lax.broadcasted_iota(jnp.int32, (ROWS, 1), 0) > ROWS - POOL
    hidden_grad = hg_ref[...] + jnp.where(after, next_ref[...], 0.0)
    out_ref[...] = (hidden_grad + row_norm_back(total, normed, factor)).astype(BF)


def whole(shape):
    return pl.BlockSpec(shape, lambda *_: (0,) * len(shape))


def columns(rows, width):
    return pl.BlockSpec((rows, width), lambda p: (0, p))


def shaped(shape, kind):
    return jax.ShapeDtypeStruct(shape, kind)


def params(mib):
    return pltpu.CompilerParams(vmem_limit_bytes=mib << 20)


def cost(flops, moved, exps=0):
    return pl.CostEstimate(flops=flops, bytes_accessed=moved, transcendentals=exps)


SCALAR = pl.BlockSpec(memory_space=pltpu.SMEM)
IN_VMEM = pl.BlockSpec(memory_space=pltpu.VMEM)
WIDTH = 4 * PAIR


def in_hbm(x):
    return pltpu.with_memory_space_constraint(x, pltpu.HBM)


def fine_prepare(place, tokens, cotangent, weights, fine_out):
    anywhere = pl.BlockSpec(memory_space=pltpu.HBM)
    return pl.pallas_call(
        fine_prepare_kernel,
        in_specs=[SCALAR] + [anywhere] * 4,
        out_specs=[IN_VMEM] * 10,
        out_shape=[
            pltpu.VMEM((ROWS, D), BF),
            pltpu.VMEM((3, D, D), BF),
            pltpu.VMEM((D, D), BF),
            pltpu.VMEM((ROWS, D), BF),
            pltpu.VMEM((ROWS, D), BF),
            pltpu.VMEM((ROWS, D), BF),
            pltpu.VMEM((ROWS, D), F32),
            pltpu.VMEM((ROWS, D), F32),
            pltpu.VMEM((2 * QUERIES, ALL_KEYS), F32),
            pltpu.VMEM((COARSE, D), F32),
        ],
        scratch_shapes=[pltpu.VMEM((ROWS, D), BF), pltpu.SemaphoreType.DMA((4,))],
        compiler_params=params(16),
        cost_estimate=cost(900_000_000, 17_000_000),
        name="fine_prepare",
    )(place, *(in_hbm(x) for x in (tokens, cotangent, weights, fine_out)))


def fine_forward(place, tail, slots, prepared, peers):
    return pl.pallas_call(
        fine_forward_kernel,
        in_specs=[SCALAR] + [IN_VMEM] * 12,
        out_specs=[IN_VMEM] * 9,
        out_shape=[
            pltpu.VMEM((QUERIES, D), BF),
            pltpu.VMEM((ALL_KEYS, D), BF),
            pltpu.VMEM((ALL_KEYS, D), BF),
            pltpu.VMEM((QUERIES, D), F32),
            pltpu.VMEM((ALL_KEYS, D), F32),
            pltpu.VMEM((HEADS, QUERIES, ALL_KEYS), BF),
            pltpu.VMEM((QUERIES, D), BF),
            shaped((ROWS, D), BF),
            shaped((peers, 2 * COARSE, D), BF),
        ],
        scratch_shapes=[pltpu.VMEM((HALO + EXTRA, D), BF), pltpu.VMEM((QUERIES, D), F32)],
        compiler_params=params(16),
        cost_estimate=cost(4_500_000_000, 20_000_000, 1_600_000),
        name="fine_forward",
    )(place, tail, slots, *prepared)


def coarse_prepare(core, weights, back):
    return pl.pallas_call(
        coarse_prepare_kernel,
        in_specs=[SCALAR, IN_VMEM, IN_VMEM],
        out_specs=[IN_VMEM] * 2,
        out_shape=[shaped((D, 2 * PAIR), BF), shaped((2 * PAIR, D), BF)],
        compiler_params=params(8),
        cost_estimate=cost(1_000_000, 2_500_000),
        name="coarse_prepare",
    )(core, weights, back)


def coarse_project(gathered, coarse_in, coarse_back, groups):
    rows = gathered.shape[0] * COARSE
    return pl.pallas_call(
        coarse_project_kernel,
        out_shape=[shaped((groups, rows, 2 * PAIR), BF), shaped((rows, 2 * PAIR), F32)],
        compiler_params=params(VMEM_MIB),
        cost_estimate=cost(140_000_000, 3_000_000),
        name="coarse_project",
    )(gathered, coarse_in, coarse_back)


def coarse_attention(place, everyone, factor, coarse_in, coarse_back):
    rows = factor.shape[0]
    return pl.pallas_call(
        coarse_attention_kernel,
        in_specs=[SCALAR] + [IN_VMEM] * 4,
        out_shape=shaped((rows // COARSE, 2 * COARSE, D), BF),
        scratch_shapes=[pltpu.VMEM((rows, PAIR), F32)],
        compiler_params=params(VMEM_MIB),
        cost_estimate=cost(1_500_000_000, 3_000_000, 3_000_000),
        name="coarse_attention",
    )(place, everyone, factor, coarse_in, coarse_back)


def coarse_finish(returned, message, coarse_grad):
    return pl.pallas_call(
        coarse_finish_kernel,
        grid=(1,),
        in_specs=[whole(returned.shape), whole((1, 2 * COARSE, D)), whole((COARSE, D))],
        out_specs=[whole((COARSE, D)), whole((1, D)), whole((COARSE, D))],
        out_shape=[shaped((COARSE, D), F32), shaped((1, D), F32), shaped((COARSE, D), F32)],
        compiler_params=params(VMEM_MIB),
        cost_estimate=cost(1_000_000, 1_000_000),
        name="coarse_finish",
    )(returned, message, coarse_grad)


def fine_backward(
    place, cotangent, spread, fine_out, weights, query, key, value, q_factor, k_factor, probs,
    attended,
):
    return pl.pallas_call(
        fine_backward_kernel,
        in_specs=[SCALAR] + [IN_VMEM] * 11,
        out_specs=[IN_VMEM] * 7,
        out_shape=[shaped((ROWS, D), BF)] * 4
        + [shaped((EXTRA, D), BF)]
        + [shaped((ROWS, D), F32)] * 2,
        scratch_shapes=[pltpu.VMEM((QUERIES, D), BF), pltpu.VMEM((ALL_KEYS, D), F32)],
        compiler_params=params(16),
        cost_estimate=cost(5_000_000_000, 20_000_000),
        name="fine_backward",
    )(
        place, cotangent, spread, fine_out, weights, query, key, value, q_factor, k_factor, probs,
        attended,
    )


def halo_send(place, own, before, count):
    return pl.pallas_call(
        halo_send_kernel,
        grid=(count,),
        in_specs=[SCALAR, whole((ROWS, D)), whole((ROWS, D))],
        out_specs=pl.BlockSpec((1, ROWS, D), lambda p: (p, 0, 0)),
        out_shape=shaped((count, ROWS, D), BF),
        compiler_params=params(8),
        cost_estimate=cost(1_000_000, 1_500_000),
        name="halo_send",
    )(place, own, before)


def repeated(block, count):
    return pl.pallas_call(
        repeated_kernel,
        out_shape=shaped((count, *block.shape), BF),
        compiler_params=params(VMEM_MIB),
        cost_estimate=cost(1_000_000, 1_300_000),
        name="repeated",
    )(block)


def fine_finish(own, arrived, tail, after, hidden_grad, tokens):
    return pl.pallas_call(
        fine_finish_kernel,
        out_shape=shaped((ROWS, D), BF),
        compiler_params=params(VMEM_MIB),
        cost_estimate=cost(1_000_000, 3_000_000),
        name="fine_finish",
    )(own, *arrived, tail, after, hidden_grad, tokens)


def per_device(tokens, cotangent, fine_qkv, fine_out, coarse_qkv, coarse_out):
    peers = 1
    for name in GROUP:
        peers *= lax.axis_size(name)
    groups = 1
    for name in FAR:
        groups *= lax.axis_size(name)
    weights = jnp.transpose(fine_qkv, (1, 0, 2))
    core = lax.axis_index("core").astype(jnp.int32).reshape(1)
    column_at = lax.axis_index("x")
    columns_along = lax.axis_size("x")
    tail = shifted_by(tokens[ROWS - EXTRA :], columns_along + 1)
    row_before = shifted_by(tokens, columns_along)
    group_start = lax.axis_index(FAR) * (peers * COARSE)
    place = jnp.stack([lax.axis_index(LINE) * ROWS, column_at, group_start]).astype(jnp.int32)
    prepared = fine_prepare(place, tokens, cotangent, weights, fine_out)
    coarse_weights = coarse_prepare(core, jnp.transpose(coarse_qkv, (1, 0, 2)), coarse_out)
    tail, row_before, prepared, coarse_weights, place = lax.optimization_barrier(
        (tail, row_before, prepared, coarse_weights, place)
    )
    own, weights, fine_out, *_, coarse_grad = prepared
    coarse_in, coarse_back = coarse_weights
    slots = exchanged(halo_send(place, own, row_before, columns_along), "x")
    *kept, hidden, message = fine_forward(place, tail, slots, prepared, peers)
    gathered = exchanged(message, GROUP)
    near, further = lax.axis_size("z_hi"), lax.axis_size("y")
    coarse_send, coarse_factor = coarse_project(gathered, coarse_in, coarse_back, near)
    group_rows = coarse_factor.shape[0]
    nearby = exchanged(coarse_send, "z_hi").reshape(near * group_rows, 2 * PAIR)
    everyone = exchanged(repeated(nearby, further), "y").reshape(groups * group_rows, 2 * PAIR)
    partial = coarse_attention(place, everyone, coarse_factor, coarse_in, coarse_back)
    returned = exchanged(partial, GROUP)
    spread, first, state = coarse_finish(returned, message, coarse_grad)
    output = (
        hidden.astype(F32) + jnp.repeat(state.astype(BF), POOL, axis=0).astype(F32)
    ).astype(BF)
    *backs, tail_back, own_grad, hidden_grad = fine_backward(
        place, cotangent, spread, fine_out, weights, *kept
    )
    arrived = [shifted_by(rows, -steps) for steps, rows in enumerate(backs, 1)]
    tail_back, first, _ = lax.optimization_barrier((tail_back, first, own_grad))
    tail_arrived = shifted_by(tail_back, -(columns_along + 1))
    after = shifted_by(first, -1)
    return (output, fine_finish(own_grad, arrived, tail_arrived, after, hidden_grad, own))


def solution(mesh):
    sizes = (4, 4, 2, 2, 4)
    fine_mesh = Mesh(mesh.devices.reshape(sizes), LINE)
    placed = (
        P(LINE, None),
        P(LINE, None),
        P(),
        P(),
        P(None, None, ("z_lo", "x")),
        P(("z_lo", "x"), None),
    )
    return jax.shard_map(
        per_device,
        mesh=fine_mesh,
        in_specs=placed,
        out_specs=(P(LINE, None), P(LINE, None)),
        check_vma=False,
    )
```

```python
import jax
import jax.numpy as jnp
from jax import lax
from jax.experimental import pallas as pl
from jax.experimental.pallas import tpu as pltpu
from jax.sharding import Mesh
from jax.sharding import PartitionSpec as P

D = 1024
HEADS = 16
HEAD_DIM = 64
WINDOW = 512
POOL = 16
EPS = 1e-06

LINE = ("y", "z_hi", "core", "z_lo", "x")
GROUP = ("core", "z_lo", "x")
FAR = ("y", "z_hi")

ROWS = 128
HALO = WINDOW
OWN_KEYS = HALO + ROWS
EXTRA = 16
ALL_KEYS = OWN_KEYS + EXTRA
QUERIES = EXTRA + ROWS
PAIR = 2 * HEAD_DIM
COARSE = ROWS // POOL
SCALE = HEAD_DIM ** (-0.5)
NEG = -1e30
VMEM_MIB = 16

BF = jnp.bfloat16
F32 = jnp.float32


def shifted_by(value, steps):
    count = 1
    for name in LINE:
        count *= lax.axis_size(name)
    first, last = (max(0, -steps), min(count, count - steps))
    return lax.ppermute(value, LINE, [(source, source + steps) for source in range(first, last)])


def exchanged(pieces, axes):
    return lax.all_to_all(pieces, axes, 0, 0, tiled=True)


def last_last(left, right):
    return lax.dot_general(left, right, (((1,), (1,)), ((), ())), preferred_element_type=F32)


def first_first(left, right):
    return lax.dot_general(left, right, (((0,), (0,)), ((), ())), preferred_element_type=F32)


def plain(left, right):
    return jnp.dot(left, right, preferred_element_type=F32)


def low_lanes():
    return lax.broadcasted_iota(jnp.int32, (1, PAIR), 1) < HEAD_DIM


def pair_sums(values, low):
    low_sum = jnp.sum(jnp.where(low, values, 0.0), axis=-1, keepdims=True)
    high_sum = jnp.sum(jnp.where(low, 0.0, values), axis=-1, keepdims=True)
    return jnp.where(low, low_sum, high_sum)


def pair_norm(values, low):
    factor = lax.rsqrt(pair_sums(values * values, low) * (1.0 / HEAD_DIM) + EPS)
    return values * factor, factor


def pair_norm_back(grad, unit, factor, low):
    return factor * (grad - unit * (pair_sums(unit * grad, low) * (1.0 / HEAD_DIM)))


def row_norm(rows):
    factor = lax.rsqrt(jnp.mean(rows * rows, axis=-1, keepdims=True) + EPS)
    return rows * factor, factor


def row_norm_back(grad, normed, factor):
    return factor * (grad - normed * jnp.mean(normed * grad, axis=-1, keepdims=True))


def fine_prepare_kernel(
    place_ref, own_hbm, cot_hbm, w_hbm, out_w_hbm,
    own_ref, w_ref, out_w_ref, q_ref, k_ref, v_ref, qf_ref, kf_ref, bias_ref, cg_ref,
    cot, copied,
):
    anchor = place_ref[0]
    column_at = place_ref[1]
    low = low_lanes()
    copies = [
        pltpu.make_async_copy(source, target, copied.at[at])
        for at, (source, target) in enumerate(
            ((own_hbm, own_ref), (cot_hbm, cot), (w_hbm, w_ref), (out_w_hbm, out_w_ref))
        )
    ]
    for copy in copies:
        copy.start()

    row = lax.broadcasted_iota(jnp.int32, (2 * QUERIES, ALL_KEYS), 0)
    query_pos = jnp.where(row < QUERIES, row, row - QUERIES) - EXTRA
    column = lax.broadcasted_iota(jnp.int32, (2 * QUERIES, ALL_KEYS), 1)
    turned = column_at * ROWS
    halo_pos = column - jnp.where(column >= turned, turned + HALO, turned)
    key_pos = jnp.where(
        column < HALO,
        halo_pos,
        jnp.where(column < OWN_KEYS, column - HALO, column - (OWN_KEYS + HALO + EXTRA)),
    )
    gap = query_pos - key_pos
    allowed = (gap >= 0) & (gap < WINDOW) & (anchor + key_pos >= 0)
    bias_ref[...] = jnp.where(allowed, 0.0, NEG)

    copies[0].wait()
    normed = row_norm(own_ref[...].astype(F32))[0].astype(BF)
    copies[1].wait()
    chunk = lax.broadcasted_iota(jnp.int32, (COARSE, ROWS), 0) * POOL
    row = lax.broadcasted_iota(jnp.int32, (COARSE, ROWS), 1)
    member = jnp.where((row >= chunk) & (row < chunk + POOL), 1.0, 0.0).astype(BF)
    cg_ref[...] = plain(member, cot[...])
    copies[2].wait()
    for at in range(0, D, WIDTH):
        here = slice(at, at + WIDTH)
        queries = plain(normed, w_ref[0, :, here])
        keys = plain(normed, w_ref[1, :, here])
        v_ref[:, here] = plain(normed, w_ref[2, :, here]).astype(BF)
        for part in range(0, WIDTH, PAIR):
            inner = slice(part, part + PAIR)
            outer = slice(at + part, at + part + PAIR)
            query, q_factor = pair_norm(queries[:, inner], low)
            key, k_factor = pair_norm(keys[:, inner], low)
            q_ref[:, outer] = query.astype(BF)
            k_ref[:, outer] = key.astype(BF)
            qf_ref[:, outer] = q_factor
            kf_ref[:, outer] = k_factor
    copies[3].wait()


def fine_forward_kernel(
    place_ref, tail_ref, slots_ref, own_ref, w_ref, out_w_ref, own_q_ref, own_k_ref, own_v_ref,
    own_qf_ref, own_kf_ref, bias, cg_ref,
    q_ref, k_ref, v_ref, qf_ref, kf_ref, p_ref, att_ref, hid_ref, send_ref,
    normed, acc,
):
    anchor = place_ref[0]
    column_at = place_ref[1]
    low = low_lanes()
    slots = slots_ref.shape[0]
    nearest = lax.rem(column_at + (slots - 1), slots)
    for slot in range(slots):
        at = slot * ROWS
        normed[at : at + ROWS, :] = row_norm(slots_ref[slot].astype(F32))[0].astype(BF)
    normed[HALO:, :] = row_norm(tail_ref[...].astype(F32))[0].astype(BF)
    acc[...] = jnp.zeros_like(acc)
    extra_at = pl.multiple_of(nearest * ROWS + (ROWS - EXTRA), EXTRA)

    def one_step(step, carry):
        first = pl.multiple_of(step * WIDTH, WIDTH)
        here = pl.ds(first, WIDTH)
        extra = plain(normed[pl.ds(extra_at, EXTRA), :], w_ref[0, :, here])
        both = plain(
            normed[...], jnp.concatenate([w_ref[1, :, here], w_ref[2, :, here]], axis=1)
        )
        own_q, own_k, own_v = own_q_ref[:, here], own_k_ref[:, here], own_v_ref[:, here]
        own_kf = own_kf_ref[:, here]
        mixed = []
        for part in range(0, WIDTH, PAIR):
            inner = slice(part, part + PAIR)
            outer = pl.ds(pl.multiple_of(first + part, PAIR), PAIR)
            key, k_factor = pair_norm(both[:, inner], low)
            key = key.astype(BF)
            value = both[:, WIDTH + part : WIDTH + part + PAIR].astype(BF)
            key = jnp.concatenate([key[:HALO], own_k[:, inner], key[HALO:]], axis=0)
            value = jnp.concatenate([value[:HALO], own_v[:, inner], value[HALO:]], axis=0)
            k_ref[:, outer] = key
            v_ref[:, outer] = value
            kf_ref[:HALO, outer] = k_factor[:HALO]
            kf_ref[HALO:OWN_KEYS, outer] = own_kf[:, inner]
            kf_ref[OWN_KEYS:, outer] = k_factor[HALO:]
            before, before_factor = pair_norm(extra[:, inner], low)
            query = jnp.concatenate([before.astype(BF), own_q[:, inner]], axis=0)
            q_ref[:, outer] = query
            qf_ref[:EXTRA, outer] = before_factor
            qf_ref[EXTRA:, outer] = own_qf_ref[:, outer]
            scaled = query.astype(F32) * SCALE
            stacked = jnp.concatenate(
                [jnp.where(low, scaled, 0.0), jnp.where(low, 0.0, scaled)], axis=0
            )
            numer = jnp.exp(last_last(stacked.astype(BF), key) + bias[...])
            total = jnp.sum(numer, axis=-1, keepdims=True)
            prob = (numer * (1.0 / jnp.where(total > 0.0, total, 1.0))).astype(BF)
            head = (first + part) // HEAD_DIM
            p_ref[head] = prob[:QUERIES]
            p_ref[head + 1] = prob[QUERIES:]
            twice = plain(prob, value)
            attended = jnp.where(low, twice[:QUERIES], twice[QUERIES:]).astype(BF)
            att_ref[:, outer] = attended
            mixed.append(attended)
        acc[...] += plain(jnp.concatenate(mixed, axis=1), out_w_ref[here, :])
        return carry

    lax.fori_loop(0, D // WIDTH, one_step, 0, unroll=True)
    before = slots_ref[nearest, ROWS - EXTRA :, :].astype(F32) + acc[:EXTRA, :]
    before = jnp.where(anchor > 0, before, 0.0).astype(BF)
    own = (own_ref[...].astype(F32) + acc[EXTRA:, :]).astype(BF)
    hid_ref[...] = own
    chunk = lax.broadcasted_iota(jnp.int32, (COARSE, QUERIES), 0) * POOL
    row = lax.broadcasted_iota(jnp.int32, (COARSE, QUERIES), 1)
    member = jnp.where((row > chunk) & (row <= chunk + POOL), 1.0, 0.0).astype(BF)
    pooled = plain(member, jnp.concatenate([before, own], axis=0)) * (1.0 / POOL)
    message = jnp.concatenate([pooled, cg_ref[...]], axis=0).astype(BF)
    for peer in range(send_ref.shape[0]):
        send_ref[peer] = message


def coarse_prepare_kernel(core_ref, w_ref, back_ref, in_ref, out_ref):
    low = low_lanes()
    second = core_ref[0] > 0
    parts = [w_ref[at].astype(F32) for at in range(3)]
    turned = [pltpu.roll(part, HEAD_DIM, 1) for part in parts]
    query = jnp.where(second, turned[0], parts[0])
    key = jnp.where(second, turned[1], parts[1])
    value = jnp.where(second, parts[2], turned[2])
    in_ref[:, :PAIR] = jnp.where(low, query, 0.0).astype(BF)
    in_ref[:, PAIR:] = jnp.where(low, key, value).astype(BF)
    out_ref[...] = jnp.zeros_like(out_ref)
    out_ref[HEAD_DIM:PAIR, :] = jnp.where(second, back_ref[HEAD_DIM:, :], back_ref[:HEAD_DIM, :])


def coarse_project_kernel(got_ref, in_w_ref, out_w_ref, send_ref, factor_ref):
    low = low_lanes()
    rows = got_ref[...].astype(F32)
    count = rows.shape[0] * COARSE
    pooled = rows[:, :COARSE, :].reshape(count, D)
    coarse_grad = rows[:, COARSE:, :].reshape(count, D)
    normed = row_norm(pooled)[0].astype(BF)
    raw = plain(normed, in_w_ref[...]) + last_last(coarse_grad.astype(BF), out_w_ref[...])
    units, factors = [], []
    for tile in (raw[:, :PAIR], raw[:, PAIR:]):
        unit, factor = pair_norm(tile, low)
        units.append(jnp.where(low, unit, tile))
        factors.append(factor)
    message = jnp.concatenate(units, axis=1).astype(BF)
    factor_ref[...] = jnp.concatenate(factors, axis=1)
    for peer in range(send_ref.shape[0]):
        send_ref[peer] = message


def coarse_attention_kernel(place_ref, got_ref, factor_ref, in_w_ref, out_w_ref, send_ref, own_grad):
    low = low_lanes()
    own_start = pl.multiple_of(place_ref[2], ROWS)
    length = got_ref.shape[0]
    block = 512
    own_left = got_ref[pl.ds(own_start, ROWS), :PAIR]
    own_right = got_ref[pl.ds(own_start, ROWS), PAIR:]
    own_grad[...] = jnp.zeros_like(own_grad)

    def masked_halves(tile):
        wide = tile.astype(F32)
        return (
            jnp.where(low, wide * SCALE, 0.0).astype(BF),
            jnp.where(low, 0.0, wide).astype(BF),
        )

    def lane_partials(values):
        total = values[:, :PAIR]
        for at in range(PAIR, values.shape[1], PAIR):
            total = total + values[:, at : at + PAIR]
        return total

    def one_block(index):
        first = index * block
        query, grad = masked_halves(got_ref[first : first + block, :PAIR])
        stacked = jnp.concatenate([query, grad], axis=0)

        def scored(keys):
            both = last_last(stacked, keys)
            return jnp.exp(both[:block]), both[block:]

        query_at = lax.broadcasted_iota(jnp.int32, (block, 1), 0)
        total = product = None
        for at in range(index + 1):
            numer, prob_grad = scored(got_ref[at * block : (at + 1) * block, PAIR:])
            if at == index:
                key_at = lax.broadcasted_iota(jnp.int32, (1, block), 1)
                numer = jnp.where(key_at <= query_at, numer, 0.0)
            sums = lane_partials(numer), lane_partials(numer * prob_grad)
            total, product = sums if at == 0 else (total + sums[0], product + sums[1])
        inverse = 1.0 / jnp.sum(total, axis=-1, keepdims=True)
        delta = jnp.sum(product, axis=-1, keepdims=True) * inverse
        own_pos = own_start + lax.broadcasted_iota(jnp.int32, (1, ROWS), 1)
        numer, prob_grad = scored(own_right)
        numer = jnp.where(own_pos <= query_at + first, numer, 0.0)
        prob = numer * inverse
        score_grad = (prob * (prob_grad - delta)).astype(BF)
        own_grad[...] += first_first(
            jnp.concatenate([score_grad, prob.astype(BF)], axis=0), stacked
        )

    for index in range(length // block):
        pl.when(own_start < (index + 1) * block)(lambda index=index: one_block(index))

    query, grad = masked_halves(own_left)
    stacked = jnp.concatenate([query, grad], axis=0)
    query_pos = own_start + lax.broadcasted_iota(jnp.int32, (ROWS, 1), 0)

    def own_chunk(at):
        key_start = pl.multiple_of(at * block, block)
        keys = got_ref[pl.ds(key_start, block), PAIR:]
        both = last_last(stacked, keys)
        key_pos = key_start + lax.broadcasted_iota(jnp.int32, (1, block), 1)
        return keys, jnp.where(key_pos <= query_pos, jnp.exp(both[:ROWS]), 0.0), both[ROWS:]

    def own_sums(at, sums):
        numer, prob_grad = own_chunk(at)[1:]
        return sums[0] + lane_partials(numer), sums[1] + lane_partials(numer * prob_grad)

    nothing = jnp.zeros((ROWS, PAIR), F32)
    chunks = own_start // block + 1
    total, product = lax.fori_loop(0, chunks, own_sums, (nothing, nothing))
    inverse = 1.0 / jnp.sum(total, axis=-1, keepdims=True)
    delta = jnp.sum(product, axis=-1, keepdims=True) * inverse

    def own_results(at, mine):
        keys, numer, prob_grad = own_chunk(at)
        key_scaled, value = masked_halves(keys)
        prob = numer * inverse
        score_grad = (prob * (prob_grad - delta)).astype(BF)
        return mine + plain(score_grad, key_scaled) + plain(prob.astype(BF), value)

    mine = lax.fori_loop(0, chunks, own_results, nothing)

    parts = []
    for tile, unit, factor in (
        (mine, own_left, factor_ref[:, :PAIR]),
        (own_grad[...], own_right, factor_ref[:, PAIR:]),
    ):
        back = pair_norm_back(tile, unit.astype(F32), factor, low)
        parts.append(jnp.where(low, back, tile))
    parts = jnp.concatenate(parts, axis=1).astype(BF)
    peers = send_ref.shape[0]
    normed_grad = last_last(parts, in_w_ref[...]).reshape(peers, COARSE, D)
    mixed = plain(parts, out_w_ref[...]).reshape(peers, COARSE, D)
    send_ref[...] = jnp.concatenate([normed_grad, mixed], axis=1).astype(BF)


def coarse_finish_kernel(got_ref, message_ref, cg_ref, spread_ref, state_ref):
    summed = jnp.sum(got_ref[...].astype(F32), axis=0)
    pooled = message_ref[0].astype(F32)[:COARSE]
    normed, factor = row_norm(pooled)
    pooled_grad = cg_ref[...] + row_norm_back(summed[:COARSE], normed, factor)
    spread_ref[...] = pooled_grad * (1.0 / POOL)
    state_ref[...] = pooled + summed[COARSE:]


def fine_backward_kernel(
    place_ref, cot_ref, spread_ref, out_w_ref, w_ref, q_ref, k_ref, v_ref, qf_ref, kf_ref, p_ref,
    att_ref,
    back1, back2, back3, back4, tail_ref, own_ref, hg_ref, hidden_grad, acc,
):
    low = low_lanes()
    block = (lax.broadcasted_iota(jnp.int32, (ROWS, 1), 0) + (POOL - 1)) // POOL
    added = jnp.zeros((ROWS, D), F32)
    for at in range(COARSE):
        added = jnp.where(block == at, spread_ref[at : at + 1, :], added)
    total = cot_ref[...].astype(F32) + added
    hg_ref[...] = total
    counted = lax.broadcasted_iota(jnp.int32, (EXTRA, 1), 0) > EXTRA - POOL
    hidden_grad[:EXTRA, :] = jnp.where(counted, spread_ref[0:1, :], 0.0).astype(BF)
    hidden_grad[EXTRA:, :] = total.astype(BF)
    backs = (back1, back2, back3, back4)
    slots = len(backs)
    nearest = lax.rem(place_ref[1] + (slots - 1), slots)
    extra_at = pl.multiple_of(nearest * ROWS + (ROWS - EXTRA), EXTRA)
    acc[...] = jnp.zeros_like(acc)

    def one_step(step, carry):
        first = pl.multiple_of(step * WIDTH, WIDTH)
        here = pl.ds(first, WIDTH)
        att_grads = last_last(hidden_grad[...], out_w_ref[here, :]).astype(BF).astype(F32)
        query_grads, key_grads, value_grads = [], [], []
        for part in range(0, WIDTH, PAIR):
            outer = pl.ds(pl.multiple_of(first + part, PAIR), PAIR)
            att_grad = att_grads[:, part : part + PAIR]
            delta_all = att_grad * att_ref[:, outer].astype(F32)
            value = v_ref[:, outer]
            key_wide = k_ref[:, outer].astype(F32)
            query_wide = q_ref[:, outer].astype(F32)
            grad = jnp.concatenate(
                [jnp.where(low, att_grad, 0.0), jnp.where(low, 0.0, att_grad)], axis=0
            ).astype(BF)
            delta = jnp.sum(
                jnp.concatenate(
                    [jnp.where(low, delta_all, 0.0), jnp.where(low, 0.0, delta_all)], axis=0
                ),
                axis=-1,
                keepdims=True,
            )
            scaled = query_wide * SCALE
            query = jnp.concatenate(
                [jnp.where(low, scaled, 0.0), jnp.where(low, 0.0, scaled)], axis=0
            ).astype(BF)
            head = (first + part) // HEAD_DIM
            prob = p_ref[pl.ds(head, 2)].reshape(2 * QUERIES, ALL_KEYS)
            score_grad = (prob.astype(F32) * (last_last(grad, value) - delta)).astype(BF)
            twice = plain(score_grad, (key_wide * SCALE).astype(BF))
            query_grad = jnp.where(low, twice[:QUERIES], twice[QUERIES:])
            key_grad = first_first(score_grad, query)
            value_grad = first_first(prob, grad)
            query_grads.append(pair_norm_back(query_grad, query_wide, qf_ref[:, outer], low).astype(BF))
            key_grads.append(pair_norm_back(key_grad, key_wide, kf_ref[:, outer], low).astype(BF))
            value_grads.append(value_grad.astype(BF))
        both = jnp.concatenate(key_grads + value_grads, axis=1)
        acc[...] += last_last(
            both, jnp.concatenate([w_ref[1, :, here], w_ref[2, :, here]], axis=1)
        )
        from_query = last_last(jnp.concatenate(query_grads, axis=1), w_ref[0, :, here])
        acc[pl.ds(extra_at, EXTRA), :] += from_query[:EXTRA]
        acc[HALO:OWN_KEYS, :] += from_query[EXTRA:]
        return carry

    lax.fori_loop(0, D // WIDTH, one_step, 0, unroll=True)
    for distance, ref in enumerate(backs, 1):
        slot = lax.rem(place_ref[1] + (slots - distance), slots)
        ref[:ROWS, :] = acc[pl.ds(pl.multiple_of(slot * ROWS, ROWS), ROWS), :].astype(BF)
    back1[ROWS:, :] = jnp.broadcast_to(spread_ref[0:1, :], (EXTRA, D)).astype(BF)
    tail_ref[...] = acc[OWN_KEYS:, :].astype(BF)
    own_ref[...] = acc[HALO:OWN_KEYS, :]


def halo_send_kernel(place_ref, own_ref, before_ref, send_ref):
    send_ref[0] = jnp.where(place_ref[1] < pl.program_id(0), own_ref[...], before_ref[...])


def repeated_kernel(block_ref, send_ref):
    for peer in range(send_ref.shape[0]):
        send_ref[peer] = block_ref[...]


def fine_finish_kernel(own_ref, a1, a2, a3, a4, tail_ref, hg_ref, tokens_ref, out_ref):
    total = own_ref[...]
    for ref in (a1, a2, a3, a4):
        total = total + ref[:ROWS, :].astype(F32)
    split = ROWS - EXTRA
    total = jnp.concatenate([total[:split], total[split:] + tail_ref[...].astype(F32)], axis=0)
    normed, factor = row_norm(tokens_ref[...].astype(F32))
    after = lax.broadcasted_iota(jnp.int32, (ROWS, 1), 0) > ROWS - POOL
    hidden_grad = hg_ref[...] + jnp.where(after, a1[ROWS:, :].astype(F32)[:1], 0.0)
    out_ref[...] = (hidden_grad + row_norm_back(total, normed, factor)).astype(BF)


def whole(shape):
    return pl.BlockSpec(shape, lambda *_: (0,) * len(shape))


def columns(rows, width):
    return pl.BlockSpec((rows, width), lambda p: (0, p))


def shaped(shape, kind):
    return jax.ShapeDtypeStruct(shape, kind)


def params(mib):
    return pltpu.CompilerParams(vmem_limit_bytes=mib << 20)


def cost(flops, moved, exps=0):
    return pl.CostEstimate(flops=flops, bytes_accessed=moved, transcendentals=exps)


SCALAR = pl.BlockSpec(memory_space=pltpu.SMEM)
IN_VMEM = pl.BlockSpec(memory_space=pltpu.VMEM)
WIDTH = 4 * PAIR


def in_hbm(x):
    return pltpu.with_memory_space_constraint(x, pltpu.HBM)


def fine_prepare(place, tokens, cotangent, weights, fine_out):
    anywhere = pl.BlockSpec(memory_space=pltpu.HBM)
    return pl.pallas_call(
        fine_prepare_kernel,
        in_specs=[SCALAR] + [anywhere] * 4,
        out_specs=[IN_VMEM] * 10,
        out_shape=[
            pltpu.VMEM((ROWS, D), BF),
            pltpu.VMEM((3, D, D), BF),
            pltpu.VMEM((D, D), BF),
            pltpu.VMEM((ROWS, D), BF),
            pltpu.VMEM((ROWS, D), BF),
            pltpu.VMEM((ROWS, D), BF),
            pltpu.VMEM((ROWS, D), F32),
            pltpu.VMEM((ROWS, D), F32),
            pltpu.VMEM((2 * QUERIES, ALL_KEYS), F32),
            pltpu.VMEM((COARSE, D), F32),
        ],
        scratch_shapes=[pltpu.VMEM((ROWS, D), BF), pltpu.SemaphoreType.DMA((4,))],
        compiler_params=params(16),
        cost_estimate=cost(900_000_000, 17_000_000),
        name="fine_prepare",
    )(place, *(in_hbm(x) for x in (tokens, cotangent, weights, fine_out)))


def fine_forward(place, tail, slots, prepared, peers):
    return pl.pallas_call(
        fine_forward_kernel,
        in_specs=[SCALAR] + [IN_VMEM] * 12,
        out_specs=[IN_VMEM] * 9,
        out_shape=[
            pltpu.VMEM((QUERIES, D), BF),
            pltpu.VMEM((ALL_KEYS, D), BF),
            pltpu.VMEM((ALL_KEYS, D), BF),
            pltpu.VMEM((QUERIES, D), F32),
            pltpu.VMEM((ALL_KEYS, D), F32),
            pltpu.VMEM((HEADS, QUERIES, ALL_KEYS), BF),
            pltpu.VMEM((QUERIES, D), BF),
            shaped((ROWS, D), BF),
            shaped((peers, 2 * COARSE, D), BF),
        ],
        scratch_shapes=[pltpu.VMEM((HALO + EXTRA, D), BF), pltpu.VMEM((QUERIES, D), F32)],
        compiler_params=params(16),
        cost_estimate=cost(4_500_000_000, 20_000_000, 1_600_000),
        name="fine_forward",
    )(place, tail, slots, *prepared)


def coarse_prepare(core, weights, back):
    return pl.pallas_call(
        coarse_prepare_kernel,
        in_specs=[SCALAR, IN_VMEM, IN_VMEM],
        out_specs=[IN_VMEM] * 2,
        out_shape=[shaped((D, 2 * PAIR), BF), shaped((2 * PAIR, D), BF)],
        compiler_params=params(8),
        cost_estimate=cost(1_000_000, 2_500_000),
        name="coarse_prepare",
    )(core, weights, back)


def coarse_project(gathered, coarse_in, coarse_back, groups):
    rows = gathered.shape[0] * COARSE
    return pl.pallas_call(
        coarse_project_kernel,
        out_shape=[shaped((groups, rows, 2 * PAIR), BF), shaped((rows, 2 * PAIR), F32)],
        compiler_params=params(VMEM_MIB),
        cost_estimate=cost(140_000_000, 3_000_000),
        name="coarse_project",
    )(gathered, coarse_in, coarse_back)


def coarse_attention(place, everyone, factor, coarse_in, coarse_back):
    rows = factor.shape[0]
    return pl.pallas_call(
        coarse_attention_kernel,
        in_specs=[SCALAR] + [IN_VMEM] * 4,
        out_shape=shaped((rows // COARSE, 2 * COARSE, D), BF),
        scratch_shapes=[pltpu.VMEM((rows, PAIR), F32)],
        compiler_params=params(VMEM_MIB),
        cost_estimate=cost(1_500_000_000, 3_000_000, 3_000_000),
        name="coarse_attention",
    )(place, everyone, factor, coarse_in, coarse_back)


def coarse_finish(returned, message, coarse_grad):
    return pl.pallas_call(
        coarse_finish_kernel,
        grid=(1,),
        in_specs=[whole(returned.shape), whole((1, 2 * COARSE, D)), whole((COARSE, D))],
        out_specs=[whole((COARSE, D))] * 2,
        out_shape=[shaped((COARSE, D), F32)] * 2,
        compiler_params=params(VMEM_MIB),
        cost_estimate=cost(1_000_000, 1_000_000),
        name="coarse_finish",
    )(returned, message, coarse_grad)


def fine_backward(
    place, cotangent, spread, fine_out, weights, query, key, value, q_factor, k_factor, probs,
    attended,
):
    return pl.pallas_call(
        fine_backward_kernel,
        in_specs=[SCALAR] + [IN_VMEM] * 11,
        out_specs=[IN_VMEM] * 7,
        out_shape=[shaped((ROWS + EXTRA, D), BF)]
        + [shaped((ROWS, D), BF)] * 3
        + [shaped((EXTRA, D), BF)]
        + [shaped((ROWS, D), F32)] * 2,
        scratch_shapes=[pltpu.VMEM((QUERIES, D), BF), pltpu.VMEM((ALL_KEYS, D), F32)],
        compiler_params=params(16),
        cost_estimate=cost(5_000_000_000, 20_000_000),
        name="fine_backward",
    )(
        place, cotangent, spread, fine_out, weights, query, key, value, q_factor, k_factor, probs,
        attended,
    )


def halo_send(place, own, before, count):
    return pl.pallas_call(
        halo_send_kernel,
        grid=(count,),
        in_specs=[SCALAR, whole((ROWS, D)), whole((ROWS, D))],
        out_specs=pl.BlockSpec((1, ROWS, D), lambda p: (p, 0, 0)),
        out_shape=shaped((count, ROWS, D), BF),
        compiler_params=params(8),
        cost_estimate=cost(1_000_000, 1_500_000),
        name="halo_send",
    )(place, own, before)


def repeated(block, count):
    return pl.pallas_call(
        repeated_kernel,
        out_shape=shaped((count, *block.shape), BF),
        compiler_params=params(VMEM_MIB),
        cost_estimate=cost(1_000_000, 1_300_000),
        name="repeated",
    )(block)


def fine_finish(own, arrived, tail, hidden_grad, tokens):
    return pl.pallas_call(
        fine_finish_kernel,
        out_shape=shaped((ROWS, D), BF),
        compiler_params=params(VMEM_MIB),
        cost_estimate=cost(1_000_000, 3_000_000),
        name="fine_finish",
    )(own, *arrived, tail, hidden_grad, tokens)


def per_device(tokens, cotangent, fine_qkv, fine_out, coarse_qkv, coarse_out):
    peers = 1
    for name in GROUP:
        peers *= lax.axis_size(name)
    groups = 1
    for name in FAR:
        groups *= lax.axis_size(name)
    weights = jnp.transpose(fine_qkv, (1, 0, 2))
    core = lax.axis_index("core").astype(jnp.int32).reshape(1)
    column_at = lax.axis_index("x")
    columns_along = lax.axis_size("x")
    tail = shifted_by(tokens[ROWS - EXTRA :], columns_along + 1)
    row_before = shifted_by(tokens, columns_along)
    group_start = lax.axis_index(FAR) * (peers * COARSE)
    place = jnp.stack([lax.axis_index(LINE) * ROWS, column_at, group_start]).astype(jnp.int32)
    prepared = fine_prepare(place, tokens, cotangent, weights, fine_out)
    coarse_weights = coarse_prepare(core, jnp.transpose(coarse_qkv, (1, 0, 2)), coarse_out)
    tail, row_before, prepared, coarse_weights, place = lax.optimization_barrier(
        (tail, row_before, prepared, coarse_weights, place)
    )
    own, weights, fine_out, *_, coarse_grad = prepared
    coarse_in, coarse_back = coarse_weights
    slots = exchanged(halo_send(place, own, row_before, columns_along), "x")
    *kept, hidden, message = fine_forward(place, tail, slots, prepared, peers)
    gathered = exchanged(message, GROUP)
    near, further = lax.axis_size("z_hi"), lax.axis_size("y")
    coarse_send, coarse_factor = coarse_project(gathered, coarse_in, coarse_back, near)
    group_rows = coarse_factor.shape[0]
    nearby = exchanged(coarse_send, "z_hi").reshape(near * group_rows, 2 * PAIR)
    everyone = exchanged(repeated(nearby, further), "y").reshape(groups * group_rows, 2 * PAIR)
    partial = coarse_attention(place, everyone, coarse_factor, coarse_in, coarse_back)
    returned = exchanged(partial, GROUP)
    spread, state = coarse_finish(returned, message, coarse_grad)
    output = (
        hidden.astype(F32) + jnp.repeat(state.astype(BF), POOL, axis=0).astype(F32)
    ).astype(BF)
    *backs, tail_back, own_grad, hidden_grad = fine_backward(
        place, cotangent, spread, fine_out, weights, *kept
    )
    arrived = [shifted_by(rows, -steps) for steps, rows in enumerate(backs, 1)]
    tail_arrived = shifted_by(tail_back, -(columns_along + 1))
    return (output, fine_finish(own_grad, arrived, tail_arrived, hidden_grad, own))


def solution(mesh):
    sizes = (4, 4, 2, 2, 4)
    fine_mesh = Mesh(mesh.devices.reshape(sizes), LINE)
    placed = (
        P(LINE, None),
        P(LINE, None),
        P(),
        P(),
        P(None, None, ("z_lo", "x")),
        P(("z_lo", "x"), None),
    )
    return jax.shard_map(
        per_device,
        mesh=fine_mesh,
        in_specs=placed,
        out_specs=(P(LINE, None), P(LINE, None)),
        check_vma=False,
    )
```

```python
import jax
import jax.numpy as jnp
from jax import lax
from jax.experimental import pallas as pl
from jax.experimental.pallas import tpu as pltpu
from jax.sharding import Mesh
from jax.sharding import PartitionSpec as P

D = 1024
HEADS = 16
HEAD_DIM = 64
WINDOW = 512
POOL = 16
EPS = 1e-06

LINE = ("y", "z_hi", "core", "z_lo", "x")
GROUP = ("core", "z_lo", "x")
FAR = ("y", "z_hi")

ROWS = 128
HALO = WINDOW
OWN_KEYS = HALO + ROWS
EXTRA = 16
ALL_KEYS = OWN_KEYS + EXTRA
QUERIES = EXTRA + ROWS
PAIR = 2 * HEAD_DIM
COARSE = ROWS // POOL
SCALE = HEAD_DIM ** (-0.5)
NEG = -1e30
VMEM_MIB = 16

BF = jnp.bfloat16
F32 = jnp.float32


def shifted_by(value, steps):
    count = 1
    for name in LINE:
        count *= lax.axis_size(name)
    first, last = (max(0, -steps), min(count, count - steps))
    return lax.ppermute(value, LINE, [(source, source + steps) for source in range(first, last)])


def exchanged(pieces, axes):
    return lax.all_to_all(pieces, axes, 0, 0, tiled=True)


def last_last(left, right):
    return lax.dot_general(left, right, (((1,), (1,)), ((), ())), preferred_element_type=F32)


def first_first(left, right):
    return lax.dot_general(left, right, (((0,), (0,)), ((), ())), preferred_element_type=F32)


def plain(left, right):
    return jnp.dot(left, right, preferred_element_type=F32)


def low_lanes():
    return lax.broadcasted_iota(jnp.int32, (1, PAIR), 1) < HEAD_DIM


def pair_sums(values, low):
    low_sum = jnp.sum(jnp.where(low, values, 0.0), axis=-1, keepdims=True)
    high_sum = jnp.sum(jnp.where(low, 0.0, values), axis=-1, keepdims=True)
    return jnp.where(low, low_sum, high_sum)


def pair_norm(values, low):
    factor = lax.rsqrt(pair_sums(values * values, low) * (1.0 / HEAD_DIM) + EPS)
    return values * factor, factor


def pair_norm_back(grad, unit, factor, low):
    return factor * (grad - unit * (pair_sums(unit * grad, low) * (1.0 / HEAD_DIM)))


def row_norm(rows):
    factor = lax.rsqrt(jnp.mean(rows * rows, axis=-1, keepdims=True) + EPS)
    return rows * factor, factor


def row_norm_back(grad, normed, factor):
    return factor * (grad - normed * jnp.mean(normed * grad, axis=-1, keepdims=True))


def fine_prepare_kernel(
    place_ref, own_hbm, cot_hbm, w_hbm, out_w_hbm,
    own_ref, w_ref, out_w_ref, q_ref, k_ref, v_ref, qf_ref, kf_ref, bias_ref, cg_ref,
    cot, copied,
):
    anchor = place_ref[0]
    column_at = place_ref[1]
    low = low_lanes()
    copies = [
        pltpu.make_async_copy(source, target, copied.at[at])
        for at, (source, target) in enumerate(
            ((own_hbm, own_ref), (cot_hbm, cot), (w_hbm, w_ref), (out_w_hbm, out_w_ref))
        )
    ]
    for copy in copies:
        copy.start()

    row = lax.broadcasted_iota(jnp.int32, (2 * QUERIES, ALL_KEYS), 0)
    query_pos = jnp.where(row < QUERIES, row, row - QUERIES) - EXTRA
    column = lax.broadcasted_iota(jnp.int32, (2 * QUERIES, ALL_KEYS), 1)
    turned = column_at * ROWS
    halo_pos = column - jnp.where(column >= turned, turned + HALO, turned)
    key_pos = jnp.where(
        column < HALO,
        halo_pos,
        jnp.where(column < OWN_KEYS, column - HALO, column - (OWN_KEYS + HALO + EXTRA)),
    )
    gap = query_pos - key_pos
    allowed = (gap >= 0) & (gap < WINDOW) & (anchor + key_pos >= 0)
    bias_ref[...] = jnp.where(allowed, 0.0, NEG)

    copies[0].wait()
    normed = row_norm(own_ref[...].astype(F32))[0].astype(BF)
    copies[1].wait()
    chunk = lax.broadcasted_iota(jnp.int32, (COARSE, ROWS), 0) * POOL
    row = lax.broadcasted_iota(jnp.int32, (COARSE, ROWS), 1)
    member = jnp.where((row >= chunk) & (row < chunk + POOL), 1.0, 0.0).astype(BF)
    cg_ref[...] = plain(member, cot[...])
    copies[2].wait()
    for at in range(0, D, WIDTH):
        here = slice(at, at + WIDTH)
        queries = plain(normed, w_ref[0, :, here])
        keys = plain(normed, w_ref[1, :, here])
        v_ref[:, here] = plain(normed, w_ref[2, :, here]).astype(BF)
        for part in range(0, WIDTH, PAIR):
            inner = slice(part, part + PAIR)
            outer = slice(at + part, at + part + PAIR)
            query, q_factor = pair_norm(queries[:, inner], low)
            key, k_factor = pair_norm(keys[:, inner], low)
            q_ref[:, outer] = query.astype(BF)
            k_ref[:, outer] = key.astype(BF)
            qf_ref[:, outer] = q_factor
            kf_ref[:, outer] = k_factor
    copies[3].wait()


def fine_forward_kernel(
    place_ref, tail_ref, slots_ref, own_ref, w_ref, out_w_ref, own_q_ref, own_k_ref, own_v_ref,
    own_kf_ref, bias, cg_ref,
    k_ref, v_ref, kf_ref, p_ref, att_ref, hid_ref, send_ref,
    normed, acc,
):
    anchor = place_ref[0]
    column_at = place_ref[1]
    low = low_lanes()
    slots = slots_ref.shape[0]
    nearest = lax.rem(column_at + (slots - 1), slots)
    for slot in range(slots):
        at = slot * ROWS
        normed[at : at + ROWS, :] = row_norm(slots_ref[slot].astype(F32))[0].astype(BF)
    normed[HALO:, :] = row_norm(tail_ref[...].astype(F32))[0].astype(BF)
    acc[...] = jnp.zeros_like(acc)
    extra_at = pl.multiple_of(nearest * ROWS + (ROWS - EXTRA), EXTRA)

    def one_step(step, carry):
        first = pl.multiple_of(step * WIDTH, WIDTH)
        here = pl.ds(first, WIDTH)
        extra = plain(normed[pl.ds(extra_at, EXTRA), :], w_ref[0, :, here])
        both = plain(
            normed[...], jnp.concatenate([w_ref[1, :, here], w_ref[2, :, here]], axis=1)
        )
        own_q, own_k, own_v = own_q_ref[:, here], own_k_ref[:, here], own_v_ref[:, here]
        own_kf = own_kf_ref[:, here]
        mixed = []
        for part in range(0, WIDTH, PAIR):
            inner = slice(part, part + PAIR)
            outer = pl.ds(pl.multiple_of(first + part, PAIR), PAIR)
            key, k_factor = pair_norm(both[:, inner], low)
            key = key.astype(BF)
            value = both[:, WIDTH + part : WIDTH + part + PAIR].astype(BF)
            k_ref[:HALO, outer] = key[:HALO]
            k_ref[HALO:, outer] = own_k[:, inner]
            v_ref[:HALO, outer] = value[:HALO]
            v_ref[HALO:, outer] = own_v[:, inner]
            kf_ref[:HALO, outer] = k_factor[:HALO]
            kf_ref[HALO:, outer] = own_kf[:, inner]
            key = jnp.concatenate([key[:HALO], own_k[:, inner], key[HALO:]], axis=0)
            value = jnp.concatenate([value[:HALO], own_v[:, inner], value[HALO:]], axis=0)
            before = pair_norm(extra[:, inner], low)[0].astype(BF).astype(F32)
            scaled = jnp.concatenate([before, own_q[:, inner].astype(F32)], axis=0) * SCALE
            stacked = jnp.concatenate(
                [jnp.where(low, scaled, 0.0), jnp.where(low, 0.0, scaled)], axis=0
            )
            numer = jnp.exp(last_last(stacked.astype(BF), key) + bias[...])
            total = jnp.sum(numer, axis=-1, keepdims=True)
            prob = (numer * (1.0 / jnp.where(total > 0.0, total, 1.0))).astype(BF)
            head = (first + part) // HEAD_DIM
            p_ref[head] = prob[EXTRA:QUERIES, :OWN_KEYS]
            p_ref[head + 1] = prob[QUERIES + EXTRA :, :OWN_KEYS]
            twice = plain(prob, value)
            attended = jnp.where(low, twice[:QUERIES], twice[QUERIES:]).astype(BF)
            att_ref[:, outer] = attended[EXTRA:]
            mixed.append(attended)
        acc[...] += plain(jnp.concatenate(mixed, axis=1), out_w_ref[here, :])
        return carry

    lax.fori_loop(0, D // WIDTH, one_step, 0, unroll=True)
    before = slots_ref[nearest, ROWS - EXTRA :, :].astype(F32) + acc[:EXTRA, :]
    before = jnp.where(anchor > 0, before, 0.0).astype(BF)
    own = (own_ref[...].astype(F32) + acc[EXTRA:, :]).astype(BF)
    hid_ref[...] = own
    chunk = lax.broadcasted_iota(jnp.int32, (COARSE, QUERIES), 0) * POOL
    row = lax.broadcasted_iota(jnp.int32, (COARSE, QUERIES), 1)
    member = jnp.where((row > chunk) & (row <= chunk + POOL), 1.0, 0.0).astype(BF)
    pooled = plain(member, jnp.concatenate([before, own], axis=0)) * (1.0 / POOL)
    message = jnp.concatenate([pooled, cg_ref[...]], axis=0).astype(BF)
    for peer in range(send_ref.shape[0]):
        send_ref[peer] = message


def coarse_prepare_kernel(core_ref, w_ref, back_ref, in_ref, out_ref):
    low = low_lanes()
    second = core_ref[0] > 0
    parts = [w_ref[at].astype(F32) for at in range(3)]
    turned = [pltpu.roll(part, HEAD_DIM, 1) for part in parts]
    query = jnp.where(second, turned[0], parts[0])
    key = jnp.where(second, turned[1], parts[1])
    value = jnp.where(second, parts[2], turned[2])
    in_ref[:, :PAIR] = jnp.where(low, query, 0.0).astype(BF)
    in_ref[:, PAIR:] = jnp.where(low, key, value).astype(BF)
    out_ref[...] = jnp.zeros_like(out_ref)
    out_ref[HEAD_DIM:PAIR, :] = jnp.where(second, back_ref[HEAD_DIM:, :], back_ref[:HEAD_DIM, :])


def coarse_project_kernel(got_ref, in_w_ref, out_w_ref, send_ref, factor_ref):
    low = low_lanes()
    rows = got_ref[...].astype(F32)
    count = rows.shape[0] * COARSE
    pooled = rows[:, :COARSE, :].reshape(count, D)
    coarse_grad = rows[:, COARSE:, :].reshape(count, D)
    normed = row_norm(pooled)[0].astype(BF)
    raw = plain(normed, in_w_ref[...]) + last_last(coarse_grad.astype(BF), out_w_ref[...])
    units, factors = [], []
    for tile in (raw[:, :PAIR], raw[:, PAIR:]):
        unit, factor = pair_norm(tile, low)
        units.append(jnp.where(low, unit, tile))
        factors.append(factor)
    message = jnp.concatenate(units, axis=1).astype(BF)
    factor_ref[...] = jnp.concatenate(factors, axis=1)
    for peer in range(send_ref.shape[0]):
        send_ref[peer] = message


def coarse_attention_kernel(place_ref, got_ref, factor_ref, in_w_ref, out_w_ref, send_ref, own_grad):
    low = low_lanes()
    own_start = pl.multiple_of(place_ref[2], ROWS)
    length = got_ref.shape[0]
    block = 512
    own_left = got_ref[pl.ds(own_start, ROWS), :PAIR]
    own_right = got_ref[pl.ds(own_start, ROWS), PAIR:]
    own_grad[...] = jnp.zeros_like(own_grad)

    def masked_halves(tile):
        wide = tile.astype(F32)
        return (
            jnp.where(low, wide * SCALE, 0.0).astype(BF),
            jnp.where(low, 0.0, wide).astype(BF),
        )

    def lane_partials(values):
        total = values[:, :PAIR]
        for at in range(PAIR, values.shape[1], PAIR):
            total = total + values[:, at : at + PAIR]
        return total

    def one_block(index):
        first = index * block
        query, grad = masked_halves(got_ref[first : first + block, :PAIR])
        stacked = jnp.concatenate([query, grad], axis=0)

        def scored(keys):
            both = last_last(stacked, keys)
            return jnp.exp(both[:block]), both[block:]

        query_at = lax.broadcasted_iota(jnp.int32, (block, 1), 0)
        total = product = None
        for at in range(index + 1):
            numer, prob_grad = scored(got_ref[at * block : (at + 1) * block, PAIR:])
            if at == index:
                key_at = lax.broadcasted_iota(jnp.int32, (1, block), 1)
                numer = jnp.where(key_at <= query_at, numer, 0.0)
            sums = lane_partials(numer), lane_partials(numer * prob_grad)
            total, product = sums if at == 0 else (total + sums[0], product + sums[1])
        inverse = 1.0 / jnp.sum(total, axis=-1, keepdims=True)
        delta = jnp.sum(product, axis=-1, keepdims=True) * inverse
        own_pos = own_start + lax.broadcasted_iota(jnp.int32, (1, ROWS), 1)
        numer, prob_grad = scored(own_right)
        numer = jnp.where(own_pos <= query_at + first, numer, 0.0)
        prob = numer * inverse
        score_grad = (prob * (prob_grad - delta)).astype(BF)
        own_grad[...] += first_first(
            jnp.concatenate([score_grad, prob.astype(BF)], axis=0), stacked
        )

    for index in range(length // block):
        pl.when(own_start < (index + 1) * block)(lambda index=index: one_block(index))

    query, grad = masked_halves(own_left)
    stacked = jnp.concatenate([query, grad], axis=0)
    query_pos = own_start + lax.broadcasted_iota(jnp.int32, (ROWS, 1), 0)

    def own_chunk(at):
        key_start = pl.multiple_of(at * block, block)
        keys = got_ref[pl.ds(key_start, block), PAIR:]
        both = last_last(stacked, keys)
        key_pos = key_start + lax.broadcasted_iota(jnp.int32, (1, block), 1)
        return keys, jnp.where(key_pos <= query_pos, jnp.exp(both[:ROWS]), 0.0), both[ROWS:]

    def own_sums(at, sums):
        numer, prob_grad = own_chunk(at)[1:]
        return sums[0] + lane_partials(numer), sums[1] + lane_partials(numer * prob_grad)

    nothing = jnp.zeros((ROWS, PAIR), F32)
    chunks = own_start // block + 1
    total, product = lax.fori_loop(0, chunks, own_sums, (nothing, nothing))
    inverse = 1.0 / jnp.sum(total, axis=-1, keepdims=True)
    delta = jnp.sum(product, axis=-1, keepdims=True) * inverse

    def own_results(at, mine):
        keys, numer, prob_grad = own_chunk(at)
        key_scaled, value = masked_halves(keys)
        prob = numer * inverse
        score_grad = (prob * (prob_grad - delta)).astype(BF)
        return mine + plain(score_grad, key_scaled) + plain(prob.astype(BF), value)

    mine = lax.fori_loop(0, chunks, own_results, nothing)

    parts = []
    for tile, unit, factor in (
        (mine, own_left, factor_ref[:, :PAIR]),
        (own_grad[...], own_right, factor_ref[:, PAIR:]),
    ):
        back = pair_norm_back(tile, unit.astype(F32), factor, low)
        parts.append(jnp.where(low, back, tile))
    parts = jnp.concatenate(parts, axis=1).astype(BF)
    peers = send_ref.shape[0]
    normed_grad = last_last(parts, in_w_ref[...]).reshape(peers, COARSE, D)
    mixed = plain(parts, out_w_ref[...]).reshape(peers, COARSE, D)
    send_ref[...] = jnp.concatenate([normed_grad, mixed], axis=1).astype(BF)


def coarse_finish_kernel(got_ref, message_ref, cg_ref, spread_ref, first_ref, state_ref):
    summed = jnp.sum(got_ref[...].astype(F32), axis=0)
    pooled = message_ref[0].astype(F32)[:COARSE]
    normed, factor = row_norm(pooled)
    pooled_grad = cg_ref[...] + row_norm_back(summed[:COARSE], normed, factor)
    spread = pooled_grad * (1.0 / POOL)
    spread_ref[...] = spread
    first_ref[...] = spread[:1]
    state_ref[...] = pooled + summed[COARSE:]


def fine_backward_kernel(
    place_ref, cot_ref, spread_ref, next_ref, out_w_ref, w_ref, q_ref, k_ref, v_ref, qf_ref, kf_ref, p_ref,
    att_ref,
    back1, back2, back3, back4, own_ref, hg_ref, hidden_grad, acc,
):
    low = low_lanes()
    block = (lax.broadcasted_iota(jnp.int32, (ROWS, 1), 0) + (POOL - 1)) // POOL
    added = jnp.zeros((ROWS, D), F32)
    for at in range(COARSE):
        added = jnp.where(block == at, spread_ref[at : at + 1, :], added)
    added = jnp.where(block == COARSE, next_ref[0:1, :], added)
    total = cot_ref[...].astype(F32) + added
    hg_ref[...] = total
    hidden_grad[...] = total.astype(BF)
    acc[...] = jnp.zeros_like(acc)

    def one_step(step, carry):
        first = pl.multiple_of(step * WIDTH, WIDTH)
        here = pl.ds(first, WIDTH)
        att_grads = last_last(hidden_grad[...], out_w_ref[here, :]).astype(BF).astype(F32)
        query_grads, key_grads, value_grads = [], [], []
        for part in range(0, WIDTH, PAIR):
            outer = pl.ds(pl.multiple_of(first + part, PAIR), PAIR)
            att_grad = att_grads[:, part : part + PAIR]
            delta_all = att_grad * att_ref[:, outer].astype(F32)
            value = v_ref[:, outer]
            key_wide = k_ref[:, outer].astype(F32)
            query_wide = q_ref[:, outer].astype(F32)
            grad = jnp.concatenate(
                [jnp.where(low, att_grad, 0.0), jnp.where(low, 0.0, att_grad)], axis=0
            ).astype(BF)
            delta = jnp.sum(
                jnp.concatenate(
                    [jnp.where(low, delta_all, 0.0), jnp.where(low, 0.0, delta_all)], axis=0
                ),
                axis=-1,
                keepdims=True,
            )
            scaled = query_wide * SCALE
            query = jnp.concatenate(
                [jnp.where(low, scaled, 0.0), jnp.where(low, 0.0, scaled)], axis=0
            ).astype(BF)
            head = (first + part) // HEAD_DIM
            prob = p_ref[pl.ds(head, 2)].reshape(2 * ROWS, OWN_KEYS)
            score_grad = (prob.astype(F32) * (last_last(grad, value) - delta)).astype(BF)
            twice = plain(score_grad, (key_wide * SCALE).astype(BF))
            query_grad = jnp.where(low, twice[:ROWS], twice[ROWS:])
            key_grad = first_first(score_grad, query)
            value_grad = first_first(prob, grad)
            query_grads.append(pair_norm_back(query_grad, query_wide, qf_ref[:, outer], low).astype(BF))
            key_grads.append(pair_norm_back(key_grad, key_wide, kf_ref[:, outer], low).astype(BF))
            value_grads.append(value_grad.astype(BF))
        both = jnp.concatenate(key_grads + value_grads, axis=1)
        acc[...] += last_last(
            both, jnp.concatenate([w_ref[1, :, here], w_ref[2, :, here]], axis=1)
        )
        acc[HALO:, :] += last_last(jnp.concatenate(query_grads, axis=1), w_ref[0, :, here])
        return carry

    lax.fori_loop(0, D // WIDTH, one_step, 0, unroll=True)
    backs = (back1, back2, back3, back4)
    for distance, ref in enumerate(backs, 1):
        slot = lax.rem(place_ref[1] + (len(backs) - distance), len(backs))
        ref[...] = acc[pl.ds(pl.multiple_of(slot * ROWS, ROWS), ROWS), :].astype(BF)
    own_ref[...] = acc[HALO:, :]


def halo_send_kernel(place_ref, own_ref, before_ref, send_ref):
    send_ref[0] = jnp.where(place_ref[1] < pl.program_id(0), own_ref[...], before_ref[...])


def repeated_kernel(block_ref, send_ref):
    for peer in range(send_ref.shape[0]):
        send_ref[peer] = block_ref[...]


def fine_finish_kernel(own_ref, a1, a2, a3, a4, hg_ref, tokens_ref, out_ref):
    total = own_ref[...]
    for ref in (a1, a2, a3, a4):
        total = total + ref[...].astype(F32)
    normed, factor = row_norm(tokens_ref[...].astype(F32))
    out_ref[...] = (hg_ref[...] + row_norm_back(total, normed, factor)).astype(BF)


def whole(shape):
    return pl.BlockSpec(shape, lambda *_: (0,) * len(shape))


def columns(rows, width):
    return pl.BlockSpec((rows, width), lambda p: (0, p))


def shaped(shape, kind):
    return jax.ShapeDtypeStruct(shape, kind)


def params(mib):
    return pltpu.CompilerParams(vmem_limit_bytes=mib << 20)


def cost(flops, moved, exps=0):
    return pl.CostEstimate(flops=flops, bytes_accessed=moved, transcendentals=exps)


SCALAR = pl.BlockSpec(memory_space=pltpu.SMEM)
IN_VMEM = pl.BlockSpec(memory_space=pltpu.VMEM)
WIDTH = 4 * PAIR


def in_hbm(x):
    return pltpu.with_memory_space_constraint(x, pltpu.HBM)


def fine_prepare(place, tokens, cotangent, weights, fine_out):
    anywhere = pl.BlockSpec(memory_space=pltpu.HBM)
    return pl.pallas_call(
        fine_prepare_kernel,
        in_specs=[SCALAR] + [anywhere] * 4,
        out_specs=[IN_VMEM] * 10,
        out_shape=[
            pltpu.VMEM((ROWS, D), BF),
            pltpu.VMEM((3, D, D), BF),
            pltpu.VMEM((D, D), BF),
            pltpu.VMEM((ROWS, D), BF),
            pltpu.VMEM((ROWS, D), BF),
            pltpu.VMEM((ROWS, D), BF),
            pltpu.VMEM((ROWS, D), F32),
            pltpu.VMEM((ROWS, D), F32),
            pltpu.VMEM((2 * QUERIES, ALL_KEYS), F32),
            pltpu.VMEM((COARSE, D), F32),
        ],
        scratch_shapes=[pltpu.VMEM((ROWS, D), BF), pltpu.SemaphoreType.DMA((4,))],
        compiler_params=params(16),
        cost_estimate=cost(900_000_000, 17_000_000),
        name="fine_prepare",
    )(place, *(in_hbm(x) for x in (tokens, cotangent, weights, fine_out)))


def fine_forward(place, tail, slots, own, weights, fine_out, own_q, own_k, own_v, own_kf, bias, cg, peers):
    return pl.pallas_call(
        fine_forward_kernel,
        in_specs=[SCALAR] + [IN_VMEM] * 11,
        out_specs=[IN_VMEM] * 7,
        out_shape=[
            pltpu.VMEM((OWN_KEYS, D), BF),
            pltpu.VMEM((OWN_KEYS, D), BF),
            pltpu.VMEM((OWN_KEYS, D), F32),
            pltpu.VMEM((HEADS, ROWS, OWN_KEYS), BF),
            pltpu.VMEM((ROWS, D), BF),
            shaped((ROWS, D), BF),
            shaped((peers, 2 * COARSE, D), BF),
        ],
        scratch_shapes=[pltpu.VMEM((HALO + EXTRA, D), BF), pltpu.VMEM((QUERIES, D), F32)],
        compiler_params=params(16),
        cost_estimate=cost(4_500_000_000, 20_000_000, 1_600_000),
        name="fine_forward",
    )(place, tail, slots, own, weights, fine_out, own_q, own_k, own_v, own_kf, bias, cg)


def coarse_prepare(core, weights, back):
    return pl.pallas_call(
        coarse_prepare_kernel,
        in_specs=[SCALAR, IN_VMEM, IN_VMEM],
        out_specs=[IN_VMEM] * 2,
        out_shape=[shaped((D, 2 * PAIR), BF), shaped((2 * PAIR, D), BF)],
        compiler_params=params(8),
        cost_estimate=cost(1_000_000, 2_500_000),
        name="coarse_prepare",
    )(core, weights, back)


def coarse_project(gathered, coarse_in, coarse_back, groups):
    rows = gathered.shape[0] * COARSE
    return pl.pallas_call(
        coarse_project_kernel,
        out_shape=[shaped((groups, rows, 2 * PAIR), BF), shaped((rows, 2 * PAIR), F32)],
        compiler_params=params(VMEM_MIB),
        cost_estimate=cost(140_000_000, 3_000_000),
        name="coarse_project",
    )(gathered, coarse_in, coarse_back)


def coarse_attention(place, everyone, factor, coarse_in, coarse_back):
    rows = factor.shape[0]
    return pl.pallas_call(
        coarse_attention_kernel,
        in_specs=[SCALAR] + [IN_VMEM] * 4,
        out_shape=shaped((rows // COARSE, 2 * COARSE, D), BF),
        scratch_shapes=[pltpu.VMEM((rows, PAIR), F32)],
        compiler_params=params(VMEM_MIB),
        cost_estimate=cost(1_500_000_000, 3_000_000, 3_000_000),
        name="coarse_attention",
    )(place, everyone, factor, coarse_in, coarse_back)


def coarse_finish(returned, message, coarse_grad):
    return pl.pallas_call(
        coarse_finish_kernel,
        grid=(1,),
        in_specs=[whole(returned.shape), whole((1, 2 * COARSE, D)), whole((COARSE, D))],
        out_specs=[whole((COARSE, D)), whole((1, D)), whole((COARSE, D))],
        out_shape=[shaped((COARSE, D), F32), shaped((1, D), F32), shaped((COARSE, D), F32)],
        compiler_params=params(VMEM_MIB),
        cost_estimate=cost(1_000_000, 1_000_000),
        name="coarse_finish",
    )(returned, message, coarse_grad)


def fine_backward(
    place, cotangent, spread, after, fine_out, weights, query, key, value, q_factor, k_factor, probs,
    attended,
):
    return pl.pallas_call(
        fine_backward_kernel,
        in_specs=[SCALAR] + [IN_VMEM] * 12,
        out_specs=[IN_VMEM] * 6,
        out_shape=[shaped((ROWS, D), BF)] * 4 + [shaped((ROWS, D), F32)] * 2,
        scratch_shapes=[pltpu.VMEM((ROWS, D), BF), pltpu.VMEM((OWN_KEYS, D), F32)],
        compiler_params=params(16),
        cost_estimate=cost(5_000_000_000, 20_000_000),
        name="fine_backward",
    )(
        place, cotangent, spread, after, fine_out, weights, query, key, value, q_factor, k_factor, probs,
        attended,
    )


def halo_send(place, own, before, count):
    return pl.pallas_call(
        halo_send_kernel,
        grid=(count,),
        in_specs=[SCALAR, whole((ROWS, D)), whole((ROWS, D))],
        out_specs=pl.BlockSpec((1, ROWS, D), lambda p: (p, 0, 0)),
        out_shape=shaped((count, ROWS, D), BF),
        compiler_params=params(8),
        cost_estimate=cost(1_000_000, 1_500_000),
        name="halo_send",
    )(place, own, before)


def repeated(block, count):
    return pl.pallas_call(
        repeated_kernel,
        out_shape=shaped((count, *block.shape), BF),
        compiler_params=params(VMEM_MIB),
        cost_estimate=cost(1_000_000, 1_300_000),
        name="repeated",
    )(block)


def fine_finish(own, arrived, hidden_grad, tokens):
    return pl.pallas_call(
        fine_finish_kernel,
        out_shape=shaped((ROWS, D), BF),
        compiler_params=params(VMEM_MIB),
        cost_estimate=cost(1_000_000, 3_000_000),
        name="fine_finish",
    )(own, *arrived, hidden_grad, tokens)


def per_device(tokens, cotangent, fine_qkv, fine_out, coarse_qkv, coarse_out):
    peers = 1
    for name in GROUP:
        peers *= lax.axis_size(name)
    groups = 1
    for name in FAR:
        groups *= lax.axis_size(name)
    weights = jnp.transpose(fine_qkv, (1, 0, 2))
    core = lax.axis_index("core").astype(jnp.int32).reshape(1)
    column_at = lax.axis_index("x")
    columns_along = lax.axis_size("x")
    tail = shifted_by(tokens[ROWS - EXTRA :], columns_along + 1)
    row_before = shifted_by(tokens, columns_along)
    group_start = lax.axis_index(FAR) * (peers * COARSE)
    place = jnp.stack([lax.axis_index(LINE) * ROWS, column_at, group_start]).astype(jnp.int32)
    prepared = fine_prepare(place, tokens, cotangent, weights, fine_out)
    coarse_weights = coarse_prepare(core, jnp.transpose(coarse_qkv, (1, 0, 2)), coarse_out)
    tail, row_before, prepared, coarse_weights, place = lax.optimization_barrier(
        (tail, row_before, prepared, coarse_weights, place)
    )
    own, weights, fine_out, query, own_key, own_value, q_factor, own_k_factor, bias, coarse_grad = prepared
    coarse_in, coarse_back = coarse_weights
    slots = exchanged(halo_send(place, own, row_before, columns_along), "x")
    key, value, k_factor, probs, attended, hidden, message = fine_forward(
        place, tail, slots, own, weights, fine_out, query, own_key, own_value, own_k_factor, bias,
        coarse_grad, peers,
    )
    gathered = exchanged(message, GROUP)
    near, further = lax.axis_size("z_hi"), lax.axis_size("y")
    coarse_send, coarse_factor = coarse_project(gathered, coarse_in, coarse_back, near)
    group_rows = coarse_factor.shape[0]
    nearby = exchanged(coarse_send, "z_hi").reshape(near * group_rows, 2 * PAIR)
    everyone = exchanged(repeated(nearby, further), "y").reshape(groups * group_rows, 2 * PAIR)
    partial = coarse_attention(place, everyone, coarse_factor, coarse_in, coarse_back)
    returned = exchanged(partial, GROUP)
    spread, first, state = coarse_finish(returned, message, coarse_grad)
    after = shifted_by(first, -1)
    output = (
        hidden.astype(F32) + jnp.repeat(state.astype(BF), POOL, axis=0).astype(F32)
    ).astype(BF)
    *backs, own_grad, hidden_grad = fine_backward(
        place, cotangent, spread, after, fine_out, weights, query, key, value, q_factor, k_factor, probs,
        attended,
    )
    arrived = [shifted_by(backs[steps - 1], -steps) for steps in range(len(backs), 0, -1)]
    return (output, fine_finish(own_grad, arrived, hidden_grad, own))


def solution(mesh):
    sizes = (4, 4, 2, 2, 4)
    fine_mesh = Mesh(mesh.devices.reshape(sizes), LINE)
    placed = (
        P(LINE, None),
        P(LINE, None),
        P(),
        P(),
        P(None, None, ("z_lo", "x")),
        P(("z_lo", "x"), None),
    )
    return jax.shard_map(
        per_device,
        mesh=fine_mesh,
        in_specs=placed,
        out_specs=(P(LINE, None), P(LINE, None)),
        check_vma=False,
    )
```

```python
import jax
import jax.numpy as jnp
from jax import lax
from jax.experimental import pallas as pl
from jax.experimental.pallas import tpu as pltpu
from jax.sharding import Mesh
from jax.sharding import PartitionSpec as P

D = 1024
HEADS = 16
HEAD_DIM = 64
WINDOW = 512
POOL = 16
EPS = 1e-06

LINE = ("y", "z_hi", "core", "z_lo", "x")
GROUP = ("core", "z_lo", "x")
FAR = ("y", "z_hi")

ROWS = 128
HALO = WINDOW
OWN_KEYS = HALO + ROWS
EXTRA = 16
ALL_KEYS = OWN_KEYS + EXTRA
QUERIES = EXTRA + ROWS
PAIR = 2 * HEAD_DIM
COARSE = ROWS // POOL
SCALE = HEAD_DIM ** (-0.5)
NEG = -1e30
VMEM_MIB = 16

BF = jnp.bfloat16
F32 = jnp.float32


def shifted_by(value, steps):
    count = 1
    for name in LINE:
        count *= lax.axis_size(name)
    first, last = (max(0, -steps), min(count, count - steps))
    return lax.ppermute(value, LINE, [(source, source + steps) for source in range(first, last)])


def exchanged(pieces, axes):
    return lax.all_to_all(pieces, axes, 0, 0, tiled=True)


def last_last(left, right):
    return lax.dot_general(left, right, (((1,), (1,)), ((), ())), preferred_element_type=F32)


def first_first(left, right):
    return lax.dot_general(left, right, (((0,), (0,)), ((), ())), preferred_element_type=F32)


def plain(left, right):
    return jnp.dot(left, right, preferred_element_type=F32)


def low_lanes():
    return lax.broadcasted_iota(jnp.int32, (1, PAIR), 1) < HEAD_DIM


def pair_sums(values, low):
    low_sum = jnp.sum(jnp.where(low, values, 0.0), axis=-1, keepdims=True)
    high_sum = jnp.sum(jnp.where(low, 0.0, values), axis=-1, keepdims=True)
    return jnp.where(low, low_sum, high_sum)


def pair_norm(values, low):
    factor = lax.rsqrt(pair_sums(values * values, low) * (1.0 / HEAD_DIM) + EPS)
    return values * factor, factor


def pair_norm_back(grad, unit, factor, low):
    return factor * (grad - unit * (pair_sums(unit * grad, low) * (1.0 / HEAD_DIM)))


def row_norm(rows):
    factor = lax.rsqrt(jnp.mean(rows * rows, axis=-1, keepdims=True) + EPS)
    return rows * factor, factor


def row_norm_back(grad, normed, factor):
    return factor * (grad - normed * jnp.mean(normed * grad, axis=-1, keepdims=True))


def fine_prepare_kernel(
    place_ref, own_hbm, cot_hbm, w_hbm, out_w_hbm,
    own_ref, w_ref, out_w_ref, q_ref, k_ref, v_ref, qf_ref, kf_ref, bias_ref, cg_ref,
    cot, copied,
):
    anchor = place_ref[0]
    column_at = place_ref[1]
    low = low_lanes()
    copies = [
        pltpu.make_async_copy(source, target, copied.at[at])
        for at, (source, target) in enumerate(
            ((own_hbm, own_ref), (cot_hbm, cot), (w_hbm, w_ref), (out_w_hbm, out_w_ref))
        )
    ]
    for copy in copies:
        copy.start()

    row = lax.broadcasted_iota(jnp.int32, (2 * QUERIES, ALL_KEYS), 0)
    query_pos = jnp.where(row < QUERIES, row, row - QUERIES) - EXTRA
    column = lax.broadcasted_iota(jnp.int32, (2 * QUERIES, ALL_KEYS), 1)
    turned = column_at * ROWS
    halo_pos = column - jnp.where(column >= turned, turned + HALO, turned)
    key_pos = jnp.where(
        column < HALO,
        halo_pos,
        jnp.where(column < OWN_KEYS, column - HALO, column - (OWN_KEYS + HALO + EXTRA)),
    )
    gap = query_pos - key_pos
    allowed = (gap >= 0) & (gap < WINDOW) & (anchor + key_pos >= 0)
    bias_ref[...] = jnp.where(allowed, 0.0, NEG)

    copies[0].wait()
    normed = row_norm(own_ref[...].astype(F32))[0].astype(BF)
    copies[1].wait()
    chunk = lax.broadcasted_iota(jnp.int32, (COARSE, ROWS), 0) * POOL
    row = lax.broadcasted_iota(jnp.int32, (COARSE, ROWS), 1)
    member = jnp.where((row >= chunk) & (row < chunk + POOL), 1.0, 0.0).astype(BF)
    cg_ref[...] = plain(member, cot[...])
    copies[2].wait()
    for at in range(0, D, WIDTH):
        here = slice(at, at + WIDTH)
        queries = plain(normed, w_ref[0, :, here])
        keys = plain(normed, w_ref[1, :, here])
        v_ref[:, here] = plain(normed, w_ref[2, :, here]).astype(BF)
        for part in range(0, WIDTH, PAIR):
            inner = slice(part, part + PAIR)
            outer = slice(at + part, at + part + PAIR)
            query, q_factor = pair_norm(queries[:, inner], low)
            key, k_factor = pair_norm(keys[:, inner], low)
            q_ref[:, outer] = query.astype(BF)
            k_ref[:, outer] = key.astype(BF)
            qf_ref[:, outer] = q_factor
            kf_ref[:, outer] = k_factor
    copies[3].wait()


def fine_forward_kernel(
    place_ref, tail_ref, slots_ref, own_ref, w_ref, out_w_ref, own_q_ref, own_k_ref, own_v_ref,
    own_qf_ref, own_kf_ref, bias, cg_ref,
    q_ref, k_ref, v_ref, qf_ref, kf_ref, p_ref, att_ref, hid_ref, send_ref,
    normed, acc,
):
    anchor = place_ref[0]
    column_at = place_ref[1]
    low = low_lanes()
    slots = slots_ref.shape[0]
    nearest = lax.rem(column_at + (slots - 1), slots)
    for slot in range(slots):
        at = slot * ROWS
        normed[at : at + ROWS, :] = row_norm(slots_ref[slot].astype(F32))[0].astype(BF)
    normed[HALO:, :] = row_norm(tail_ref[...].astype(F32))[0].astype(BF)
    acc[...] = jnp.zeros_like(acc)
    extra_at = pl.multiple_of(nearest * ROWS + (ROWS - EXTRA), EXTRA)

    def one_step(step, carry):
        first = pl.multiple_of(step * WIDTH, WIDTH)
        here = pl.ds(first, WIDTH)
        extra = plain(normed[pl.ds(extra_at, EXTRA), :], w_ref[0, :, here])
        both = plain(
            normed[...], jnp.concatenate([w_ref[1, :, here], w_ref[2, :, here]], axis=1)
        )
        own_q, own_k, own_v = own_q_ref[:, here], own_k_ref[:, here], own_v_ref[:, here]
        own_kf = own_kf_ref[:, here]
        mixed = []
        for part in range(0, WIDTH, PAIR):
            inner = slice(part, part + PAIR)
            outer = pl.ds(pl.multiple_of(first + part, PAIR), PAIR)
            key, k_factor = pair_norm(both[:, inner], low)
            key = key.astype(BF)
            value = both[:, WIDTH + part : WIDTH + part + PAIR].astype(BF)
            key = jnp.concatenate([key[:HALO], own_k[:, inner], key[HALO:]], axis=0)
            value = jnp.concatenate([value[:HALO], own_v[:, inner], value[HALO:]], axis=0)
            k_ref[:, outer] = key
            v_ref[:, outer] = value
            kf_ref[:HALO, outer] = k_factor[:HALO]
            kf_ref[HALO:OWN_KEYS, outer] = own_kf[:, inner]
            kf_ref[OWN_KEYS:, outer] = k_factor[HALO:]
            before, before_factor = pair_norm(extra[:, inner], low)
            query = jnp.concatenate([before.astype(BF), own_q[:, inner]], axis=0)
            q_ref[:, outer] = query
            qf_ref[:EXTRA, outer] = before_factor
            qf_ref[EXTRA:, outer] = own_qf_ref[:, outer]
            scaled = query.astype(F32) * SCALE
            stacked = jnp.concatenate(
                [jnp.where(low, scaled, 0.0), jnp.where(low, 0.0, scaled)], axis=0
            )
            numer = jnp.exp(last_last(stacked.astype(BF), key) + bias[...])
            total = jnp.sum(numer, axis=-1, keepdims=True)
            prob = (numer * (1.0 / jnp.where(total > 0.0, total, 1.0))).astype(BF)
            head = (first + part) // HEAD_DIM
            p_ref[head] = prob[:QUERIES]
            p_ref[head + 1] = prob[QUERIES:]
            twice = plain(prob, value)
            attended = jnp.where(low, twice[:QUERIES], twice[QUERIES:]).astype(BF)
            att_ref[:, outer] = attended
            mixed.append(attended)
        acc[...] += plain(jnp.concatenate(mixed, axis=1), out_w_ref[here, :])
        return carry

    lax.fori_loop(0, D // WIDTH, one_step, 0, unroll=True)
    before = slots_ref[nearest, ROWS - EXTRA :, :].astype(F32) + acc[:EXTRA, :]
    before = jnp.where(anchor > 0, before, 0.0).astype(BF)
    own = (own_ref[...].astype(F32) + acc[EXTRA:, :]).astype(BF)
    hid_ref[...] = own
    chunk = lax.broadcasted_iota(jnp.int32, (COARSE, QUERIES), 0) * POOL
    row = lax.broadcasted_iota(jnp.int32, (COARSE, QUERIES), 1)
    member = jnp.where((row > chunk) & (row <= chunk + POOL), 1.0, 0.0).astype(BF)
    pooled = plain(member, jnp.concatenate([before, own], axis=0)) * (1.0 / POOL)
    message = jnp.concatenate([pooled, cg_ref[...]], axis=0).astype(BF)
    for peer in range(send_ref.shape[0]):
        send_ref[peer] = message


def coarse_prepare_kernel(core_ref, w_ref, back_ref, in_ref, out_ref):
    low = low_lanes()
    second = core_ref[0] > 0
    parts = [w_ref[at].astype(F32) for at in range(3)]
    turned = [pltpu.roll(part, HEAD_DIM, 1) for part in parts]
    query = jnp.where(second, turned[0], parts[0])
    key = jnp.where(second, turned[1], parts[1])
    value = jnp.where(second, parts[2], turned[2])
    in_ref[:, :PAIR] = jnp.where(low, query, 0.0).astype(BF)
    in_ref[:, PAIR:] = jnp.where(low, key, value).astype(BF)
    out_ref[...] = jnp.zeros_like(out_ref)
    out_ref[HEAD_DIM:PAIR, :] = jnp.where(second, back_ref[HEAD_DIM:, :], back_ref[:HEAD_DIM, :])


def coarse_project_kernel(got_ref, in_w_ref, out_w_ref, send_ref, factor_ref):
    low = low_lanes()
    rows = got_ref[...].astype(F32)
    count = rows.shape[0] * COARSE
    pooled = rows[:, :COARSE, :].reshape(count, D)
    coarse_grad = rows[:, COARSE:, :].reshape(count, D)
    normed = row_norm(pooled)[0].astype(BF)
    raw = plain(normed, in_w_ref[...]) + last_last(coarse_grad.astype(BF), out_w_ref[...])
    units, factors = [], []
    for tile in (raw[:, :PAIR], raw[:, PAIR:]):
        unit, factor = pair_norm(tile, low)
        units.append(jnp.where(low, unit, tile))
        factors.append(factor)
    message = jnp.concatenate(units, axis=1).astype(BF)
    factor_ref[...] = jnp.concatenate(factors, axis=1)
    for peer in range(send_ref.shape[0]):
        send_ref[peer] = message


def coarse_attention_kernel(place_ref, got_ref, factor_ref, in_w_ref, out_w_ref, send_ref, own_grad):
    low = low_lanes()
    own_start = pl.multiple_of(place_ref[2], ROWS)
    length = got_ref.shape[0]
    block = 512
    own_left = got_ref[pl.ds(own_start, ROWS), :PAIR]
    own_right = got_ref[pl.ds(own_start, ROWS), PAIR:]
    own_grad[...] = jnp.zeros_like(own_grad)

    def masked_halves(tile):
        wide = tile.astype(F32)
        return (
            jnp.where(low, wide * SCALE, 0.0).astype(BF),
            jnp.where(low, 0.0, wide).astype(BF),
        )

    def lane_partials(values):
        total = values[:, :PAIR]
        for at in range(PAIR, values.shape[1], PAIR):
            total = total + values[:, at : at + PAIR]
        return total

    def one_block(index):
        first = index * block
        query, grad = masked_halves(got_ref[first : first + block, :PAIR])
        stacked = jnp.concatenate([query, grad], axis=0)

        def scored(keys):
            both = last_last(stacked, keys)
            return jnp.exp(both[:block]), both[block:]

        query_at = lax.broadcasted_iota(jnp.int32, (block, 1), 0)
        total = product = None
        for at in range(index + 1):
            numer, prob_grad = scored(got_ref[at * block : (at + 1) * block, PAIR:])
            if at == index:
                key_at = lax.broadcasted_iota(jnp.int32, (1, block), 1)
                numer = jnp.where(key_at <= query_at, numer, 0.0)
            sums = lane_partials(numer), lane_partials(numer * prob_grad)
            total, product = sums if at == 0 else (total + sums[0], product + sums[1])
        inverse = 1.0 / jnp.sum(total, axis=-1, keepdims=True)
        delta = jnp.sum(product, axis=-1, keepdims=True) * inverse
        own_pos = own_start + lax.broadcasted_iota(jnp.int32, (1, ROWS), 1)
        numer, prob_grad = scored(own_right)
        numer = jnp.where(own_pos <= query_at + first, numer, 0.0)
        prob = numer * inverse
        score_grad = (prob * (prob_grad - delta)).astype(BF)
        own_grad[...] += first_first(
            jnp.concatenate([score_grad, prob.astype(BF)], axis=0), stacked
        )

    for index in range(length // block):
        pl.when(own_start < (index + 1) * block)(lambda index=index: one_block(index))

    query, grad = masked_halves(own_left)
    stacked = jnp.concatenate([query, grad], axis=0)
    query_pos = own_start + lax.broadcasted_iota(jnp.int32, (ROWS, 1), 0)

    def own_chunk(at):
        key_start = pl.multiple_of(at * block, block)
        keys = got_ref[pl.ds(key_start, block), PAIR:]
        both = last_last(stacked, keys)
        key_pos = key_start + lax.broadcasted_iota(jnp.int32, (1, block), 1)
        return keys, jnp.where(key_pos <= query_pos, jnp.exp(both[:ROWS]), 0.0), both[ROWS:]

    def own_sums(at, sums):
        numer, prob_grad = own_chunk(at)[1:]
        return sums[0] + lane_partials(numer), sums[1] + lane_partials(numer * prob_grad)

    nothing = jnp.zeros((ROWS, PAIR), F32)
    chunks = own_start // block + 1
    total, product = lax.fori_loop(0, chunks, own_sums, (nothing, nothing))
    inverse = 1.0 / jnp.sum(total, axis=-1, keepdims=True)
    delta = jnp.sum(product, axis=-1, keepdims=True) * inverse

    def own_results(at, mine):
        keys, numer, prob_grad = own_chunk(at)
        key_scaled, value = masked_halves(keys)
        prob = numer * inverse
        score_grad = (prob * (prob_grad - delta)).astype(BF)
        return mine + plain(score_grad, key_scaled) + plain(prob.astype(BF), value)

    mine = lax.fori_loop(0, chunks, own_results, nothing)

    parts = []
    for tile, unit, factor in (
        (mine, own_left, factor_ref[:, :PAIR]),
        (own_grad[...], own_right, factor_ref[:, PAIR:]),
    ):
        back = pair_norm_back(tile, unit.astype(F32), factor, low)
        parts.append(jnp.where(low, back, tile))
    parts = jnp.concatenate(parts, axis=1).astype(BF)
    peers = send_ref.shape[0]
    normed_grad = last_last(parts, in_w_ref[...]).reshape(peers, COARSE, D)
    mixed = plain(parts, out_w_ref[...]).reshape(peers, COARSE, D)
    send_ref[...] = jnp.concatenate([normed_grad, mixed], axis=1).astype(BF)


def coarse_finish_kernel(got_ref, message_ref, cg_ref, spread_ref, state_ref):
    summed = jnp.sum(got_ref[...].astype(F32), axis=0)
    pooled = message_ref[0].astype(F32)[:COARSE]
    normed, factor = row_norm(pooled)
    pooled_grad = cg_ref[...] + row_norm_back(summed[:COARSE], normed, factor)
    spread_ref[...] = pooled_grad * (1.0 / POOL)
    state_ref[...] = pooled + summed[COARSE:]


def fine_backward_kernel(
    place_ref, cot_ref, spread_ref, out_w_ref, w_ref, q_ref, k_ref, v_ref, qf_ref, kf_ref, p_ref,
    att_ref,
    back1, back2, back3, back4, tail_ref, own_ref, hg_ref, hidden_grad, acc,
):
    low = low_lanes()
    block = (lax.broadcasted_iota(jnp.int32, (ROWS, 1), 0) + (POOL - 1)) // POOL
    added = jnp.zeros((ROWS, D), F32)
    for at in range(COARSE):
        added = jnp.where(block == at, spread_ref[at : at + 1, :], added)
    total = cot_ref[...].astype(F32) + added
    hg_ref[...] = total
    counted = lax.broadcasted_iota(jnp.int32, (EXTRA, 1), 0) > EXTRA - POOL
    hidden_grad[:EXTRA, :] = jnp.where(counted, spread_ref[0:1, :], 0.0).astype(BF)
    hidden_grad[EXTRA:, :] = total.astype(BF)
    backs = (back1, back2, back3, back4)
    slots = len(backs)
    nearest = lax.rem(place_ref[1] + (slots - 1), slots)
    extra_at = pl.multiple_of(nearest * ROWS + (ROWS - EXTRA), EXTRA)
    acc[...] = jnp.zeros_like(acc)

    def one_step(step, carry):
        first = pl.multiple_of(step * WIDTH, WIDTH)
        here = pl.ds(first, WIDTH)
        att_grads = last_last(hidden_grad[...], out_w_ref[here, :]).astype(BF).astype(F32)
        query_grads, key_grads, value_grads = [], [], []
        for part in range(0, WIDTH, PAIR):
            outer = pl.ds(pl.multiple_of(first + part, PAIR), PAIR)
            att_grad = att_grads[:, part : part + PAIR]
            delta_all = att_grad * att_ref[:, outer].astype(F32)
            value = v_ref[:, outer]
            key_wide = k_ref[:, outer].astype(F32)
            query_wide = q_ref[:, outer].astype(F32)
            grad = jnp.concatenate(
                [jnp.where(low, att_grad, 0.0), jnp.where(low, 0.0, att_grad)], axis=0
            ).astype(BF)
            delta = jnp.sum(
                jnp.concatenate(
                    [jnp.where(low, delta_all, 0.0), jnp.where(low, 0.0, delta_all)], axis=0
                ),
                axis=-1,
                keepdims=True,
            )
            scaled = query_wide * SCALE
            query = jnp.concatenate(
                [jnp.where(low, scaled, 0.0), jnp.where(low, 0.0, scaled)], axis=0
            ).astype(BF)
            head = (first + part) // HEAD_DIM
            prob = p_ref[pl.ds(head, 2)].reshape(2 * QUERIES, ALL_KEYS)
            score_grad = (prob.astype(F32) * (last_last(grad, value) - delta)).astype(BF)
            twice = plain(score_grad, (key_wide * SCALE).astype(BF))
            query_grad = jnp.where(low, twice[:QUERIES], twice[QUERIES:])
            key_grad = first_first(score_grad, query)
            value_grad = first_first(prob, grad)
            query_grads.append(pair_norm_back(query_grad, query_wide, qf_ref[:, outer], low).astype(BF))
            key_grads.append(pair_norm_back(key_grad, key_wide, kf_ref[:, outer], low).astype(BF))
            value_grads.append(value_grad.astype(BF))
        both = jnp.concatenate(key_grads + value_grads, axis=1)
        acc[...] += last_last(
            both, jnp.concatenate([w_ref[1, :, here], w_ref[2, :, here]], axis=1)
        )
        from_query = last_last(jnp.concatenate(query_grads, axis=1), w_ref[0, :, here])
        acc[pl.ds(extra_at, EXTRA), :] += from_query[:EXTRA]
        acc[HALO:OWN_KEYS, :] += from_query[EXTRA:]
        return carry

    lax.fori_loop(0, D // WIDTH, one_step, 0, unroll=True)
    for distance, ref in enumerate(backs, 1):
        slot = lax.rem(place_ref[1] + (slots - distance), slots)
        ref[:ROWS, :] = acc[pl.ds(pl.multiple_of(slot * ROWS, ROWS), ROWS), :].astype(BF)
    back1[ROWS:, :] = jnp.broadcast_to(spread_ref[0:1, :], (EXTRA, D)).astype(BF)
    tail_ref[...] = acc[OWN_KEYS:, :].astype(BF)
    own_ref[...] = acc[HALO:OWN_KEYS, :]


def halo_send_kernel(place_ref, own_ref, before_ref, send_ref):
    send_ref[0] = jnp.where(place_ref[1] < pl.program_id(0), own_ref[...], before_ref[...])


def repeated_kernel(block_ref, send_ref):
    for peer in range(send_ref.shape[0]):
        send_ref[peer] = block_ref[...]


def fine_finish_kernel(own_ref, a1, a2, a3, a4, tail_ref, hg_ref, tokens_ref, out_ref):
    total = own_ref[...]
    for ref in (a1, a2, a3, a4):
        total = total + ref[:ROWS, :].astype(F32)
    split = ROWS - EXTRA
    total = jnp.concatenate([total[:split], total[split:] + tail_ref[...].astype(F32)], axis=0)
    normed, factor = row_norm(tokens_ref[...].astype(F32))
    after = lax.broadcasted_iota(jnp.int32, (ROWS, 1), 0) > ROWS - POOL
    hidden_grad = hg_ref[...] + jnp.where(after, a1[ROWS:, :].astype(F32)[:1], 0.0)
    out_ref[...] = (hidden_grad + row_norm_back(total, normed, factor)).astype(BF)


def whole(shape):
    return pl.BlockSpec(shape, lambda *_: (0,) * len(shape))


def columns(rows, width):
    return pl.BlockSpec((rows, width), lambda p: (0, p))


def shaped(shape, kind):
    return jax.ShapeDtypeStruct(shape, kind)


def params(mib):
    return pltpu.CompilerParams(vmem_limit_bytes=mib << 20)


def cost(flops, moved, exps=0):
    return pl.CostEstimate(flops=flops, bytes_accessed=moved, transcendentals=exps)


SCALAR = pl.BlockSpec(memory_space=pltpu.SMEM)
IN_VMEM = pl.BlockSpec(memory_space=pltpu.VMEM)
WIDTH = 4 * PAIR


def in_hbm(x):
    return pltpu.with_memory_space_constraint(x, pltpu.HBM)


def fine_prepare(place, tokens, cotangent, weights, fine_out):
    anywhere = pl.BlockSpec(memory_space=pltpu.HBM)
    return pl.pallas_call(
        fine_prepare_kernel,
        in_specs=[SCALAR] + [anywhere] * 4,
        out_specs=[IN_VMEM] * 10,
        out_shape=[
            pltpu.VMEM((ROWS, D), BF),
            pltpu.VMEM((3, D, D), BF),
            pltpu.VMEM((D, D), BF),
            pltpu.VMEM((ROWS, D), BF),
            pltpu.VMEM((ROWS, D), BF),
            pltpu.VMEM((ROWS, D), BF),
            pltpu.VMEM((ROWS, D), F32),
            pltpu.VMEM((ROWS, D), F32),
            pltpu.VMEM((2 * QUERIES, ALL_KEYS), F32),
            pltpu.VMEM((COARSE, D), F32),
        ],
        scratch_shapes=[pltpu.VMEM((ROWS, D), BF), pltpu.SemaphoreType.DMA((4,))],
        compiler_params=params(16),
        cost_estimate=cost(900_000_000, 17_000_000),
        name="fine_prepare",
    )(place, *(in_hbm(x) for x in (tokens, cotangent, weights, fine_out)))


def fine_forward(place, tail, slots, prepared, peers):
    return pl.pallas_call(
        fine_forward_kernel,
        in_specs=[SCALAR] + [IN_VMEM] * 12,
        out_specs=[IN_VMEM] * 9,
        out_shape=[
            pltpu.VMEM((QUERIES, D), BF),
            pltpu.VMEM((ALL_KEYS, D), BF),
            pltpu.VMEM((ALL_KEYS, D), BF),
            pltpu.VMEM((QUERIES, D), F32),
            pltpu.VMEM((ALL_KEYS, D), F32),
            pltpu.VMEM((HEADS, QUERIES, ALL_KEYS), BF),
            pltpu.VMEM((QUERIES, D), BF),
            shaped((ROWS, D), BF),
            shaped((peers, 2 * COARSE, D), BF),
        ],
        scratch_shapes=[pltpu.VMEM((HALO + EXTRA, D), BF), pltpu.VMEM((QUERIES, D), F32)],
        compiler_params=params(16),
        cost_estimate=cost(4_500_000_000, 20_000_000, 1_600_000),
        name="fine_forward",
    )(place, tail, slots, *prepared)


def coarse_prepare(core, weights, back):
    return pl.pallas_call(
        coarse_prepare_kernel,
        in_specs=[SCALAR, IN_VMEM, IN_VMEM],
        out_specs=[IN_VMEM] * 2,
        out_shape=[shaped((D, 2 * PAIR), BF), shaped((2 * PAIR, D), BF)],
        compiler_params=params(8),
        cost_estimate=cost(1_000_000, 2_500_000),
        name="coarse_prepare",
    )(core, weights, back)


def coarse_project(gathered, coarse_in, coarse_back, groups):
    rows = gathered.shape[0] * COARSE
    return pl.pallas_call(
        coarse_project_kernel,
        out_shape=[shaped((groups, rows, 2 * PAIR), BF), shaped((rows, 2 * PAIR), F32)],
        compiler_params=params(VMEM_MIB),
        cost_estimate=cost(140_000_000, 3_000_000),
        name="coarse_project",
    )(gathered, coarse_in, coarse_back)


def coarse_attention(place, everyone, factor, coarse_in, coarse_back):
    rows = factor.shape[0]
    return pl.pallas_call(
        coarse_attention_kernel,
        in_specs=[SCALAR] + [IN_VMEM] * 4,
        out_shape=shaped((rows // COARSE, 2 * COARSE, D), BF),
        scratch_shapes=[pltpu.VMEM((rows, PAIR), F32)],
        compiler_params=params(VMEM_MIB),
        cost_estimate=cost(1_500_000_000, 3_000_000, 3_000_000),
        name="coarse_attention",
    )(place, everyone, factor, coarse_in, coarse_back)


def coarse_finish(returned, message, coarse_grad):
    return pl.pallas_call(
        coarse_finish_kernel,
        grid=(1,),
        in_specs=[whole(returned.shape), whole((1, 2 * COARSE, D)), whole((COARSE, D))],
        out_specs=[whole((COARSE, D))] * 2,
        out_shape=[shaped((COARSE, D), F32)] * 2,
        compiler_params=params(VMEM_MIB),
        cost_estimate=cost(1_000_000, 1_000_000),
        name="coarse_finish",
    )(returned, message, coarse_grad)


def fine_backward(
    place, cotangent, spread, fine_out, weights, query, key, value, q_factor, k_factor, probs,
    attended,
):
    return pl.pallas_call(
        fine_backward_kernel,
        in_specs=[SCALAR] + [IN_VMEM] * 11,
        out_specs=[IN_VMEM] * 7,
        out_shape=[shaped((ROWS + EXTRA, D), BF)]
        + [shaped((ROWS, D), BF)] * 3
        + [shaped((EXTRA, D), BF)]
        + [shaped((ROWS, D), F32)] * 2,
        scratch_shapes=[pltpu.VMEM((QUERIES, D), BF), pltpu.VMEM((ALL_KEYS, D), F32)],
        compiler_params=params(16),
        cost_estimate=cost(5_000_000_000, 20_000_000),
        name="fine_backward",
    )(
        place, cotangent, spread, fine_out, weights, query, key, value, q_factor, k_factor, probs,
        attended,
    )


def halo_send(place, own, before, count):
    return pl.pallas_call(
        halo_send_kernel,
        grid=(count,),
        in_specs=[SCALAR, whole((ROWS, D)), whole((ROWS, D))],
        out_specs=pl.BlockSpec((1, ROWS, D), lambda p: (p, 0, 0)),
        out_shape=shaped((count, ROWS, D), BF),
        compiler_params=params(8),
        cost_estimate=cost(1_000_000, 1_500_000),
        name="halo_send",
    )(place, own, before)


def repeated(block, count):
    return pl.pallas_call(
        repeated_kernel,
        out_shape=shaped((count, *block.shape), BF),
        compiler_params=params(VMEM_MIB),
        cost_estimate=cost(1_000_000, 1_300_000),
        name="repeated",
    )(block)


def fine_finish(own, arrived, tail, hidden_grad, tokens):
    return pl.pallas_call(
        fine_finish_kernel,
        out_shape=shaped((ROWS, D), BF),
        compiler_params=params(VMEM_MIB),
        cost_estimate=cost(1_000_000, 3_000_000),
        name="fine_finish",
    )(own, *arrived, tail, hidden_grad, tokens)


def per_device(tokens, cotangent, fine_qkv, fine_out, coarse_qkv, coarse_out):
    peers = 1
    for name in GROUP:
        peers *= lax.axis_size(name)
    groups = 1
    for name in FAR:
        groups *= lax.axis_size(name)
    weights = jnp.transpose(fine_qkv, (1, 0, 2))
    core = lax.axis_index("core").astype(jnp.int32).reshape(1)
    column_at = lax.axis_index("x")
    columns_along = lax.axis_size("x")
    tail = shifted_by(tokens[ROWS - EXTRA :], columns_along + 1)
    row_before = shifted_by(tokens, columns_along)
    group_start = lax.axis_index(FAR) * (peers * COARSE)
    place = jnp.stack([lax.axis_index(LINE) * ROWS, column_at, group_start]).astype(jnp.int32)
    prepared = fine_prepare(place, tokens, cotangent, weights, fine_out)
    coarse_weights = coarse_prepare(core, jnp.transpose(coarse_qkv, (1, 0, 2)), coarse_out)
    tail, row_before, prepared, coarse_weights, place = lax.optimization_barrier(
        (tail, row_before, prepared, coarse_weights, place)
    )
    own, weights, fine_out, *_, coarse_grad = prepared
    coarse_in, coarse_back = coarse_weights
    slots = exchanged(halo_send(place, own, row_before, columns_along), "x")
    *kept, hidden, message = fine_forward(place, tail, slots, prepared, peers)
    gathered = exchanged(message, GROUP)
    near, further = lax.axis_size("z_hi"), lax.axis_size("y")
    coarse_send, coarse_factor = coarse_project(gathered, coarse_in, coarse_back, near)
    group_rows = coarse_factor.shape[0]
    nearby = exchanged(coarse_send, "z_hi").reshape(near * group_rows, 2 * PAIR)
    everyone = exchanged(repeated(nearby, further), "y").reshape(groups * group_rows, 2 * PAIR)
    partial = coarse_attention(place, everyone, coarse_factor, coarse_in, coarse_back)
    returned = exchanged(partial, GROUP)
    spread, state = coarse_finish(returned, message, coarse_grad)
    output = (
        hidden.astype(F32) + jnp.repeat(state.astype(BF), POOL, axis=0).astype(F32)
    ).astype(BF)
    *backs, tail_back, own_grad, hidden_grad = fine_backward(
        place, cotangent, spread, fine_out, weights, *kept
    )
    arrived = [shifted_by(backs[steps - 1], -steps) for steps in range(len(backs), 0, -1)]
    tail_arrived = shifted_by(tail_back, -(columns_along + 1))
    return (output, fine_finish(own_grad, arrived[::-1], tail_arrived, hidden_grad, own))


def solution(mesh):
    sizes = (4, 4, 2, 2, 4)
    fine_mesh = Mesh(mesh.devices.reshape(sizes), LINE)
    placed = (
        P(LINE, None),
        P(LINE, None),
        P(),
        P(),
        P(None, None, ("z_lo", "x")),
        P(("z_lo", "x"), None),
    )
    return jax.shard_map(
        per_device,
        mesh=fine_mesh,
        in_specs=placed,
        out_specs=(P(LINE, None), P(LINE, None)),
        check_vma=False,
    )
```

```python
import jax
import jax.numpy as jnp
from jax import lax
from jax.experimental import pallas as pl
from jax.experimental.pallas import tpu as pltpu
from jax.sharding import Mesh
from jax.sharding import PartitionSpec as P

D = 1024
HEADS = 16
HEAD_DIM = 64
WINDOW = 512
POOL = 16
EPS = 1e-06

LINE = ("y", "z_hi", "core", "z_lo", "x")
GROUP = ("core", "z_lo", "x")
FAR = ("y", "z_hi")

ROWS = 128
HALO = WINDOW
OWN_KEYS = HALO + ROWS
EXTRA = 16
ALL_KEYS = OWN_KEYS + EXTRA
QUERIES = EXTRA + ROWS
PAIR = 2 * HEAD_DIM
COARSE = ROWS // POOL
SCALE = HEAD_DIM ** (-0.5)
NEG = -1e30
VMEM_MIB = 16

BF = jnp.bfloat16
F32 = jnp.float32


def shifted_by(value, steps):
    count = 1
    for name in LINE:
        count *= lax.axis_size(name)
    first, last = (max(0, -steps), min(count, count - steps))
    return lax.ppermute(value, LINE, [(source, source + steps) for source in range(first, last)])


def exchanged(pieces, axes):
    return lax.all_to_all(pieces, axes, 0, 0, tiled=True)


def last_last(left, right):
    return lax.dot_general(left, right, (((1,), (1,)), ((), ())), preferred_element_type=F32)


def first_first(left, right):
    return lax.dot_general(left, right, (((0,), (0,)), ((), ())), preferred_element_type=F32)


def plain(left, right):
    return jnp.dot(left, right, preferred_element_type=F32)


def low_lanes():
    return lax.broadcasted_iota(jnp.int32, (1, PAIR), 1) < HEAD_DIM


def pair_sums(values, low):
    low_sum = jnp.sum(jnp.where(low, values, 0.0), axis=-1, keepdims=True)
    high_sum = jnp.sum(jnp.where(low, 0.0, values), axis=-1, keepdims=True)
    return jnp.where(low, low_sum, high_sum)


def pair_norm(values, low):
    factor = lax.rsqrt(pair_sums(values * values, low) * (1.0 / HEAD_DIM) + EPS)
    return values * factor, factor


def pair_norm_back(grad, unit, factor, low):
    return factor * (grad - unit * (pair_sums(unit * grad, low) * (1.0 / HEAD_DIM)))


def row_norm(rows):
    factor = lax.rsqrt(jnp.mean(rows * rows, axis=-1, keepdims=True) + EPS)
    return rows * factor, factor


def row_norm_back(grad, normed, factor):
    return factor * (grad - normed * jnp.mean(normed * grad, axis=-1, keepdims=True))


def fine_prepare_kernel(
    place_ref, own_hbm, cot_hbm, w_hbm, out_w_hbm,
    own_ref, w_ref, out_w_ref, q_ref, k_ref, v_ref, qf_ref, kf_ref, bias_ref, cg_ref,
    cot, copied,
):
    anchor = place_ref[0]
    column_at = place_ref[1]
    low = low_lanes()
    copies = [
        pltpu.make_async_copy(source, target, copied.at[at])
        for at, (source, target) in enumerate(
            ((own_hbm, own_ref), (cot_hbm, cot), (w_hbm, w_ref), (out_w_hbm, out_w_ref))
        )
    ]
    for copy in copies:
        copy.start()

    row = lax.broadcasted_iota(jnp.int32, (2 * QUERIES, ALL_KEYS), 0)
    query_pos = jnp.where(row < QUERIES, row, row - QUERIES) - EXTRA
    column = lax.broadcasted_iota(jnp.int32, (2 * QUERIES, ALL_KEYS), 1)
    turned = column_at * ROWS
    halo_pos = column - jnp.where(column >= turned, turned + HALO, turned)
    key_pos = jnp.where(
        column < HALO,
        halo_pos,
        jnp.where(column < OWN_KEYS, column - HALO, column - (OWN_KEYS + HALO + EXTRA)),
    )
    gap = query_pos - key_pos
    allowed = (gap >= 0) & (gap < WINDOW) & (anchor + key_pos >= 0)
    bias_ref[...] = jnp.where(allowed, 0.0, NEG)

    copies[0].wait()
    normed = row_norm(own_ref[...].astype(F32))[0].astype(BF)
    copies[1].wait()
    chunk = lax.broadcasted_iota(jnp.int32, (COARSE, ROWS), 0) * POOL
    row = lax.broadcasted_iota(jnp.int32, (COARSE, ROWS), 1)
    member = jnp.where((row >= chunk) & (row < chunk + POOL), 1.0, 0.0).astype(BF)
    cg_ref[...] = plain(member, cot[...])
    copies[2].wait()
    for at in range(0, D, WIDTH):
        here = slice(at, at + WIDTH)
        queries = plain(normed, w_ref[0, :, here])
        keys = plain(normed, w_ref[1, :, here])
        v_ref[:, here] = plain(normed, w_ref[2, :, here]).astype(BF)
        for part in range(0, WIDTH, PAIR):
            inner = slice(part, part + PAIR)
            outer = slice(at + part, at + part + PAIR)
            query, q_factor = pair_norm(queries[:, inner], low)
            key, k_factor = pair_norm(keys[:, inner], low)
            q_ref[:, outer] = query.astype(BF)
            k_ref[:, outer] = key.astype(BF)
            qf_ref[:, outer] = q_factor
            kf_ref[:, outer] = k_factor
    copies[3].wait()


def fine_forward_kernel(
    place_ref, tail_ref, slots_ref, own_ref, w_ref, out_w_ref, own_q_ref, own_k_ref, own_v_ref,
    own_kf_ref, bias, cg_ref,
    k_ref, v_ref, kf_ref, p_ref, att_ref, hid_ref, send_ref,
    normed, acc,
):
    anchor = place_ref[0]
    column_at = place_ref[1]
    low = low_lanes()
    slots = slots_ref.shape[0]
    nearest = lax.rem(column_at + (slots - 1), slots)
    for slot in range(slots):
        at = slot * ROWS
        normed[at : at + ROWS, :] = row_norm(slots_ref[slot].astype(F32))[0].astype(BF)
    normed[HALO:, :] = row_norm(tail_ref[...].astype(F32))[0].astype(BF)
    acc[...] = jnp.zeros_like(acc)
    extra_at = pl.multiple_of(nearest * ROWS + (ROWS - EXTRA), EXTRA)

    def one_step(step, carry):
        first = pl.multiple_of(step * WIDTH, WIDTH)
        here = pl.ds(first, WIDTH)
        extra = plain(normed[pl.ds(extra_at, EXTRA), :], w_ref[0, :, here])
        both = plain(
            normed[...], jnp.concatenate([w_ref[1, :, here], w_ref[2, :, here]], axis=1)
        )
        own_q, own_k, own_v = own_q_ref[:, here], own_k_ref[:, here], own_v_ref[:, here]
        own_kf = own_kf_ref[:, here]
        mixed = []
        for part in range(0, WIDTH, PAIR):
            inner = slice(part, part + PAIR)
            outer = pl.ds(pl.multiple_of(first + part, PAIR), PAIR)
            key, k_factor = pair_norm(both[:, inner], low)
            key = key.astype(BF)
            value = both[:, WIDTH + part : WIDTH + part + PAIR].astype(BF)
            k_ref[:HALO, outer] = key[:HALO]
            k_ref[HALO:, outer] = own_k[:, inner]
            v_ref[:HALO, outer] = value[:HALO]
            v_ref[HALO:, outer] = own_v[:, inner]
            kf_ref[:HALO, outer] = k_factor[:HALO]
            kf_ref[HALO:, outer] = own_kf[:, inner]
            key = jnp.concatenate([key[:HALO], own_k[:, inner], key[HALO:]], axis=0)
            value = jnp.concatenate([value[:HALO], own_v[:, inner], value[HALO:]], axis=0)
            before = pair_norm(extra[:, inner], low)[0].astype(BF).astype(F32)
            scaled = jnp.concatenate([before, own_q[:, inner].astype(F32)], axis=0) * SCALE
            stacked = jnp.concatenate(
                [jnp.where(low, scaled, 0.0), jnp.where(low, 0.0, scaled)], axis=0
            )
            numer = jnp.exp(last_last(stacked.astype(BF), key) + bias[...])
            total = jnp.sum(numer, axis=-1, keepdims=True)
            prob = (numer * (1.0 / jnp.where(total > 0.0, total, 1.0))).astype(BF)
            head = (first + part) // HEAD_DIM
            p_ref[head] = prob[EXTRA:QUERIES, :OWN_KEYS]
            p_ref[head + 1] = prob[QUERIES + EXTRA :, :OWN_KEYS]
            twice = plain(prob, value)
            attended = jnp.where(low, twice[:QUERIES], twice[QUERIES:]).astype(BF)
            att_ref[:, outer] = attended[EXTRA:]
            mixed.append(attended)
        acc[...] += plain(jnp.concatenate(mixed, axis=1), out_w_ref[here, :])
        return carry

    lax.fori_loop(0, D // WIDTH, one_step, 0, unroll=True)
    before = slots_ref[nearest, ROWS - EXTRA :, :].astype(F32) + acc[:EXTRA, :]
    before = jnp.where(anchor > 0, before, 0.0).astype(BF)
    own = (own_ref[...].astype(F32) + acc[EXTRA:, :]).astype(BF)
    hid_ref[...] = own
    chunk = lax.broadcasted_iota(jnp.int32, (COARSE, QUERIES), 0) * POOL
    row = lax.broadcasted_iota(jnp.int32, (COARSE, QUERIES), 1)
    member = jnp.where((row > chunk) & (row <= chunk + POOL), 1.0, 0.0).astype(BF)
    pooled = plain(member, jnp.concatenate([before, own], axis=0)) * (1.0 / POOL)
    message = jnp.concatenate([pooled, cg_ref[...]], axis=0).astype(BF)
    for peer in range(send_ref.shape[0]):
        send_ref[peer] = message


def coarse_prepare_kernel(core_ref, w_ref, back_ref, in_ref, out_ref):
    low = low_lanes()
    second = core_ref[0] > 0
    parts = [w_ref[at].astype(F32) for at in range(3)]
    turned = [pltpu.roll(part, HEAD_DIM, 1) for part in parts]
    query = jnp.where(second, turned[0], parts[0])
    key = jnp.where(second, turned[1], parts[1])
    value = jnp.where(second, parts[2], turned[2])
    in_ref[:, :PAIR] = jnp.where(low, query, 0.0).astype(BF)
    in_ref[:, PAIR:] = jnp.where(low, key, value).astype(BF)
    out_ref[...] = jnp.zeros_like(out_ref)
    out_ref[HEAD_DIM:PAIR, :] = jnp.where(second, back_ref[HEAD_DIM:, :], back_ref[:HEAD_DIM, :])


def coarse_project_kernel(got_ref, in_w_ref, out_w_ref, send_ref, factor_ref):
    low = low_lanes()
    rows = got_ref[...].astype(F32)
    count = rows.shape[0] * COARSE
    pooled = rows[:, :COARSE, :].reshape(count, D)
    coarse_grad = rows[:, COARSE:, :].reshape(count, D)
    normed = row_norm(pooled)[0].astype(BF)
    raw = plain(normed, in_w_ref[...]) + last_last(coarse_grad.astype(BF), out_w_ref[...])
    units, factors = [], []
    for tile in (raw[:, :PAIR], raw[:, PAIR:]):
        unit, factor = pair_norm(tile, low)
        units.append(jnp.where(low, unit, tile))
        factors.append(factor)
    message = jnp.concatenate(units, axis=1).astype(BF)
    factor_ref[...] = jnp.concatenate(factors, axis=1)
    for peer in range(send_ref.shape[0]):
        send_ref[peer] = message


def coarse_attention_kernel(place_ref, got_ref, factor_ref, in_w_ref, out_w_ref, send_ref, own_grad):
    low = low_lanes()
    own_start = pl.multiple_of(place_ref[2], ROWS)
    length = got_ref.shape[0]
    block = 512
    own_left = got_ref[pl.ds(own_start, ROWS), :PAIR]
    own_right = got_ref[pl.ds(own_start, ROWS), PAIR:]
    own_grad[...] = jnp.zeros_like(own_grad)

    def masked_halves(tile):
        wide = tile.astype(F32)
        return (
            jnp.where(low, wide * SCALE, 0.0).astype(BF),
            jnp.where(low, 0.0, wide).astype(BF),
        )

    def lane_partials(values):
        total = values[:, :PAIR]
        for at in range(PAIR, values.shape[1], PAIR):
            total = total + values[:, at : at + PAIR]
        return total

    def one_block(index):
        first = index * block
        query, grad = masked_halves(got_ref[first : first + block, :PAIR])
        stacked = jnp.concatenate([query, grad], axis=0)

        def scored(keys):
            both = last_last(stacked, keys)
            return jnp.exp(both[:block]), both[block:]

        query_at = lax.broadcasted_iota(jnp.int32, (block, 1), 0)
        total = product = None
        for at in range(index + 1):
            numer, prob_grad = scored(got_ref[at * block : (at + 1) * block, PAIR:])
            if at == index:
                key_at = lax.broadcasted_iota(jnp.int32, (1, block), 1)
                numer = jnp.where(key_at <= query_at, numer, 0.0)
            sums = lane_partials(numer), lane_partials(numer * prob_grad)
            total, product = sums if at == 0 else (total + sums[0], product + sums[1])
        inverse = 1.0 / jnp.sum(total, axis=-1, keepdims=True)
        delta = jnp.sum(product, axis=-1, keepdims=True) * inverse
        own_pos = own_start + lax.broadcasted_iota(jnp.int32, (1, ROWS), 1)
        numer, prob_grad = scored(own_right)
        numer = jnp.where(own_pos <= query_at + first, numer, 0.0)
        prob = numer * inverse
        score_grad = (prob * (prob_grad - delta)).astype(BF)
        own_grad[...] += first_first(
            jnp.concatenate([score_grad, prob.astype(BF)], axis=0), stacked
        )

    for index in range(length // block):
        pl.when(own_start < (index + 1) * block)(lambda index=index: one_block(index))

    query, grad = masked_halves(own_left)
    stacked = jnp.concatenate([query, grad], axis=0)
    query_pos = own_start + lax.broadcasted_iota(jnp.int32, (ROWS, 1), 0)

    def own_chunk(at):
        key_start = pl.multiple_of(at * block, block)
        keys = got_ref[pl.ds(key_start, block), PAIR:]
        both = last_last(stacked, keys)
        key_pos = key_start + lax.broadcasted_iota(jnp.int32, (1, block), 1)
        return keys, jnp.where(key_pos <= query_pos, jnp.exp(both[:ROWS]), 0.0), both[ROWS:]

    def own_sums(at, sums):
        numer, prob_grad = own_chunk(at)[1:]
        return sums[0] + lane_partials(numer), sums[1] + lane_partials(numer * prob_grad)

    nothing = jnp.zeros((ROWS, PAIR), F32)
    chunks = own_start // block + 1
    total, product = lax.fori_loop(0, chunks, own_sums, (nothing, nothing))
    inverse = 1.0 / jnp.sum(total, axis=-1, keepdims=True)
    delta = jnp.sum(product, axis=-1, keepdims=True) * inverse

    def own_results(at, mine):
        keys, numer, prob_grad = own_chunk(at)
        key_scaled, value = masked_halves(keys)
        prob = numer * inverse
        score_grad = (prob * (prob_grad - delta)).astype(BF)
        return mine + plain(score_grad, key_scaled) + plain(prob.astype(BF), value)

    mine = lax.fori_loop(0, chunks, own_results, nothing)

    parts = []
    for tile, unit, factor in (
        (mine, own_left, factor_ref[:, :PAIR]),
        (own_grad[...], own_right, factor_ref[:, PAIR:]),
    ):
        back = pair_norm_back(tile, unit.astype(F32), factor, low)
        parts.append(jnp.where(low, back, tile))
    parts = jnp.concatenate(parts, axis=1).astype(BF)
    peers = send_ref.shape[0]
    normed_grad = last_last(parts, in_w_ref[...]).reshape(peers, COARSE, D)
    mixed = plain(parts, out_w_ref[...]).reshape(peers, COARSE, D)
    send_ref[...] = jnp.concatenate([normed_grad, mixed], axis=1).astype(BF)


def coarse_finish_kernel(got_ref, message_ref, cg_ref, spread_ref, first_ref, state_ref):
    summed = jnp.sum(got_ref[...].astype(F32), axis=0)
    pooled = message_ref[0].astype(F32)[:COARSE]
    normed, factor = row_norm(pooled)
    pooled_grad = cg_ref[...] + row_norm_back(summed[:COARSE], normed, factor)
    spread = pooled_grad * (1.0 / POOL)
    spread_ref[...] = spread
    first_ref[...] = spread[:1]
    state_ref[...] = pooled + summed[COARSE:]


def fine_backward_kernel(
    place_ref, cot_ref, spread_ref, next_ref, out_w_ref, w_ref, q_ref, k_ref, v_ref, qf_ref, kf_ref, p_ref,
    att_ref,
    back1, back2, back3, back4, own_ref, hg_ref, hidden_grad, acc,
):
    low = low_lanes()
    block = (lax.broadcasted_iota(jnp.int32, (ROWS, 1), 0) + (POOL - 1)) // POOL
    added = jnp.zeros((ROWS, D), F32)
    for at in range(COARSE):
        added = jnp.where(block == at, spread_ref[at : at + 1, :], added)
    added = jnp.where(block == COARSE, next_ref[0:1, :], added)
    total = cot_ref[...].astype(F32) + added
    hg_ref[...] = total
    hidden_grad[...] = total.astype(BF)
    acc[...] = jnp.zeros_like(acc)

    def one_step(step, carry):
        first = pl.multiple_of(step * WIDTH, WIDTH)
        here = pl.ds(first, WIDTH)
        att_grads = last_last(hidden_grad[...], out_w_ref[here, :]).astype(BF).astype(F32)
        query_grads, key_grads, value_grads = [], [], []
        for part in range(0, WIDTH, PAIR):
            outer = pl.ds(pl.multiple_of(first + part, PAIR), PAIR)
            att_grad = att_grads[:, part : part + PAIR]
            delta_all = att_grad * att_ref[:, outer].astype(F32)
            value = v_ref[:, outer]
            key_wide = k_ref[:, outer].astype(F32)
            query_wide = q_ref[:, outer].astype(F32)
            grad = jnp.concatenate(
                [jnp.where(low, att_grad, 0.0), jnp.where(low, 0.0, att_grad)], axis=0
            ).astype(BF)
            delta = jnp.sum(
                jnp.concatenate(
                    [jnp.where(low, delta_all, 0.0), jnp.where(low, 0.0, delta_all)], axis=0
                ),
                axis=-1,
                keepdims=True,
            )
            scaled = query_wide * SCALE
            query = jnp.concatenate(
                [jnp.where(low, scaled, 0.0), jnp.where(low, 0.0, scaled)], axis=0
            ).astype(BF)
            head = (first + part) // HEAD_DIM
            prob = p_ref[pl.ds(head, 2)].reshape(2 * ROWS, OWN_KEYS)
            score_grad = (prob.astype(F32) * (last_last(grad, value) - delta)).astype(BF)
            twice = plain(score_grad, (key_wide * SCALE).astype(BF))
            query_grad = jnp.where(low, twice[:ROWS], twice[ROWS:])
            key_grad = first_first(score_grad, query)
            value_grad = first_first(prob, grad)
            query_grads.append(pair_norm_back(query_grad, query_wide, qf_ref[:, outer], low).astype(BF))
            key_grads.append(pair_norm_back(key_grad, key_wide, kf_ref[:, outer], low).astype(BF))
            value_grads.append(value_grad.astype(BF))
        both = jnp.concatenate(key_grads + value_grads, axis=1)
        acc[...] += last_last(
            both, jnp.concatenate([w_ref[1, :, here], w_ref[2, :, here]], axis=1)
        )
        acc[HALO:, :] += last_last(jnp.concatenate(query_grads, axis=1), w_ref[0, :, here])
        return carry

    lax.fori_loop(0, D // WIDTH, one_step, 0, unroll=True)
    backs = (back1, back2, back3, back4)
    for distance, ref in enumerate(backs, 1):
        slot = lax.rem(place_ref[1] + (len(backs) - distance), len(backs))
        ref[...] = acc[pl.ds(pl.multiple_of(slot * ROWS, ROWS), ROWS), :].astype(BF)
    own_ref[...] = acc[HALO:, :]


def halo_send_kernel(place_ref, own_ref, before_ref, send_ref):
    send_ref[0] = jnp.where(place_ref[1] < pl.program_id(0), own_ref[...], before_ref[...])


def repeated_kernel(block_ref, send_ref):
    for peer in range(send_ref.shape[0]):
        send_ref[peer] = block_ref[...]


def fine_finish_kernel(own_ref, a1, a2, a3, a4, hg_ref, tokens_ref, out_ref):
    total = own_ref[...]
    for ref in (a1, a2, a3, a4):
        total = total + ref[...].astype(F32)
    normed, factor = row_norm(tokens_ref[...].astype(F32))
    out_ref[...] = (hg_ref[...] + row_norm_back(total, normed, factor)).astype(BF)


def whole(shape):
    return pl.BlockSpec(shape, lambda *_: (0,) * len(shape))


def columns(rows, width):
    return pl.BlockSpec((rows, width), lambda p: (0, p))


def shaped(shape, kind):
    return jax.ShapeDtypeStruct(shape, kind)


def params(mib):
    return pltpu.CompilerParams(vmem_limit_bytes=mib << 20)


def cost(flops, moved, exps=0):
    return pl.CostEstimate(flops=flops, bytes_accessed=moved, transcendentals=exps)


SCALAR = pl.BlockSpec(memory_space=pltpu.SMEM)
IN_VMEM = pl.BlockSpec(memory_space=pltpu.VMEM)
WIDTH = 4 * PAIR


def in_hbm(x):
    return pltpu.with_memory_space_constraint(x, pltpu.HBM)


def fine_prepare(place, tokens, cotangent, weights, fine_out):
    anywhere = pl.BlockSpec(memory_space=pltpu.HBM)
    return pl.pallas_call(
        fine_prepare_kernel,
        in_specs=[SCALAR] + [anywhere] * 4,
        out_specs=[IN_VMEM] * 10,
        out_shape=[
            pltpu.VMEM((ROWS, D), BF),
            pltpu.VMEM((3, D, D), BF),
            pltpu.VMEM((D, D), BF),
            pltpu.VMEM((ROWS, D), BF),
            pltpu.VMEM((ROWS, D), BF),
            pltpu.VMEM((ROWS, D), BF),
            pltpu.VMEM((ROWS, D), F32),
            pltpu.VMEM((ROWS, D), F32),
            pltpu.VMEM((2 * QUERIES, ALL_KEYS), F32),
            pltpu.VMEM((COARSE, D), F32),
        ],
        scratch_shapes=[pltpu.VMEM((ROWS, D), BF), pltpu.SemaphoreType.DMA((4,))],
        compiler_params=params(16),
        cost_estimate=cost(900_000_000, 17_000_000),
        name="fine_prepare",
    )(place, *(in_hbm(x) for x in (tokens, cotangent, weights, fine_out)))


def fine_forward(place, tail, slots, own, weights, fine_out, own_q, own_k, own_v, own_kf, bias, cg, peers):
    return pl.pallas_call(
        fine_forward_kernel,
        in_specs=[SCALAR] + [IN_VMEM] * 11,
        out_specs=[IN_VMEM] * 7,
        out_shape=[
            pltpu.VMEM((OWN_KEYS, D), BF),
            pltpu.VMEM((OWN_KEYS, D), BF),
            pltpu.VMEM((OWN_KEYS, D), F32),
            pltpu.VMEM((HEADS, ROWS, OWN_KEYS), BF),
            pltpu.VMEM((ROWS, D), BF),
            shaped((ROWS, D), BF),
            shaped((peers, 2 * COARSE, D), BF),
        ],
        scratch_shapes=[pltpu.VMEM((HALO + EXTRA, D), BF), pltpu.VMEM((QUERIES, D), F32)],
        compiler_params=params(16),
        cost_estimate=cost(4_500_000_000, 20_000_000, 1_600_000),
        name="fine_forward",
    )(place, tail, slots, own, weights, fine_out, own_q, own_k, own_v, own_kf, bias, cg)


def coarse_prepare(core, weights, back):
    return pl.pallas_call(
        coarse_prepare_kernel,
        in_specs=[SCALAR, IN_VMEM, IN_VMEM],
        out_specs=[IN_VMEM] * 2,
        out_shape=[shaped((D, 2 * PAIR), BF), shaped((2 * PAIR, D), BF)],
        compiler_params=params(8),
        cost_estimate=cost(1_000_000, 2_500_000),
        name="coarse_prepare",
    )(core, weights, back)


def coarse_project(gathered, coarse_in, coarse_back, groups):
    rows = gathered.shape[0] * COARSE
    return pl.pallas_call(
        coarse_project_kernel,
        out_shape=[shaped((groups, rows, 2 * PAIR), BF), shaped((rows, 2 * PAIR), F32)],
        compiler_params=params(VMEM_MIB),
        cost_estimate=cost(140_000_000, 3_000_000),
        name="coarse_project",
    )(gathered, coarse_in, coarse_back)


def coarse_attention(place, everyone, factor, coarse_in, coarse_back):
    rows = factor.shape[0]
    return pl.pallas_call(
        coarse_attention_kernel,
        in_specs=[SCALAR] + [IN_VMEM] * 4,
        out_shape=shaped((rows // COARSE, 2 * COARSE, D), BF),
        scratch_shapes=[pltpu.VMEM((rows, PAIR), F32)],
        compiler_params=params(VMEM_MIB),
        cost_estimate=cost(1_500_000_000, 3_000_000, 3_000_000),
        name="coarse_attention",
    )(place, everyone, factor, coarse_in, coarse_back)


def coarse_finish(returned, message, coarse_grad):
    return pl.pallas_call(
        coarse_finish_kernel,
        grid=(1,),
        in_specs=[whole(returned.shape), whole((1, 2 * COARSE, D)), whole((COARSE, D))],
        out_specs=[whole((COARSE, D)), whole((1, D)), whole((COARSE, D))],
        out_shape=[shaped((COARSE, D), F32), shaped((1, D), F32), shaped((COARSE, D), F32)],
        compiler_params=params(VMEM_MIB),
        cost_estimate=cost(1_000_000, 1_000_000),
        name="coarse_finish",
    )(returned, message, coarse_grad)


def fine_backward(
    place, cotangent, spread, after, fine_out, weights, query, key, value, q_factor, k_factor, probs,
    attended,
):
    return pl.pallas_call(
        fine_backward_kernel,
        in_specs=[SCALAR] + [IN_VMEM] * 12,
        out_specs=[IN_VMEM] * 6,
        out_shape=[shaped((ROWS, D), BF)] * 4 + [shaped((ROWS, D), F32)] * 2,
        scratch_shapes=[pltpu.VMEM((ROWS, D), BF), pltpu.VMEM((OWN_KEYS, D), F32)],
        compiler_params=params(16),
        cost_estimate=cost(5_000_000_000, 20_000_000),
        name="fine_backward",
    )(
        place, cotangent, spread, after, fine_out, weights, query, key, value, q_factor, k_factor, probs,
        attended,
    )


def halo_send(place, own, before, count):
    return pl.pallas_call(
        halo_send_kernel,
        grid=(count,),
        in_specs=[SCALAR, whole((ROWS, D)), whole((ROWS, D))],
        out_specs=pl.BlockSpec((1, ROWS, D), lambda p: (p, 0, 0)),
        out_shape=shaped((count, ROWS, D), BF),
        compiler_params=params(8),
        cost_estimate=cost(1_000_000, 1_500_000),
        name="halo_send",
    )(place, own, before)


def repeated(block, count):
    return pl.pallas_call(
        repeated_kernel,
        out_shape=shaped((count, *block.shape), BF),
        compiler_params=params(VMEM_MIB),
        cost_estimate=cost(1_000_000, 1_300_000),
        name="repeated",
    )(block)


def fine_finish(own, arrived, hidden_grad, tokens):
    return pl.pallas_call(
        fine_finish_kernel,
        out_shape=shaped((ROWS, D), BF),
        compiler_params=params(VMEM_MIB),
        cost_estimate=cost(1_000_000, 3_000_000),
        name="fine_finish",
    )(own, *arrived, hidden_grad, tokens)


def per_device(tokens, cotangent, fine_qkv, fine_out, coarse_qkv, coarse_out):
    peers = 1
    for name in GROUP:
        peers *= lax.axis_size(name)
    groups = 1
    for name in FAR:
        groups *= lax.axis_size(name)
    weights = jnp.transpose(fine_qkv, (1, 0, 2))
    core = lax.axis_index("core").astype(jnp.int32).reshape(1)
    column_at = lax.axis_index("x")
    columns_along = lax.axis_size("x")
    tail = shifted_by(tokens[ROWS - EXTRA :], columns_along + 1)
    row_before = shifted_by(tokens, columns_along)
    group_start = lax.axis_index(FAR) * (peers * COARSE)
    place = jnp.stack([lax.axis_index(LINE) * ROWS, column_at, group_start]).astype(jnp.int32)
    prepared = fine_prepare(place, tokens, cotangent, weights, fine_out)
    coarse_weights = coarse_prepare(core, jnp.transpose(coarse_qkv, (1, 0, 2)), coarse_out)
    tail, row_before, prepared, coarse_weights, place = lax.optimization_barrier(
        (tail, row_before, prepared, coarse_weights, place)
    )
    own, weights, fine_out, query, own_key, own_value, q_factor, own_k_factor, bias, coarse_grad = prepared
    coarse_in, coarse_back = coarse_weights
    slots = exchanged(halo_send(place, own, row_before, columns_along), "x")
    key, value, k_factor, probs, attended, hidden, message = fine_forward(
        place, tail, slots, own, weights, fine_out, query, own_key, own_value, own_k_factor, bias,
        coarse_grad, peers,
    )
    gathered = exchanged(message, GROUP)
    near, further = lax.axis_size("z_hi"), lax.axis_size("y")
    coarse_send, coarse_factor = coarse_project(gathered, coarse_in, coarse_back, near)
    group_rows = coarse_factor.shape[0]
    nearby = exchanged(coarse_send, "z_hi").reshape(near * group_rows, 2 * PAIR)
    everyone = exchanged(repeated(nearby, further), "y").reshape(groups * group_rows, 2 * PAIR)
    partial = coarse_attention(place, everyone, coarse_factor, coarse_in, coarse_back)
    returned = exchanged(partial, GROUP)
    spread, first, state = coarse_finish(returned, message, coarse_grad)
    after = shifted_by(first, -1)
    output = (
        hidden.astype(F32) + jnp.repeat(state.astype(BF), POOL, axis=0).astype(F32)
    ).astype(BF)
    *backs, own_grad, hidden_grad = fine_backward(
        place, cotangent, spread, after, fine_out, weights, query, key, value, q_factor, k_factor, probs,
        attended,
    )
    arrived = [shifted_by(backs[steps - 1], -steps) for steps in (4, 2, 3, 1)]
    return (output, fine_finish(own_grad, arrived, hidden_grad, own))


def solution(mesh):
    sizes = (4, 4, 2, 2, 4)
    fine_mesh = Mesh(mesh.devices.reshape(sizes), LINE)
    placed = (
        P(LINE, None),
        P(LINE, None),
        P(),
        P(),
        P(None, None, ("z_lo", "x")),
        P(("z_lo", "x"), None),
    )
    return jax.shard_map(
        per_device,
        mesh=fine_mesh,
        in_specs=placed,
        out_specs=(P(LINE, None), P(LINE, None)),
        check_vma=False,
    )
```
